32 devices in a mesh: groups: 2 (over x), frame: 16 (over z, y, core).
Axes of the slice: x: 2, y: 2, z: 4, core: 2. Of those that a mesh axis runs over, the one named last changes fastest.
Arguments:
- query_rows: bfloat16 [8192, 2560], P(('groups', 'frame')), parts along dimension 0, may hold values from -60 to 60
- key_rows: bfloat16 [8192, 2560], P(('groups', 'frame')), parts along dimension 0, may hold values from -4 to 4
- value_rows: bfloat16 [8192, 2560], P(('groups', 'frame')), parts along dimension 0, may hold values from -6 to 6
- tile_mask: int32 [128, 27], P(('groups', 'frame')), parts along dimension 0, may hold values from 0 to 1, as said below
- head_weight: bfloat16 [2560, 64], replicated, may hold values from -0.125 to 0.125
- latent: float32 [8192, 64], P(('groups', 'frame')), parts along dimension 0, may hold values from -6 to 6
- step_index: int32 [2], P('groups'), parts along dimension 0, may hold values from 0 to 24
Outputs:
- guided: float32 [8192, 64], P(('groups', 'frame')), parts along dimension 0
- clean: float32 [8192, 64], P(('groups', 'frame')), parts along dimension 0
- latent_next: float32 [8192, 64], P(('groups', 'frame')), parts along dimension 0
The draws below stay inside these ranges and needn't reach their ends.
There are 2 independent parts, one for each index of `groups`. The reference program is written for one: setup_inputs(seed, part) draws one part's arguments, and reference() takes and returns one part's arrays. A program takes and returns all parts, laid end to end along the dimension named above; an argument that names none is the same for every part. Nothing has to cross between parts.
Inputs may be any that keep to these rules, and one draw needn't show every extreme that they name: `tile_mask`: entries are 0 or 1; entry 13 (the query tile itself) is always 1.
All inputs are finite; a program needn't handle non-finite values.
Results may differ from the reference program's by a relative error of at most 0.0041.
Values may be sent and summed in bfloat16 or wider, within the bound.
No kernel may reach another device: no remote copies, remote signals or barrier semaphores. Data moves between devices by JAX's collectives and lax.ppermute only.
A program may use at most 128 MiB of HBM per device.

```python
import math
import jax
import jax.numpy as jnp
from jax import lax

HEADS = 20
HD = 128
CH = 64
SH = 4
SW = 8
SAMPLE_STEPS = 50
TILE_TOK = 64
NFT = 1
TOKENS = 2048
QT = 64
INNER = 2560


def joint_draw(key):
    base = jax.random.fold_in(key, 7)
    first, second = jax.random.split(base, 2)
    total_rows = 2 * TOKENS
    width = HEADS * HD
    keys_done = jnp.clip(jax.random.normal(first, (total_rows, width), jnp.float32), -4.0, 4.0)
    query_done = jnp.clip(2.0 * jax.random.normal(second, (total_rows, width), jnp.float32), -8.0, 8.0)
    return (query_done, keys_done)


def draw_query_rows(key, part):
    return joint_draw(key)[0].astype(jnp.bfloat16)


def draw_key_rows(key, part):
    return joint_draw(key)[1].astype(jnp.bfloat16)


def draw_tile_mask(key, part):
    base = jax.random.fold_in(key, 11)
    first, second, third = jax.random.split(base, 3)
    tile_count = 4
    slab_count = QT // tile_count
    slab_number = jnp.arange(slab_count, dtype=jnp.int32)[:, None, None]
    full_slab = slab_number % 4 == 0
    density = jax.random.randint(first, (slab_count, 1, 1), 15, 91)
    density = jnp.where(full_slab, 101, density)
    sides = jax.random.randint(second, (slab_count, 1, 3), 0, 4)
    plane_on = (sides != 0) | (jnp.arange(3, dtype=jnp.int32)[None, None, :] == 1) | full_slab
    draws = jax.random.randint(third, (slab_count, tile_count, 27), 0, 100)
    window_code = jnp.arange(27, dtype=jnp.int32)
    plane = window_code // 9
    plane_entry = jnp.take_along_axis(plane_on, jnp.broadcast_to(plane[None, None, :], (slab_count, 1, 27)), axis=2)
    entries = (draws < density) & plane_entry
    entries = entries | (window_code == 13)[None, None, :]
    return entries.astype(jnp.int32).reshape(QT, 27)


def levels(own_key, dims, pieces, low, largest):
    def one(position, blocks):
        steps = jax.random.uniform(jax.random.fold_in(jax.random.fold_in(own_key, 6), position), (blocks,), jnp.float32, low / len(pieces), largest / len(pieces))
        return jnp.repeat(jnp.exp(steps), dims[position] // blocks).reshape((-1,) + (1,) * (len(dims) - position - 1))

    level = one(*pieces[0])
    for cut in pieces[1:]:
        level = level * one(*cut)
    return level


def centred(key, dims, spread, reach, cuts=(), kind=jnp.bfloat16):
    values = spread * jax.random.normal(key, dims, jnp.float32)
    if cuts:
        values = values * levels(key, dims, cuts, -0.22, 0.18)
    return jnp.clip(values, -reach, reach).astype(kind)


def setup_inputs(seed: int = 0, part: int = 0) -> dict:
    keys = jax.random.split(jax.random.key(seed), 8)
    own_keys = jax.random.split(jax.random.fold_in(keys[7], part), 8)
    query_rows = draw_query_rows(jax.random.fold_in(jax.random.fold_in(keys[7], part), 71), part)
    key_rows = draw_key_rows(jax.random.fold_in(jax.random.fold_in(keys[7], part), 71), part)
    value_rows = centred(own_keys[2], (2 * TOKENS, INNER), 1.0, 6.0, ((0, 16),))
    tile_mask = draw_tile_mask(jax.random.fold_in(jax.random.fold_in(keys[7], part), 71), part)
    head_weight = centred(keys[4], (INNER, CH), INNER ** -0.5, 0.125)
    latent = centred(own_keys[5], (2 * TOKENS, CH), 1.0, 6.0, ((0, 16),), jnp.float32)
    step_index = jax.random.randint(own_keys[6], (1,), 0, SAMPLE_STEPS // 2).astype(jnp.int32)
    return dict(query_rows=query_rows, key_rows=key_rows, value_rows=value_rows, tile_mask=tile_mask, head_weight=head_weight, latent=latent, step_index=step_index)


GUIDANCE = 5.0
FLOW_SHIFT = 5.0

def flow_sigma(moment):
    remain = 1.0 - moment / SAMPLE_STEPS
    return FLOW_SHIFT * remain / (1.0 + (FLOW_SHIFT - 1.0) * remain)

def to_grid(rows):
    width = rows.shape[1]
    grid = rows.reshape(2, NFT, SH // 2, SW // 2, 2, 2, TILE_TOK, width)
    grid = grid.transpose(0, 1, 2, 4, 3, 5, 6, 7)
    return grid.reshape(2, NFT, SH, SW, TILE_TOK, width)

def attend_tile(query_tile, key_window, value_window, key_usable):
    query_float = query_tile.astype(jnp.float32).reshape(-1, HEADS, HD)
    key_float = key_window.astype(jnp.float32).reshape(-1, HEADS, HD)
    value_float = value_window.astype(jnp.float32).reshape(-1, HEADS, HD)
    scores = jnp.einsum('qhd,khd->hqk', query_float, key_float) / math.sqrt(HD)
    scores = jnp.where(key_usable[None, None, :], scores, -1e+30)
    row_max = lax.optimization_barrier(jnp.max(scores, axis=2, keepdims=True))
    shifted = jnp.where(key_usable[None, None, :], jnp.exp(scores - row_max), 0.0)
    weights = (shifted / lax.optimization_barrier(jnp.sum(shifted, axis=2, keepdims=True))).astype(jnp.bfloat16)
    result_rows = jnp.einsum('hqk,khd->qhd', weights.astype(jnp.float32), value_float)
    return result_rows.reshape(-1, HEADS * HD).astype(jnp.bfloat16)

def reference(query_rows, key_rows, value_rows, tile_mask, head_weight, latent, step_index):
    padding = ((0, 0), (1, 1), (1, 1), (1, 1), (0, 0), (0, 0))
    query_grid = to_grid(query_rows)
    key_pad = jnp.pad(to_grid(key_rows), padding)
    value_pad = jnp.pad(to_grid(value_rows), padding)
    mask_grid = tile_mask.reshape(2, NFT, SH // 2, SW // 2, 2, 2, 27).transpose(0, 1, 2, 4, 3, 5, 6).reshape(2, NFT, SH, SW, 27)
    offsets = jnp.arange(27, dtype=jnp.int32)
    frame_step = offsets // 9 - 1
    row_step = offsets // 3 % 3 - 1
    col_step = offsets % 3 - 1
    zero = jnp.zeros((), jnp.int32)

    def one_tile(tile_number):
        branch = tile_number // (NFT * SH * SW)
        frame_tile = tile_number // (SH * SW) % NFT
        tile_row = tile_number // SW % SH
        tile_col = tile_number % SW
        starts = (branch, frame_tile, tile_row, tile_col, zero, zero)
        query_tile = lax.dynamic_slice(query_grid, starts, (1, 1, 1, 1, TILE_TOK, INNER)).reshape(TILE_TOK, INNER)
        key_window = lax.dynamic_slice(key_pad, starts, (1, 3, 3, 3, TILE_TOK, INNER)).reshape(27 * TILE_TOK, INNER)
        value_window = lax.dynamic_slice(value_pad, starts, (1, 3, 3, 3, TILE_TOK, INNER)).reshape(27 * TILE_TOK, INNER)
        mask_row = lax.dynamic_slice(mask_grid, (branch, frame_tile, tile_row, tile_col, zero), (1, 1, 1, 1, 27)).reshape(27)
        frame_there = frame_tile + frame_step
        row_there = tile_row + row_step
        col_there = tile_col + col_step
        usable = (frame_there >= 0) & (frame_there < NFT) & (row_there >= 0) & (row_there < SH)
        usable = usable & (col_there >= 0) & (col_there < SW) & (mask_row > 0)
        key_usable = jnp.repeat(usable, TILE_TOK)
        attention = attend_tile(query_tile, key_window, value_window, key_usable)
        return jnp.dot(attention, head_weight, preferred_element_type=jnp.float32)
    velocity_grid = lax.map(one_tile, jnp.arange(2 * NFT * SH * SW, dtype=jnp.int32))
    velocity = velocity_grid.reshape(2, NFT, SH // 2, 2, SW // 2, 2, TILE_TOK, CH)
    velocity = velocity.transpose(0, 1, 2, 4, 3, 5, 6, 7).reshape(2, TOKENS, CH)
    blended = velocity[1] + GUIDANCE * (velocity[0] - velocity[1])
    guided = jnp.concatenate([blended, blended], axis=0)
    moment = step_index[0].astype(jnp.float32)
    sigma_now = flow_sigma(moment)
    step_size = flow_sigma(moment + 1.0) - sigma_now
    clean = latent - sigma_now * guided
    latent_next = latent + step_size * guided
    return (guided, clean, latent_next)
```

```python
import functools
import math

import jax
import jax.numpy as jnp
from jax import lax
from jax.experimental import pallas as pl
from jax.experimental.pallas import tpu as pltpu
from jax.sharding import PartitionSpec as P

HEADS = 20
HD = 128
SH = 4
SW = 8
SAMPLE_STEPS = 50


GUIDANCE = 5.0
FLOW_SHIFT = 5.0


def passed_along(value, axis, steps):
    count = lax.axis_size(axis)
    pairs = [(source, (source + steps) % count) for source in range(count)]
    return lax.ppermute(value, axis, pairs)


def flow_sigma(moment):
    remain = 1.0 - moment / SAMPLE_STEPS
    return FLOW_SHIFT * remain / (1.0 + (FLOW_SHIFT - 1.0) * remain)


def edge_range(offset):
    if offset < 0:
        return (1, 2)
    if offset > 0:
        return (0, 1)
    return (0, 2)


def direct_window(stacked, block_count, block_cols):
    received_parts = {}
    for frame_step in (1, 0, -1):
        for row_step in (1, 0, -1):
            for col_step in (1, 0, -1):
                distance = frame_step * block_count + row_step * block_cols + col_step
                row_start, row_stop = edge_range(row_step)
                col_start, col_stop = edge_range(col_step)
                outgoing = stacked[row_start:row_stop, col_start:col_stop]
                if frame_step == 0 and row_step == 0 and (col_step == 0):
                    received = outgoing
                elif row_step == 0 and col_step == 0:
                    received = passed_along(outgoing, "frame", -distance)
                elif row_step != 0 and col_step != 0:
                    received = passed_along(outgoing, "frame", -distance)
                else:
                    received = passed_along(outgoing, "frame", -distance)
                received_parts[frame_step, row_step, col_step] = received
    planes = []
    for frame_step in (-1, 0, 1):
        row_parts = []
        for row_step in (-1, 0, 1):
            col_parts = [received_parts[frame_step, row_step, col_step] for col_step in (-1, 0, 1)]
            row_parts.append(jnp.concatenate(col_parts, axis=1))
        planes.append(jnp.concatenate(row_parts, axis=0))
    return planes


def window_allowed(tile_mask, frame_tile, block_row, block_col, tile_frames):
    offsets = jnp.arange(27, dtype=jnp.int32)
    frame_step = offsets // 9 - 1
    row_step = offsets // 3 % 3 - 1
    col_step = offsets % 3 - 1
    local_tile = jnp.arange(4, dtype=jnp.int32)
    tile_row = 2 * block_row + local_tile // 2
    tile_col = 2 * block_col + local_tile % 2
    frame_there = frame_tile + frame_step
    row_there = tile_row[:, None] + row_step[None, :]
    col_there = tile_col[:, None] + col_step[None, :]
    usable = ((frame_there >= 0) & (frame_there < tile_frames))[None, :]
    usable = usable & (row_there >= 0) & (row_there < SH) & (col_there >= 0) & (col_there < SW)
    return usable & (tile_mask > 0)


def attend_window(query_rows, planes, allowed):
    tok_rows, inner_width = query_rows.shape
    tile_tok = tok_rows // 4
    query_tiles = query_rows.reshape(4, tile_tok, inner_width)
    mask_full = allowed[:, None, :, None]

    def one_head(head_number, result_rows):
        key_planes = [lax.dynamic_slice_in_dim(plane, head_number * HD, HD, 3) for plane in planes]
        value_planes = [
            lax.dynamic_slice_in_dim(plane, inner_width + head_number * HD, HD, 3)
            for plane in planes
        ]
        key_list = []
        value_list = []
        for row_local in range(2):
            for col_local in range(2):
                key_list.append(
                    jnp.stack(
                        [
                            part[row_local : row_local + 3, col_local : col_local + 3]
                            for part in key_planes
                        ]
                    ).reshape(27 * tile_tok, HD)
                )
                value_list.append(
                    jnp.stack(
                        [
                            part[row_local : row_local + 3, col_local : col_local + 3]
                            for part in value_planes
                        ]
                    ).reshape(27 * tile_tok, HD)
                )
        key_tiles = jnp.stack(key_list)
        value_tiles = jnp.stack(value_list)
        head_query = lax.dynamic_slice_in_dim(query_tiles, head_number * HD, HD, 2)
        scores = jnp.einsum(
            "qtd,qkd->qtk", head_query, key_tiles, preferred_element_type=jnp.float32
        ) / math.sqrt(HD)
        scores = scores.reshape(4, tile_tok, 27, tile_tok)
        scores = jnp.where(mask_full, scores, -1e30)
        row_max = jnp.max(scores, axis=(2, 3), keepdims=True)
        shifted = jnp.where(mask_full, jnp.exp(scores - row_max), 0.0)
        weights = (shifted / jnp.sum(shifted, axis=(2, 3), keepdims=True)).astype(jnp.bfloat16)
        weights = weights.reshape(4, tile_tok, 27 * tile_tok)
        head_out = jnp.einsum(
            "qtk,qkd->qtd", weights, value_tiles, preferred_element_type=jnp.float32
        ).astype(jnp.bfloat16)
        return lax.dynamic_update_slice_in_dim(result_rows, head_out, head_number * HD, 2)

    result_rows = lax.fori_loop(
        0, HEADS, one_head, jnp.zeros((4, tile_tok, inner_width), jnp.bfloat16)
    )
    return result_rows.reshape(tok_rows, inner_width)


def per_device_frames(query_rows, key_rows, value_rows, tile_mask, head_weight, latent, step_index):
    frame_count = lax.axis_size("frame")
    frame_index = lax.axis_index("frame")
    half_size = frame_count // 2
    block_cols = SW // 2
    block_count = SH // 2 * block_cols
    tile_frames = frame_count // (2 * block_count)
    frame_tile = frame_index // block_count % tile_frames
    block_spot = frame_index % block_count
    block_row = block_spot // block_cols
    block_col = block_spot % block_cols
    tok_rows, inner_width = query_rows.shape
    tile_tok = tok_rows // 4
    stacked = jnp.concatenate([key_rows, value_rows], axis=1).reshape(
        2, 2, tile_tok, 2 * inner_width
    )
    planes = direct_window(stacked, block_count, block_cols)
    allowed = window_allowed(tile_mask, frame_tile, block_row, block_col, tile_frames)
    attention = attend_window(query_rows, planes, allowed)
    velocity = jnp.dot(attention, head_weight, preferred_element_type=jnp.float32)
    partner_rows = passed_along(velocity, "frame", half_size)
    is_cond = frame_index < half_size
    cond_rows = jnp.where(is_cond, velocity, partner_rows)
    uncond_rows = jnp.where(is_cond, partner_rows, velocity)
    guided = uncond_rows + GUIDANCE * (cond_rows - uncond_rows)
    moment = step_index[0].astype(jnp.float32)
    sigma_now = flow_sigma(moment)
    step_size = flow_sigma(moment + 1.0) - sigma_now
    clean = latent - sigma_now * guided
    latent_next = latent + step_size * guided
    return (guided, clean, latent_next)


NEG = -1e30
EXP_SCALE = math.log2(math.e) / math.sqrt(HD)
GROUP = 4


def contract_last(left, right):
    return lax.dot_general(
        left, right, (((1,), (1,)), ((), ())), preferred_element_type=jnp.float32
    )


def contract(left, right):
    return jnp.dot(left, right, preferred_element_type=jnp.float32)


def spread(flags, tile_tok):
    lanes = len(flags) * tile_tok
    lane = lax.broadcasted_iota(jnp.int32, (1, lanes), 1)
    row = jnp.zeros((1, lanes), jnp.float32)
    for number, flag in enumerate(flags):
        bias = jnp.where(flag, jnp.float32(0.0), jnp.float32(NEG))
        inside = (lane >= number * tile_tok) & (lane < (number + 1) * tile_tok)
        row = jnp.where(inside, bias, row)
    return row


def biased(scores, rows, tile_tok):
    return jnp.concatenate(
        [scores[t * tile_tok : (t + 1) * tile_tok] + row for t, row in enumerate(rows)],
        axis=0,
    )


def folded_values(weight_t, values):
    exact = contract_last(weight_t, values)
    high = exact.astype(jnp.bfloat16)
    low = (exact - high.astype(jnp.float32)).astype(jnp.bfloat16)
    return jnp.concatenate([high, low], axis=0)


def weighted(pair, weights):
    both = contract(pair, weights)
    half = both.shape[0] // 2
    return both[:half] + both[half:]


def spot_of(index_ref, block_count, block_cols):
    spot = index_ref[0] % block_count
    block_row = spot // block_cols
    block_col = spot % block_cols
    return block_row, block_col, block_col % 2


def per_head(step):
    def run(group, carry):
        for inner in range(GROUP):
            step(group * GROUP + inner)
        return carry

    lax.fori_loop(0, HEADS // GROUP, run, 0)


def head_lanes(head):
    return pl.ds(pl.multiple_of(head * HD, HD), HD)


def own_kernel(
    block_count, block_cols, tile_tok,
    index_ref, mask_ref, query_ref, key_ref, value_ref, inner_ref, weight_ref,
    out_ref, top_ref, sum_ref,
):
    _, _, odd = spot_of(index_ref, block_count, block_cols)
    side = 1 - 2 * odd
    rows = []
    for key_tile in range(4):
        flags = []
        for tile in range(4):
            row_step = key_tile // 2 - tile // 2
            col_step = key_tile % 2 - tile % 2
            flags.append(mask_ref[tile, 9 + 3 * (row_step + 1) + col_step + 1] > 0)
        rows.append(spread(flags, tile_tok))
    for key_row in range(2):
        flags = []
        for tile in range(4):
            row_step = key_row - tile // 2
            entry = mask_ref[tile, 9 + 3 * (row_step + 1) + side + 1] > 0
            flags.append(entry & (tile % 2 == 1 - odd))
        rows.append(spread(flags, tile_tok))

    def step(head):
        lanes = head_lanes(head)
        query = query_ref[:, lanes]
        weight_t = weight_ref[:, lanes]
        scores = jnp.concatenate(
            [
                contract_last(key_ref[:, lanes], query),
                contract_last(inner_ref[0, :, lanes], query),
            ],
            axis=0,
        )
        scores = biased(scores, rows, tile_tok)
        top = jnp.max(scores, axis=0, keepdims=True)
        weights = jnp.exp2((scores - top) * EXP_SCALE)
        top_ref[pl.ds(head, 1), :] = top
        sum_ref[pl.ds(head, 1), :] = jnp.sum(weights, axis=0, keepdims=True)
        pair = jnp.concatenate(
            [
                folded_values(weight_t, value_ref[:, lanes]),
                folded_values(weight_t, inner_ref[1, :, lanes]),
            ],
            axis=1,
        )
        out_ref[head] = weighted(pair, weights.astype(jnp.bfloat16))

    per_head(step)


def edge_kernel(
    block_count, block_cols, tile_tok,
    index_ref, mask_ref, guest_mask_ref,
    query_ref, key_ref, value_ref, inner_ref, outer_ref, guest_ref, weight_ref,
    old_out_ref, old_top_ref, old_sum_ref,
    out_ref, guest_out_ref, top_ref, sum_ref, send_ref,
):
    block_row, block_col, odd = spot_of(index_ref, block_count, block_cols)
    side = 2 * odd - 1
    there = (block_col + side >= 0) & (block_col + side < block_cols)
    edge_row = 1 - block_row
    edge_rows = pl.ds(pl.multiple_of(edge_row * 2 * tile_tok, 2 * tile_tok), 2 * tile_tok)
    halo_rows = pl.ds(pl.multiple_of(edge_row * tile_tok, tile_tok), tile_tok)
    guest_step = 2 * block_row - 1
    rows = []
    for key_row in range(2):
        flags = []
        for tile in range(4):
            row_step = key_row - tile // 2
            entry = mask_ref[tile, 9 + 3 * (row_step + 1) + side + 1] > 0
            flags.append(entry & (tile % 2 == odd) & there)
        rows.append(spread(flags, tile_tok))
    guest_rows = []
    base = 9 + 3 * (guest_step + 1) + 1
    for key_col in range(2):
        guest_rows.append(
            spread(
                [guest_mask_ref[col, base + key_col - col] > 0.5 for col in range(2)],
                tile_tok,
            )
        )
    guest_rows.append(
        spread(
            [
                (guest_mask_ref[col, base - side] > 0.5) & (col == 1 - odd)
                for col in range(2)
            ],
            tile_tok,
        )
    )
    guest_rows.append(
        spread(
            [
                (guest_mask_ref[col, base + side] > 0.5) & (col == odd) & there
                for col in range(2)
            ],
            tile_tok,
        )
    )

    def step(head):
        lanes = head_lanes(head)
        weight_t = weight_ref[:, lanes]
        outer_pair = folded_values(weight_t, outer_ref[1, :, lanes])
        scores = biased(
            contract_last(outer_ref[0, :, lanes], query_ref[:, lanes]), rows, tile_tok
        )
        old_top = old_top_ref[pl.ds(head, 1), :]
        top = jnp.maximum(old_top, jnp.max(scores, axis=0, keepdims=True))
        shrink = jnp.exp2((old_top - top) * EXP_SCALE)
        weights = jnp.exp2((scores - top) * EXP_SCALE)
        top_ref[pl.ds(head, 1), :] = top
        sum_ref[pl.ds(head, 1), :] = shrink * old_sum_ref[pl.ds(head, 1), :] + jnp.sum(
            weights, axis=0, keepdims=True
        )
        out_ref[head] = shrink * old_out_ref[head] + weighted(
            outer_pair, weights.astype(jnp.bfloat16)
        )
        guest_keys = jnp.concatenate(
            [
                key_ref[edge_rows, lanes],
                inner_ref[0, halo_rows, lanes],
                outer_ref[0, halo_rows, lanes],
            ],
            axis=0,
        )
        guest_values = jnp.concatenate(
            [
                value_ref[edge_rows, lanes],
                inner_ref[1, halo_rows, lanes],
                outer_ref[1, halo_rows, lanes],
            ],
            axis=0,
        )
        guest_scores = biased(
            contract_last(guest_keys, guest_ref[:, lanes]), guest_rows, tile_tok
        )
        guest_top = jnp.max(guest_scores, axis=0, keepdims=True)
        guest_weights = jnp.exp2((guest_scores - guest_top) * EXP_SCALE)
        send_ref[2, pl.ds(head, 1), :] = guest_top
        send_ref[3, pl.ds(head, 1), :] = jnp.sum(guest_weights, axis=0, keepdims=True)
        guest_out_ref[head] = weighted(
            folded_values(weight_t, guest_values), guest_weights.astype(jnp.bfloat16)
        )

    per_head(step)
    send_ref[0] = top_ref[:, edge_rows]
    send_ref[1] = sum_ref[:, edge_rows]


def blend_kernel(
    block_count, block_cols, tile_tok,
    index_ref, out_ref, guest_out_ref, top_ref, sum_ref, sent_ref, got_ref,
    velocity_ref, guest_velocity_ref, far_top, far_sum,
):
    block_row, _, _ = spot_of(index_ref, block_count, block_cols)
    edge_lanes = pl.ds(
        pl.multiple_of((1 - block_row) * 2 * tile_tok, 2 * tile_tok), 2 * tile_tok
    )
    far_top[...] = jnp.full_like(far_top, NEG)
    far_sum[...] = jnp.zeros_like(far_sum)
    far_top[:, edge_lanes] = got_ref[2]
    far_sum[:, edge_lanes] = got_ref[3]

    def share(near_top, near_sum, away_top, away_sum):
        top = jnp.maximum(near_top, away_top)
        near = jnp.exp2((near_top - top) * EXP_SCALE)
        away = jnp.exp2((away_top - top) * EXP_SCALE)
        return near / (near * near_sum + away * away_sum)

    own_share = share(top_ref[...], sum_ref[...], far_top[...], far_sum[...])
    guest_share = share(sent_ref[2], sent_ref[3], got_ref[0], got_ref[1])
    velocity = jnp.zeros(velocity_ref.shape, jnp.float32)
    guest_velocity = jnp.zeros(guest_velocity_ref.shape, jnp.float32)
    for head in range(HEADS):
        velocity = velocity + own_share[head : head + 1] * out_ref[head]
        guest_velocity = guest_velocity + guest_share[head : head + 1] * guest_out_ref[head]
    velocity_ref[...] = velocity
    guest_velocity_ref[...] = guest_velocity


def kernel_call(body, args, outs, smem, scratch=()):
    specs = [
        pl.BlockSpec(memory_space=pltpu.SMEM if number < smem else pltpu.VMEM)
        for number in range(len(args))
    ]
    return pl.pallas_call(
        body,
        out_shape=[jax.ShapeDtypeStruct(shape, jnp.float32) for shape in outs],
        in_specs=specs,
        out_specs=[pl.BlockSpec(memory_space=pltpu.VMEM) for _ in outs],
        scratch_shapes=list(scratch),
    )(*args)


def per_device(query_rows, key_rows, value_rows, tile_mask, head_weight, latent, step_index):
    frame_count = lax.axis_size("frame")
    half_size = frame_count // 2
    block_cols = SW // 2
    block_rows = SH // 2
    block_count = block_rows * block_cols
    if half_size != block_count or block_rows != 2 or block_cols % 2:
        return per_device_frames(
            query_rows, key_rows, value_rows, tile_mask, head_weight, latent, step_index
        )
    frame_index = lax.axis_index("frame")
    spot = frame_index % block_count
    edge_row = 1 - spot // block_cols
    odd = spot % 2
    tok_rows, width = query_rows.shape
    tile_tok = tok_rows // 4
    channels = head_weight.shape[1]
    places = range(frame_count)
    row_pairs = [
        (f, f + block_cols if f % block_count < block_cols else f - block_cols)
        for f in places
    ]
    mate_pairs = [(f, f + 1 - 2 * (f % 2)) for f in places]
    side_pairs = []
    for f in places:
        step = 2 * (f % 2) - 1
        if 0 <= f % block_cols + step < block_cols:
            side_pairs.append((f, f + step))
    branch_pairs = [(f, (f + half_size) % frame_count) for f in places]

    guest_query = lax.ppermute(
        lax.dynamic_slice_in_dim(query_rows, edge_row * 2 * tile_tok, 2 * tile_tok, 0),
        "frame",
        row_pairs,
    )
    grid = (2, 2, tile_tok, width)

    def column(number):
        parts = [
            lax.dynamic_index_in_dim(rows.reshape(grid), number, 1, keepdims=False)
            for rows in (key_rows, value_rows)
        ]
        return jnp.stack(parts).reshape(2, 2 * tile_tok, width)

    outer = lax.ppermute(column(odd), "frame", side_pairs)
    inner = lax.ppermute(column(1 - odd), "frame", mate_pairs)
    guest_mask = lax.ppermute(
        lax.dynamic_slice_in_dim(tile_mask, edge_row * 2, 2, 0).astype(jnp.float32),
        "frame",
        row_pairs,
    )
    index = frame_index.astype(jnp.int32).reshape(1)
    weight_t = head_weight.T
    sizes = (block_count, block_cols, tile_tok)
    stats = (HEADS, tok_rows)
    own_out = (HEADS, channels, tok_rows)
    own, top, total = kernel_call(
        functools.partial(own_kernel, *sizes),
        (index, tile_mask, query_rows, key_rows, value_rows, inner, weight_t),
        (own_out, stats, stats),
        2,
    )
    own, guest_out, top, total, sent = kernel_call(
        functools.partial(edge_kernel, *sizes),
        (
            index, tile_mask, guest_mask, query_rows, key_rows, value_rows, inner, outer,
            guest_query, weight_t, own, top, total,
        ),
        (
            own_out,
            (HEADS, channels, 2 * tile_tok),
            stats,
            stats,
            (4, HEADS, 2 * tile_tok),
        ),
        3,
    )
    got = lax.ppermute(sent, "frame", row_pairs)
    velocity, guest_velocity = kernel_call(
        functools.partial(blend_kernel, *sizes),
        (index, own, guest_out, top, total, sent, got),
        ((channels, tok_rows), (channels, 2 * tile_tok)),
        1,
        (pltpu.VMEM(stats, jnp.float32), pltpu.VMEM(stats, jnp.float32)),
    )
    back = lax.ppermute(guest_velocity, "frame", row_pairs)
    lane = jnp.arange(tok_rows)[None, :] // (2 * tile_tok)
    velocity = velocity + jnp.where(lane == edge_row, jnp.tile(back, (1, 2)), 0.0)
    partner = lax.ppermute(velocity, "frame", branch_pairs)
    is_cond = frame_index < half_size
    cond = jnp.where(is_cond, velocity, partner).T
    uncond = jnp.where(is_cond, partner, velocity).T
    guided = uncond + GUIDANCE * (cond - uncond)
    moment = step_index[0].astype(jnp.float32)
    sigma_now = flow_sigma(moment)
    step_size = flow_sigma(moment + 1.0) - sigma_now
    clean = latent - sigma_now * guided
    latent_next = latent + step_size * guided
    return (guided, clean, latent_next)


def solution(mesh):
    placed = (
        P(("groups", "frame"), None),
        P(("groups", "frame"), None),
        P(("groups", "frame"), None),
        P(("groups", "frame"), None),
        P(),
        P(("groups", "frame"), None),
        P("groups"),
    )
    return jax.shard_map(
        per_device,
        mesh=mesh,
        in_specs=placed,
        out_specs=(
            P(("groups", "frame"), None),
            P(("groups", "frame"), None),
            P(("groups", "frame"), None),
        ),
        check_vma=False,
    )
```

```python
import functools
import math

import jax
import jax.numpy as jnp
from jax import lax
from jax.experimental import pallas as pl
from jax.experimental.pallas import tpu as pltpu
from jax.sharding import PartitionSpec as P


HEADS = 20
HD = 128
SH = 4
SW = 8
SAMPLE_STEPS = 50


GUIDANCE = 5.0
FLOW_SHIFT = 5.0


def passed_along(value, axis, steps):
    count = lax.axis_size(axis)
    pairs = [(source, (source + steps) % count) for source in range(count)]
    return lax.ppermute(value, axis, pairs)


def flow_sigma(moment):
    remain = 1.0 - moment / SAMPLE_STEPS
    return FLOW_SHIFT * remain / (1.0 + (FLOW_SHIFT - 1.0) * remain)


def edge_range(offset):
    if offset < 0:
        return (1, 2)
    if offset > 0:
        return (0, 1)
    return (0, 2)


def direct_window(stacked, block_count, block_cols):
    received_parts = {}
    for frame_step in (1, 0, -1):
        for row_step in (1, 0, -1):
            for col_step in (1, 0, -1):
                distance = frame_step * block_count + row_step * block_cols + col_step
                row_start, row_stop = edge_range(row_step)
                col_start, col_stop = edge_range(col_step)
                outgoing = stacked[row_start:row_stop, col_start:col_stop]
                if frame_step == 0 and row_step == 0 and (col_step == 0):
                    received = outgoing
                elif row_step == 0 and col_step == 0:
                    received = passed_along(outgoing, "frame", -distance)
                elif row_step != 0 and col_step != 0:
                    received = passed_along(outgoing, "frame", -distance)
                else:
                    received = passed_along(outgoing, "frame", -distance)
                received_parts[frame_step, row_step, col_step] = received
    planes = []
    for frame_step in (-1, 0, 1):
        row_parts = []
        for row_step in (-1, 0, 1):
            col_parts = [received_parts[frame_step, row_step, col_step] for col_step in (-1, 0, 1)]
            row_parts.append(jnp.concatenate(col_parts, axis=1))
        planes.append(jnp.concatenate(row_parts, axis=0))
    return planes


def window_allowed(tile_mask, frame_tile, block_row, block_col, tile_frames):
    offsets = jnp.arange(27, dtype=jnp.int32)
    frame_step = offsets // 9 - 1
    row_step = offsets // 3 % 3 - 1
    col_step = offsets % 3 - 1
    local_tile = jnp.arange(4, dtype=jnp.int32)
    tile_row = 2 * block_row + local_tile // 2
    tile_col = 2 * block_col + local_tile % 2
    frame_there = frame_tile + frame_step
    row_there = tile_row[:, None] + row_step[None, :]
    col_there = tile_col[:, None] + col_step[None, :]
    usable = ((frame_there >= 0) & (frame_there < tile_frames))[None, :]
    usable = usable & (row_there >= 0) & (row_there < SH) & (col_there >= 0) & (col_there < SW)
    return usable & (tile_mask > 0)


def attend_window(query_rows, planes, allowed):
    tok_rows, inner_width = query_rows.shape
    tile_tok = tok_rows // 4
    query_tiles = query_rows.reshape(4, tile_tok, inner_width)
    mask_full = allowed[:, None, :, None]

    def one_head(head_number, result_rows):
        key_planes = [lax.dynamic_slice_in_dim(plane, head_number * HD, HD, 3) for plane in planes]
        value_planes = [
            lax.dynamic_slice_in_dim(plane, inner_width + head_number * HD, HD, 3)
            for plane in planes
        ]
        key_list = []
        value_list = []
        for row_local in range(2):
            for col_local in range(2):
                key_list.append(
                    jnp.stack(
                        [
                            part[row_local : row_local + 3, col_local : col_local + 3]
                            for part in key_planes
                        ]
                    ).reshape(27 * tile_tok, HD)
                )
                value_list.append(
                    jnp.stack(
                        [
                            part[row_local : row_local + 3, col_local : col_local + 3]
                            for part in value_planes
                        ]
                    ).reshape(27 * tile_tok, HD)
                )
        key_tiles = jnp.stack(key_list)
        value_tiles = jnp.stack(value_list)
        head_query = lax.dynamic_slice_in_dim(query_tiles, head_number * HD, HD, 2)
        scores = jnp.einsum(
            "qtd,qkd->qtk", head_query, key_tiles, preferred_element_type=jnp.float32
        ) / math.sqrt(HD)
        scores = scores.reshape(4, tile_tok, 27, tile_tok)
        scores = jnp.where(mask_full, scores, -1e30)
        row_max = jnp.max(scores, axis=(2, 3), keepdims=True)
        shifted = jnp.where(mask_full, jnp.exp(scores - row_max), 0.0)
        weights = (shifted / jnp.sum(shifted, axis=(2, 3), keepdims=True)).astype(jnp.bfloat16)
        weights = weights.reshape(4, tile_tok, 27 * tile_tok)
        head_out = jnp.einsum(
            "qtk,qkd->qtd", weights, value_tiles, preferred_element_type=jnp.float32
        ).astype(jnp.bfloat16)
        return lax.dynamic_update_slice_in_dim(result_rows, head_out, head_number * HD, 2)

    result_rows = lax.fori_loop(
        0, HEADS, one_head, jnp.zeros((4, tile_tok, inner_width), jnp.bfloat16)
    )
    return result_rows.reshape(tok_rows, inner_width)


def per_device_frames(query_rows, key_rows, value_rows, tile_mask, head_weight, latent, step_index):
    frame_count = lax.axis_size("frame")
    frame_index = lax.axis_index("frame")
    half_size = frame_count // 2
    block_cols = SW // 2
    block_count = SH // 2 * block_cols
    tile_frames = frame_count // (2 * block_count)
    frame_tile = frame_index // block_count % tile_frames
    block_spot = frame_index % block_count
    block_row = block_spot // block_cols
    block_col = block_spot % block_cols
    tok_rows, inner_width = query_rows.shape
    tile_tok = tok_rows // 4
    stacked = jnp.concatenate([key_rows, value_rows], axis=1).reshape(
        2, 2, tile_tok, 2 * inner_width
    )
    planes = direct_window(stacked, block_count, block_cols)
    allowed = window_allowed(tile_mask, frame_tile, block_row, block_col, tile_frames)
    attention = attend_window(query_rows, planes, allowed)
    velocity = jnp.dot(attention, head_weight, preferred_element_type=jnp.float32)
    partner_rows = passed_along(velocity, "frame", half_size)
    is_cond = frame_index < half_size
    cond_rows = jnp.where(is_cond, velocity, partner_rows)
    uncond_rows = jnp.where(is_cond, partner_rows, velocity)
    guided = uncond_rows + GUIDANCE * (cond_rows - uncond_rows)
    moment = step_index[0].astype(jnp.float32)
    sigma_now = flow_sigma(moment)
    step_size = flow_sigma(moment + 1.0) - sigma_now
    clean = latent - sigma_now * guided
    latent_next = latent + step_size * guided
    return (guided, clean, latent_next)


NEG = -1e30
VMEM_LIMIT = 16 << 20
PIECES = 4
EXP_SCALE = math.log2(math.e) / math.sqrt(HD)


def contract_last(left, right):
    return lax.dot_general(
        left, right, (((1,), (1,)), ((), ())), preferred_element_type=jnp.float32
    )


def contract(left, right):
    return jnp.dot(left, right, preferred_element_type=jnp.float32)


def head_lanes(head):
    return slice(head * HD, (head + 1) * HD)


class Spot:
    def __init__(self, index, block_count, block_cols):
        spot = index % block_count
        block_row = spot // block_cols
        block_col = spot % block_cols
        odd = block_col % 2
        self.edge = 1 - block_row
        self.rest = block_row
        self.near = 1 - odd
        self.far = odd
        self.near_step = 1 - 2 * odd
        self.far_step = 2 * odd - 1
        side = block_col + self.far_step
        self.there = (side >= 0) & (side < block_cols)
        self.guest_step = 2 * block_row - 1
        self.lane_tiles = (
            (self.rest, self.near),
            (self.edge, self.near),
            (self.edge, self.far),
            (self.rest, self.far),
        )
        self.key_tiles = (
            (self.edge, self.near),
            (self.rest, self.near),
            (self.rest, self.far),
            (self.edge, self.far),
        )


def tile_rows(tile, tile_tok):
    row, col = tile
    return pl.ds(pl.multiple_of((2 * row + col) * tile_tok, tile_tok), tile_tok)


def entry(row_step, col_step):
    return 9 + 3 * (row_step + 1) + col_step + 1


def bias_of(flag):
    return jnp.where(flag, jnp.float32(0.0), jnp.float32(NEG))


def key_bias(rows, tile_tok):
    biases = []
    for flags in rows:
        lanes = len(flags) * tile_tok
        lane = lax.broadcasted_iota(jnp.int32, (1, lanes), 1) // tile_tok
        bias = jnp.zeros((1, lanes), jnp.float32)
        for number, flag in enumerate(flags):
            bias = jnp.where(lane == number, bias_of(flag), bias)
        biases.append(bias)
    return biases


def biased(scores, biases, tile_tok):
    return above(
        *[scores[t * tile_tok : (t + 1) * tile_tok] + row for t, row in enumerate(biases)]
    )


def beside(left, right):
    return jnp.concatenate([left, right], axis=1)


def above(*parts):
    return jnp.concatenate(parts, axis=0)


def largest(scores):
    return jnp.max(scores, axis=0, keepdims=True)


def softened(scores, top):
    return jnp.exp2((scores - top) * EXP_SCALE).astype(jnp.bfloat16)


def with_ones(folded):
    return above(folded, jnp.ones((16, folded.shape[1]), folded.dtype))


def pipelined(*stages):
    for turn in range(HEADS + len(stages) - 1):
        for number, stage in enumerate(stages):
            if 0 <= turn - number < HEADS:
                stage(turn - number)


def folded_at(width, channels, head):
    row = head % 2 * channels
    lane = width + head // 2 * 2 * channels
    return slice(row, row + channels), slice(lane, lane + 2 * channels)


def copied(pairs, sems):
    copies = [
        pltpu.make_async_copy(source, target, sems.at[number])
        for number, (source, target) in enumerate(pairs)
    ]
    for copy in copies:
        copy.start()
    return copies


def piece(rows, start, stop):
    return pl.ds(pl.multiple_of(rows.start + start, stop - start), stop - start)


def guest_pack_kernel(block_count, block_cols, tile_tok, index_ref, query_ref, out_ref, sems):
    spot = Spot(index_ref[0], block_count, block_cols)
    step = tile_tok // PIECES
    pairs = []
    for number, col in enumerate((spot.near, spot.far)):
        rows = tile_rows((spot.edge, col), tile_tok)
        for start in range(0, tile_tok, step):
            source = query_ref.at[piece(rows, start, start + step)]
            pairs.append((source, out_ref.at[pl.ds(number * tile_tok + start, step)]))
    for copy in copied(pairs, sems):
        copy.wait()


def column_pack_kernel(
    block_count, block_cols, tile_tok,
    index_ref, key_ref, value_ref, weight_ref, near_ref, far_ref, values, weight, sems,
):
    spot = Spot(index_ref[0], block_count, block_cols)
    channels, width = weight_ref.shape
    half = 2 * tile_tok
    pairs = [(weight_ref, weight)]
    for number, tile in enumerate(spot.key_tiles):
        rows = pl.ds(number * tile_tok, tile_tok)
        pairs.append((value_ref.at[tile_rows(tile, tile_tok)], values.at[rows]))
    for number, tile in enumerate(spot.key_tiles):
        out_ref = (near_ref, far_ref)[number // 2]
        target = out_ref.at[pl.ds(number % 2 * tile_tok, tile_tok), pl.ds(0, width)]
        pairs.append((key_ref.at[tile_rows(tile, tile_tok)], target))
    copies = copied(pairs, sems)
    for copy in copies[:5]:
        copy.wait()
    for head in range(HEADS):
        lanes = head_lanes(head)
        folded = contract_last(weight[:, lanes], values[:, lanes]).astype(jnp.bfloat16)
        where = folded_at(width, channels, head)
        near_ref[where] = folded[:, :half]
        far_ref[where] = folded[:, half:]
    for copy in copies[5:]:
        copy.wait()


def own_kernel(
    block_count, block_cols, tile_tok,
    index_ref, mask_ref, query_ref, near_ref, far_ref, inner_ref,
    out_ref, top_ref, sum_ref,
    own_scores, halo_scores, own_weights, halo_weights,
):
    spot = Spot(index_ref[0], block_count, block_cols)
    width = query_ref.shape[1]
    channels = out_ref.shape[1]
    half = 2 * tile_tok

    def flag(tile, row_step, col_step):
        return mask_ref[2 * tile[0] + tile[1], entry(row_step, col_step)] > 0

    bias = key_bias(
        [
            [flag(t, key[0] - t[0], key[1] - t[1]) for t in spot.lane_tiles]
            for key in spot.key_tiles
        ],
        tile_tok,
    )
    halo_bias = key_bias(
        [
            [flag(t, row - t[0], spot.near_step) for t in spot.lane_tiles[:2]]
            for row in (spot.edge, spot.rest)
        ],
        tile_tok,
    )
    places = [tile_rows(tile, tile_tok) for tile in spot.lane_tiles]

    def score(head):
        lanes = head_lanes(head)
        query = above(*[query_ref[place, lanes] for place in places])
        keys = above(near_ref[:, lanes], far_ref[:, lanes])
        own = biased(contract_last(keys, query), bias, tile_tok)
        halo = biased(
            contract_last(inner_ref[:, lanes], query[:half]), halo_bias, tile_tok
        )
        own_scores[head] = own
        halo_scores[head] = halo
        top = largest(own)
        top_ref[head : head + 1, :half] = jnp.maximum(top[:, :half], largest(halo))
        top_ref[head : head + 1, half:] = top[:, half:]

    def soften(head):
        top = top_ref[head : head + 1]
        own_weights[head] = softened(own_scores[head], top)
        halo_weights[head] = softened(halo_scores[head], top[:, :half])

    def weigh(head):
        where = folded_at(width, channels, head)
        folded = with_ones(beside(near_ref[where], far_ref[where]))
        own = contract(folded, own_weights[head])
        halo = contract(with_ones(inner_ref[where]), halo_weights[head])
        left = own[:, :half] + halo
        out_ref[head, :, :half] = left[:channels]
        out_ref[head, :, half:] = own[:channels, half:]
        sum_ref[head : head + 1, :half] = left[channels : channels + 1]
        sum_ref[head : head + 1, half:] = own[channels : channels + 1, half:]

    pipelined(score, soften, weigh)


def edge_kernel(
    block_count, block_cols, tile_tok,
    index_ref, mask_ref, guest_mask_ref,
    query_ref, near_ref, far_ref, inner_ref, outer_ref, guest_ref, own_top_ref, own_sum_ref,
    out_ref, guest_out_ref, side_top_ref, top_ref, sum_ref, send_ref,
    side_scores, guest_scores, side_weights, guest_weights,
):
    spot = Spot(index_ref[0], block_count, block_cols)
    width = query_ref.shape[1]
    channels = out_ref.shape[1]
    half = 2 * tile_tok

    def flag(tile, row_step, col_step):
        return mask_ref[2 * tile[0] + tile[1], entry(row_step, col_step)] > 0

    def guest_flag(col, col_step):
        return guest_mask_ref[col, entry(spot.guest_step, col_step)] > 0.5

    never = spot.near < 0
    bias = key_bias(
        [
            [flag(t, row - t[0], spot.far_step) & spot.there for t in spot.lane_tiles[2:]]
            for row in (spot.rest, spot.edge)
        ],
        tile_tok,
    )
    guest_bias = key_bias(
        [
            [guest_flag(col, key - col) for col in (spot.near, spot.far)]
            for key in (spot.near, spot.far)
        ]
        + [
            [guest_flag(spot.near, spot.near_step), never],
            [never, guest_flag(spot.far, spot.far_step) & spot.there],
        ],
        tile_tok,
    )
    places = [tile_rows(tile, tile_tok) for tile in spot.lane_tiles[2:]]
    left = lax.broadcasted_iota(jnp.int32, (channels, half), 1) < tile_tok

    def score(head):
        lanes = head_lanes(head)
        query = above(*[query_ref[place, lanes] for place in places])
        scores = biased(contract_last(outer_ref[:, lanes], query), bias, tile_tok)
        side_scores[head] = scores
        side_top_ref[head : head + 1] = largest(scores)
        keys = above(
            near_ref[:tile_tok, lanes],
            far_ref[tile_tok:, lanes],
            inner_ref[:tile_tok, lanes],
            outer_ref[tile_tok:, lanes],
        )
        scores = biased(contract_last(keys, guest_ref[:, lanes]), guest_bias, tile_tok)
        guest_scores[head] = scores
        send_ref[2, head : head + 1] = largest(scores)

    def soften(head):
        side_weights[head] = softened(side_scores[head], side_top_ref[head : head + 1])
        guest_weights[head] = softened(guest_scores[head], send_ref[2, head : head + 1])

    def weigh(head):
        where = folded_at(width, channels, head)
        side = contract(with_ones(outer_ref[where]), side_weights[head])
        out_ref[head] = side[:channels]
        sum_ref[head : head + 1, half:] = side[channels : channels + 1]
        folded = beside(
            jnp.where(left, near_ref[where], far_ref[where]),
            jnp.where(left, inner_ref[where], outer_ref[where]),
        )
        guest = contract(with_ones(folded), guest_weights[head])
        guest_out_ref[head] = guest[:channels]
        send_ref[3, head : head + 1] = guest[channels : channels + 1]

    pipelined(score, soften, weigh)

    near_top = own_top_ref[:, :half]
    near_sum = own_sum_ref[:, :half]
    old_top = own_top_ref[:, half:]
    side_top = side_top_ref[...]
    far_top = jnp.maximum(old_top, side_top)
    far_sum = (
        jnp.exp2((old_top - far_top) * EXP_SCALE) * own_sum_ref[:, half:]
        + jnp.exp2((side_top - far_top) * EXP_SCALE) * sum_ref[:, half:]
    )
    top_ref[:, :half] = near_top
    top_ref[:, half:] = far_top
    sum_ref[:, :half] = near_sum
    sum_ref[:, half:] = far_sum
    send_ref[0] = beside(near_top[:, tile_tok:], far_top[:, :tile_tok])
    send_ref[1] = beside(near_sum[:, tile_tok:], far_sum[:, :tile_tok])


def shares(near_top, near_sum, away_top, away_sum):
    top = jnp.maximum(near_top, away_top)
    near = jnp.exp2((near_top - top) * EXP_SCALE) * near_sum
    away = jnp.exp2((away_top - top) * EXP_SCALE) * away_sum
    return top, near + away


def centred(values, fill, tile_tok):
    side = jnp.full((values.shape[0], tile_tok), fill, values.dtype)
    return jnp.concatenate([side, values, side], axis=1)


def blend_kernel(
    tile_tok,
    own_out_ref, side_out_ref, guest_out_ref, own_top_ref, side_top_ref,
    top_ref, sum_ref, sent_ref, got_ref,
    velocity_ref, guest_velocity_ref,
):
    half = 2 * tile_tok
    top, total = shares(
        top_ref[...], sum_ref[...],
        centred(got_ref[2], NEG, tile_tok), centred(got_ref[3], 0.0, tile_tok),
    )
    own_share = jnp.exp2((own_top_ref[...] - top) * EXP_SCALE) / total
    side_share = jnp.exp2((side_top_ref[...] - top[:, half:]) * EXP_SCALE) / total[:, half:]
    guest_top, guest_total = shares(sent_ref[2], sent_ref[3], got_ref[0], got_ref[1])
    guest_share = jnp.exp2((sent_ref[2] - guest_top) * EXP_SCALE) / guest_total
    guest = jnp.zeros(guest_velocity_ref.shape, jnp.float32)
    near = jnp.zeros(guest_velocity_ref.shape, jnp.float32)
    far = jnp.zeros(guest_velocity_ref.shape, jnp.float32)
    for head in range(HEADS):
        one = slice(head, head + 1)
        guest = guest + guest_share[one] * guest_out_ref[head]
        near = near + own_share[one, :half] * own_out_ref[head, :, :half]
        far = far + own_share[one, half:] * own_out_ref[head, :, half:]
        far = far + side_share[one] * side_out_ref[head]
    guest_velocity_ref[...] = guest
    velocity_ref[:, :half] = near
    velocity_ref[:, half:] = far


def join_kernel(tile_tok, velocity_ref, back_ref, out_ref):
    out_ref[...] = velocity_ref[...] + centred(back_ref[...], 0.0, tile_tok)


def update_kernel(
    block_count, block_cols, tile_tok, half_size,
    index_ref, step_ref, velocity_ref, partner_ref, latent_ref,
    guided_ref, clean_ref, next_ref,
):
    spot = Spot(index_ref[0], block_count, block_cols)
    half = 2 * tile_tok
    is_cond = index_ref[0] < half_size
    own = velocity_ref[...]
    other = partner_ref[...]
    cond = jnp.where(is_cond, own, other)
    uncond = jnp.where(is_cond, other, own)
    blended = uncond + GUIDANCE * (cond - uncond)
    edge = blended[:, tile_tok : tile_tok + half]
    rest = jnp.concatenate([blended[:, :tile_tok], blended[:, tile_tok + half :]], axis=1)

    def natural(pair):
        swapped = jnp.concatenate([pair[:, tile_tok:], pair[:, :tile_tok]], axis=1)
        return jnp.where(spot.near == 0, pair, swapped)

    edge = natural(edge)
    rest = natural(rest)
    moment = jnp.full((1, half), step_ref[0].astype(jnp.float32))
    sigma_now = flow_sigma(moment)
    step_size = flow_sigma(moment + 1.0) - sigma_now
    for row in range(2):
        lanes = slice(row * half, (row + 1) * half)
        guided = jnp.where(spot.edge == row, edge, rest)
        latent = latent_ref[:, lanes]
        guided_ref[:, lanes] = guided
        clean_ref[:, lanes] = latent - sigma_now * guided
        next_ref[:, lanes] = latent + step_size * guided


def kernel_call(body, args, outs, smem=0, scratch=(), far=(), stay=True):
    spaces = [pltpu.SMEM] * smem + [pltpu.VMEM] * (len(args) - smem)
    for number in far:
        spaces[number] = pltpu.HBM
    args = [
        arg if space == pltpu.SMEM else pltpu.with_memory_space_constraint(arg, space)
        for arg, space in zip(args, spaces)
    ]
    specs = [pl.BlockSpec(memory_space=space) for space in spaces]
    return pl.pallas_call(
        body,
        out_shape=[
            pltpu.VMEM(shape, dtype) if stay else jax.ShapeDtypeStruct(shape, dtype)
            for shape, dtype in outs
        ],
        in_specs=specs,
        out_specs=[pl.BlockSpec(memory_space=pltpu.VMEM) for _ in outs],
        scratch_shapes=list(scratch),
        compiler_params=pltpu.CompilerParams(vmem_limit_bytes=VMEM_LIMIT),
    )(*args)


def one_frame_tile(frame_count):
    return frame_count == SH // 2 * (SW // 2) * 2 and SH == 4 and SW % 4 == 0


def per_device_plan(query_rows, key_rows, value_rows, tile_mask, head_weight, latent, step_index):
    frame_count = lax.axis_size("frame")
    half_size = frame_count // 2
    block_cols = SW // 2
    block_count = SH // 2 * block_cols
    frame_index = lax.axis_index("frame")
    tok_rows, width = query_rows.shape
    tile_tok = tok_rows // 4
    half = 2 * tile_tok
    channels = head_weight.shape[1]
    places = range(frame_count)
    row_pairs = [
        (f, f + block_cols if f % block_count < block_cols else f - block_cols)
        for f in places
    ]
    mate_pairs = [(f, f + 1 - 2 * (f % 2)) for f in places]
    side_pairs = []
    for f in places:
        step = 2 * (f % 2) - 1
        if 0 <= f % block_cols + step < block_cols:
            side_pairs.append((f, f + step))
    branch_pairs = [(f, (f + half_size) % frame_count) for f in places]
    sizes = (block_count, block_cols, tile_tok)
    index = frame_index.astype(jnp.int32).reshape(1)
    single = jnp.float32
    packed_type = query_rows.dtype

    (guest_send,) = kernel_call(
        functools.partial(guest_pack_kernel, *sizes),
        (index, query_rows),
        (((half, width), packed_type),),
        1,
        (pltpu.SemaphoreType.DMA((2 * PIECES,)),),
        far=(1,),
    )
    guest_send = pltpu.with_memory_space_constraint(guest_send, pltpu.VMEM)
    guest = lax.ppermute(guest_send, "frame", row_pairs)

    packed = (half, width + (HEADS + 1) // 2 * 2 * channels)
    near, far = kernel_call(
        functools.partial(column_pack_kernel, *sizes),
        (index, key_rows, value_rows, head_weight.T),
        ((packed, packed_type), (packed, packed_type)),
        1,
        (
            pltpu.VMEM((tok_rows, width), packed_type),
            pltpu.VMEM((channels, width), packed_type),
            pltpu.SemaphoreType.DMA((9,)),
        ),
        far=(1, 2, 3),
    )
    outer = lax.ppermute(far, "frame", side_pairs)
    inner = lax.ppermute(near, "frame", mate_pairs)
    edge_row = 1 - frame_index % block_count // block_cols
    guest_mask = lax.ppermute(
        lax.dynamic_slice_in_dim(tile_mask, edge_row * 2, 2, 0).astype(single),
        "frame",
        row_pairs,
    )
    stats = ((HEADS, tok_rows), single)
    half_stats = ((HEADS, half), single)
    own_out, own_top, own_sum = kernel_call(
        functools.partial(own_kernel, *sizes),
        (index, tile_mask, query_rows, near, far, inner),
        (((HEADS, channels, tok_rows), single), stats, stats),
        2,
        (
            pltpu.VMEM((HEADS, tok_rows, tok_rows), single),
            pltpu.VMEM((HEADS, half, half), single),
            pltpu.VMEM((HEADS, tok_rows, tok_rows), packed_type),
            pltpu.VMEM((HEADS, half, half), packed_type),
        ),
    )
    half_out = ((HEADS, channels, half), single)
    side_out, guest_out, side_top, top, total, sent = kernel_call(
        functools.partial(edge_kernel, *sizes),
        (
            index, tile_mask, guest_mask, query_rows, near, far, inner, outer, guest,
            own_top, own_sum,
        ),
        (half_out, half_out, half_stats, stats, stats, ((4, HEADS, half), single)),
        3,
        (
            pltpu.VMEM((HEADS, half, half), single),
            pltpu.VMEM((HEADS, tok_rows, half), single),
            pltpu.VMEM((HEADS, half, half), packed_type),
            pltpu.VMEM((HEADS, tok_rows, half), packed_type),
        ),
    )
    got = lax.ppermute(sent, "frame", row_pairs)
    velocity, guest_velocity = kernel_call(
        functools.partial(blend_kernel, tile_tok),
        (own_out, side_out, guest_out, own_top, side_top, top, total, sent, got),
        (((channels, tok_rows), single), ((channels, half), single)),
    )
    back = lax.ppermute(guest_velocity, "frame", row_pairs)
    (velocity,) = kernel_call(
        functools.partial(join_kernel, tile_tok),
        (velocity, back),
        (((channels, tok_rows), single),),
    )
    partner = lax.ppermute(velocity, "frame", branch_pairs)
    out = ((channels, tok_rows), single)
    results = kernel_call(
        functools.partial(update_kernel, *sizes, half_size),
        (index, step_index, velocity, partner, latent.T),
        (out, out, out),
        2,
        stay=False,
    )
    return tuple(result.T for result in results)


def per_device(*args):
    return per_device_plan(*args)


def solution(mesh):
    placed = (
        P(("groups", "frame"), None),
        P(("groups", "frame"), None),
        P(("groups", "frame"), None),
        P(("groups", "frame"), None),
        P(),
        P(("groups", "frame"), None),
        P("groups"),
    )
    fast = one_frame_tile(mesh.shape["frame"])
    return jax.shard_map(
        per_device if fast else per_device_frames,
        mesh=mesh,
        in_specs=placed,
        out_specs=(
            P(("groups", "frame"), None),
            P(("groups", "frame"), None),
            P(("groups", "frame"), None),
        ),
        check_vma=False,
    )
```

```python
import functools
import math

import jax
import jax.numpy as jnp
from jax import lax
from jax.experimental import pallas as pl
from jax.experimental.pallas import tpu as pltpu
from jax.sharding import PartitionSpec as P


HEADS = 20
HD = 128
SH = 4
SW = 8
SAMPLE_STEPS = 50


GUIDANCE = 5.0
FLOW_SHIFT = 5.0


def passed_along(value, axis, steps):
    count = lax.axis_size(axis)
    pairs = [(source, (source + steps) % count) for source in range(count)]
    return lax.ppermute(value, axis, pairs)


def flow_sigma(moment):
    remain = 1.0 - moment / SAMPLE_STEPS
    return FLOW_SHIFT * remain / (1.0 + (FLOW_SHIFT - 1.0) * remain)


def edge_range(offset):
    if offset < 0:
        return (1, 2)
    if offset > 0:
        return (0, 1)
    return (0, 2)


def direct_window(stacked, block_count, block_cols):
    received_parts = {}
    for frame_step in (1, 0, -1):
        for row_step in (1, 0, -1):
            for col_step in (1, 0, -1):
                distance = frame_step * block_count + row_step * block_cols + col_step
                row_start, row_stop = edge_range(row_step)
                col_start, col_stop = edge_range(col_step)
                outgoing = stacked[row_start:row_stop, col_start:col_stop]
                if frame_step == 0 and row_step == 0 and (col_step == 0):
                    received = outgoing
                elif row_step == 0 and col_step == 0:
                    received = passed_along(outgoing, "frame", -distance)
                elif row_step != 0 and col_step != 0:
                    received = passed_along(outgoing, "frame", -distance)
                else:
                    received = passed_along(outgoing, "frame", -distance)
                received_parts[frame_step, row_step, col_step] = received
    planes = []
    for frame_step in (-1, 0, 1):
        row_parts = []
        for row_step in (-1, 0, 1):
            col_parts = [received_parts[frame_step, row_step, col_step] for col_step in (-1, 0, 1)]
            row_parts.append(jnp.concatenate(col_parts, axis=1))
        planes.append(jnp.concatenate(row_parts, axis=0))
    return planes


def window_allowed(tile_mask, frame_tile, block_row, block_col, tile_frames):
    offsets = jnp.arange(27, dtype=jnp.int32)
    frame_step = offsets // 9 - 1
    row_step = offsets // 3 % 3 - 1
    col_step = offsets % 3 - 1
    local_tile = jnp.arange(4, dtype=jnp.int32)
    tile_row = 2 * block_row + local_tile // 2
    tile_col = 2 * block_col + local_tile % 2
    frame_there = frame_tile + frame_step
    row_there = tile_row[:, None] + row_step[None, :]
    col_there = tile_col[:, None] + col_step[None, :]
    usable = ((frame_there >= 0) & (frame_there < tile_frames))[None, :]
    usable = usable & (row_there >= 0) & (row_there < SH) & (col_there >= 0) & (col_there < SW)
    return usable & (tile_mask > 0)


def attend_window(query_rows, planes, allowed):
    tok_rows, inner_width = query_rows.shape
    tile_tok = tok_rows // 4
    query_tiles = query_rows.reshape(4, tile_tok, inner_width)
    mask_full = allowed[:, None, :, None]

    def one_head(head_number, result_rows):
        key_planes = [lax.dynamic_slice_in_dim(plane, head_number * HD, HD, 3) for plane in planes]
        value_planes = [
            lax.dynamic_slice_in_dim(plane, inner_width + head_number * HD, HD, 3)
            for plane in planes
        ]
        key_list = []
        value_list = []
        for row_local in range(2):
            for col_local in range(2):
                key_list.append(
                    jnp.stack(
                        [
                            part[row_local : row_local + 3, col_local : col_local + 3]
                            for part in key_planes
                        ]
                    ).reshape(27 * tile_tok, HD)
                )
                value_list.append(
                    jnp.stack(
                        [
                            part[row_local : row_local + 3, col_local : col_local + 3]
                            for part in value_planes
                        ]
                    ).reshape(27 * tile_tok, HD)
                )
        key_tiles = jnp.stack(key_list)
        value_tiles = jnp.stack(value_list)
        head_query = lax.dynamic_slice_in_dim(query_tiles, head_number * HD, HD, 2)
        scores = jnp.einsum(
            "qtd,qkd->qtk", head_query, key_tiles, preferred_element_type=jnp.float32
        ) / math.sqrt(HD)
        scores = scores.reshape(4, tile_tok, 27, tile_tok)
        scores = jnp.where(mask_full, scores, -1e30)
        row_max = jnp.max(scores, axis=(2, 3), keepdims=True)
        shifted = jnp.where(mask_full, jnp.exp(scores - row_max), 0.0)
        weights = (shifted / jnp.sum(shifted, axis=(2, 3), keepdims=True)).astype(jnp.bfloat16)
        weights = weights.reshape(4, tile_tok, 27 * tile_tok)
        head_out = jnp.einsum(
            "qtk,qkd->qtd", weights, value_tiles, preferred_element_type=jnp.float32
        ).astype(jnp.bfloat16)
        return lax.dynamic_update_slice_in_dim(result_rows, head_out, head_number * HD, 2)

    result_rows = lax.fori_loop(
        0, HEADS, one_head, jnp.zeros((4, tile_tok, inner_width), jnp.bfloat16)
    )
    return result_rows.reshape(tok_rows, inner_width)


def per_device_frames(query_rows, key_rows, value_rows, tile_mask, head_weight, latent, step_index):
    frame_count = lax.axis_size("frame")
    frame_index = lax.axis_index("frame")
    half_size = frame_count // 2
    block_cols = SW // 2
    block_count = SH // 2 * block_cols
    tile_frames = frame_count // (2 * block_count)
    frame_tile = frame_index // block_count % tile_frames
    block_spot = frame_index % block_count
    block_row = block_spot // block_cols
    block_col = block_spot % block_cols
    tok_rows, inner_width = query_rows.shape
    tile_tok = tok_rows // 4
    stacked = jnp.concatenate([key_rows, value_rows], axis=1).reshape(
        2, 2, tile_tok, 2 * inner_width
    )
    planes = direct_window(stacked, block_count, block_cols)
    allowed = window_allowed(tile_mask, frame_tile, block_row, block_col, tile_frames)
    attention = attend_window(query_rows, planes, allowed)
    velocity = jnp.dot(attention, head_weight, preferred_element_type=jnp.float32)
    partner_rows = passed_along(velocity, "frame", half_size)
    is_cond = frame_index < half_size
    cond_rows = jnp.where(is_cond, velocity, partner_rows)
    uncond_rows = jnp.where(is_cond, partner_rows, velocity)
    guided = uncond_rows + GUIDANCE * (cond_rows - uncond_rows)
    moment = step_index[0].astype(jnp.float32)
    sigma_now = flow_sigma(moment)
    step_size = flow_sigma(moment + 1.0) - sigma_now
    clean = latent - sigma_now * guided
    latent_next = latent + step_size * guided
    return (guided, clean, latent_next)


NEG = -1e30
VMEM_LIMIT = 16 << 20
FIRST_HEADS = 14
EXP_SCALE = math.log2(math.e) / math.sqrt(HD)


def contract_last(left, right):
    return lax.dot_general(
        left, right, (((1,), (1,)), ((), ())), preferred_element_type=jnp.float32
    )


def contract(left, right):
    return jnp.dot(left, right, preferred_element_type=jnp.float32)


def head_lanes(head):
    return slice(head * HD, (head + 1) * HD)


class Spot:
    def __init__(self, block_count, block_cols):
        self.index = lax.axis_index("frame")
        spot = self.index % block_count
        block_row = spot // block_cols
        block_col = spot % block_cols
        odd = block_col % 2
        self.edge = 1 - block_row
        self.rest = block_row
        self.near = 1 - odd
        self.far = odd
        self.near_step = 1 - 2 * odd
        self.far_step = 2 * odd - 1
        side = block_col + self.far_step
        self.there = (side >= 0) & (side < block_cols)
        self.guest_step = 2 * block_row - 1
        self.lane_tiles = (
            (self.rest, self.near),
            (self.edge, self.near),
            (self.edge, self.far),
            (self.rest, self.far),
        )
        self.key_tiles = (
            (self.edge, self.near),
            (self.rest, self.near),
            (self.rest, self.far),
            (self.edge, self.far),
        )


def tile_rows(tile, tile_tok):
    row, col = tile
    return pl.ds(pl.multiple_of((2 * row + col) * tile_tok, tile_tok), tile_tok)


def entry(row_step, col_step):
    return 9 + 3 * (row_step + 1) + col_step + 1


def bias_of(flag):
    return jnp.where(flag, jnp.float32(0.0), jnp.float32(NEG))


def key_bias(rows, tile_tok):
    biases = []
    for flags in rows:
        lanes = len(flags) * tile_tok
        lane = lax.broadcasted_iota(jnp.int32, (1, lanes), 1) // tile_tok
        bias = jnp.zeros((1, lanes), jnp.float32)
        for number, flag in enumerate(flags):
            bias = jnp.where(lane == number, bias_of(flag), bias)
        biases.append(bias)
    return biases


def biased(scores, biases, tile_tok):
    return above(
        *[scores[t * tile_tok : (t + 1) * tile_tok] + row for t, row in enumerate(biases)]
    )


def beside(left, right):
    return jnp.concatenate([left, right], axis=1)


def above(*parts):
    return jnp.concatenate(parts, axis=0)


def largest(scores):
    return jnp.max(scores, axis=0, keepdims=True)


def softened(scores, top):
    return jnp.exp2((scores - top) * EXP_SCALE).astype(jnp.bfloat16)


def with_ones(folded):
    return above(folded, jnp.ones((16, folded.shape[1]), folded.dtype))


def pipelined(heads, *stages):
    for turn in range(len(heads) + len(stages) - 1):
        for number, stage in enumerate(stages):
            if 0 <= turn - number < len(heads):
                stage(heads[turn - number])


def packed_width(heads, channels):
    return heads * HD + (heads + 1) // 2 * 2 * channels


class Column:
    def __init__(self, refs, groups, channels):
        self.refs = refs
        self.groups = groups
        self.channels = channels

    def place(self, head):
        for ref, group in zip(self.refs, self.groups):
            if head in group:
                return ref, head - group.start, len(group) * HD

    def keys(self, head):
        ref, local, _ = self.place(head)
        return ref[:, head_lanes(local)]

    def folded_at(self, head):
        ref, local, width = self.place(head)
        row = local % 2 * self.channels
        lane = width + local // 2 * 2 * self.channels
        return ref, (slice(row, row + self.channels), slice(lane, lane + 2 * self.channels))

    def folded(self, head):
        ref, where = self.folded_at(head)
        return ref[where]


def copied(pairs, sems):
    copies = [
        pltpu.make_async_copy(source, target, sems.at[number])
        for number, (source, target) in enumerate(pairs)
    ]
    for copy in copies:
        copy.start()
    return copies


def guest_pack_kernel(
    block_count, block_cols, tile_tok, groups,
    query_ref, mask_ref, weight_ref, *refs
):
    spot = Spot(block_count, block_cols)
    *out_refs, bias_ref, near_weight_ref, mask, sems = refs
    pairs = [(mask_ref, mask), (weight_ref, near_weight_ref)]
    for out_ref, group in zip(out_refs, groups):
        lanes = pl.ds(group.start * HD, len(group) * HD)
        for number, col in enumerate((spot.near, spot.far)):
            rows = tile_rows((spot.edge, col), tile_tok)
            target = out_ref.at[pl.ds(number * tile_tok, tile_tok)]
            pairs.append((query_ref.at[rows, lanes], target))
    for copy in copied(pairs, sems):
        copy.wait()
    steps = -spot.guest_step

    def flag(col, col_step):
        return mask[2 * spot.edge + col, entry(steps, col_step)] > 0

    never = spot.near < 0
    cols = (spot.near, spot.far)
    rows = [[flag(col, key - col) for col in cols] for key in cols] + [
        [flag(spot.near, spot.near_step), never],
        [never, flag(spot.far, spot.far_step) & spot.there],
    ]
    for number, row in enumerate(key_bias(rows, tile_tok)):
        bias_ref[number : number + 1] = row


def column_pack_kernel(
    block_count, block_cols, tile_tok, groups, key_ref, value_ref, weight_ref, *refs
):
    spot = Spot(block_count, block_cols)
    channels = weight_ref.shape[0]
    *far_refs, near_ref, sems = refs[-2 - len(groups) :]
    sides = (
        (spot.key_tiles[2:], far_refs, groups),
        (spot.key_tiles[:2], [near_ref], (range(HEADS),)),
    )
    pairs = []
    for tiles, out_refs, out_groups in sides:
        for out_ref, group in zip(out_refs, out_groups):
            width = len(group) * HD
            for number, tile in enumerate(tiles):
                source = key_ref.at[tile_rows(tile, tile_tok), pl.ds(group.start * HD, width)]
                target = out_ref.at[pl.ds(number * tile_tok, tile_tok), pl.ds(0, width)]
                pairs.append((source, target))
    copies = copied(pairs, sems)
    for tiles, out_refs, out_groups in sides:
        column = Column(out_refs, out_groups, channels)
        places = [tile_rows(tile, tile_tok) for tile in tiles]
        for head in range(HEADS):
            lanes = head_lanes(head)
            values = above(*[value_ref[place, lanes] for place in places])
            folded = contract_last(weight_ref[:, lanes], values)
            ref, where = column.folded_at(head)
            ref[where] = folded.astype(jnp.bfloat16)
    for copy in copies:
        copy.wait()


def own_kernel(
    block_count, block_cols, tile_tok, groups, mask_ref, query_ref, *refs
):
    count = len(groups)
    far_refs = refs[1 : 1 + count]
    out_ref, top_ref, sum_ref, side_bias_ref = refs[2 + count : 6 + count]
    own_scores, halo_scores, own_weights, halo_weights = refs[6 + count :]
    spot = Spot(block_count, block_cols)
    channels = out_ref.shape[1]
    half = 2 * tile_tok
    every = (range(HEADS),)
    near_column = Column(refs[:1], every, channels)
    far_column = Column(far_refs, groups, channels)
    inner_column = Column(refs[1 + count : 2 + count], every, channels)

    def flag(tile, row_step, col_step):
        return mask_ref[2 * tile[0] + tile[1], entry(row_step, col_step)] > 0

    bias = key_bias(
        [
            [flag(t, key[0] - t[0], key[1] - t[1]) for t in spot.lane_tiles]
            for key in spot.key_tiles
        ],
        tile_tok,
    )
    halo_bias = key_bias(
        [
            [flag(t, row - t[0], spot.near_step) for t in spot.lane_tiles[:2]]
            for row in (spot.edge, spot.rest)
        ],
        tile_tok,
    )
    side_rows = [
        [flag(t, row - t[0], spot.far_step) & spot.there for t in spot.lane_tiles[2:]]
        for row in (spot.rest, spot.edge)
    ]
    for number, row in enumerate(key_bias(side_rows, tile_tok)):
        side_bias_ref[number : number + 1] = row
    places = [tile_rows(tile, tile_tok) for tile in spot.lane_tiles]

    def score(head):
        lanes = head_lanes(head)
        query = above(*[query_ref[place, lanes] for place in places])
        keys = above(near_column.keys(head), far_column.keys(head))
        own = biased(contract_last(keys, query), bias, tile_tok)
        halo = biased(
            contract_last(inner_column.keys(head), query[:half]), halo_bias, tile_tok
        )
        own_scores[head] = own
        halo_scores[head] = halo
        top = largest(own)
        top_ref[head : head + 1, :half] = jnp.maximum(top[:, :half], largest(halo))
        top_ref[head : head + 1, half:] = top[:, half:]

    def soften(head):
        top = top_ref[head : head + 1]
        own_weights[head] = softened(own_scores[head], top)
        halo_weights[head] = softened(halo_scores[head], top[:, :half])

    def weigh(head):
        folded = with_ones(beside(near_column.folded(head), far_column.folded(head)))
        own = contract(folded, own_weights[head])
        halo = contract(with_ones(inner_column.folded(head)), halo_weights[head])
        left = own[:, :half] + halo
        out_ref[head, :, :half] = left[:channels]
        out_ref[head, :, half:] = own[:channels, half:]
        sum_ref[head : head + 1, :half] = left[channels : channels + 1]
        sum_ref[head : head + 1, half:] = own[channels : channels + 1, half:]

    pipelined(range(HEADS), score, soften, weigh)


def edge_kernel(
    block_count, block_cols, tile_tok, group,
    side_bias_ref, guest_bias_ref,
    query_ref, near_ref, far_ref, inner_ref, outer_ref, guest_ref, own_top_ref, own_sum_ref,
    out_ref, guest_out_ref, side_top_ref, top_ref, sum_ref, send_ref,
    side_scores, guest_scores, side_weights, guest_weights,
):
    spot = Spot(block_count, block_cols)
    channels = out_ref.shape[1]
    half = 2 * tile_tok
    near_column = Column([near_ref], (range(HEADS),), channels)
    inner_column = Column([inner_ref], (range(HEADS),), channels)
    far_column = Column([far_ref], (group,), channels)
    outer_column = Column([outer_ref], (group,), channels)

    bias = [side_bias_ref[number : number + 1] for number in range(2)]
    guest_bias = [guest_bias_ref[number : number + 1] for number in range(4)]
    places = [tile_rows(tile, tile_tok) for tile in spot.lane_tiles[2:]]
    left = lax.broadcasted_iota(jnp.int32, (channels, half), 1) < tile_tok

    def score(head):
        row = head - group.start
        query = above(*[query_ref[place, head_lanes(head)] for place in places])
        scores = biased(contract_last(outer_column.keys(head), query), bias, tile_tok)
        side_scores[row] = scores
        side_top_ref[row : row + 1] = largest(scores)
        keys = above(
            near_column.keys(head)[:tile_tok],
            far_column.keys(head)[tile_tok:],
            inner_column.keys(head)[:tile_tok],
            outer_column.keys(head)[tile_tok:],
        )
        scores = contract_last(keys, guest_ref[:, head_lanes(row)])
        scores = biased(scores, guest_bias, tile_tok)
        guest_scores[row] = scores
        send_ref[2, row : row + 1] = largest(scores)

    def soften(head):
        row = head - group.start
        side_weights[row] = softened(side_scores[row], side_top_ref[row : row + 1])
        guest_weights[row] = softened(guest_scores[row], send_ref[2, row : row + 1])

    def weigh(head):
        row = head - group.start
        side = contract(with_ones(outer_column.folded(head)), side_weights[row])
        out_ref[row] = side[:channels]
        sum_ref[row : row + 1, half:] = side[channels : channels + 1]
        folded = beside(
            jnp.where(left, near_column.folded(head), far_column.folded(head)),
            jnp.where(left, inner_column.folded(head), outer_column.folded(head)),
        )
        guest = contract(with_ones(folded), guest_weights[row])
        guest_out_ref[row] = guest[:channels].astype(guest_out_ref.dtype)
        send_ref[3, row : row + 1] = guest[channels : channels + 1]

    pipelined(group, score, soften, weigh)

    mine = slice(group.start, group.stop)
    near_top = own_top_ref[mine, :half]
    near_sum = own_sum_ref[mine, :half]
    old_top = own_top_ref[mine, half:]
    side_top = side_top_ref[...]
    far_top, far_sum = shares(
        old_top, own_sum_ref[mine, half:], side_top, sum_ref[:, half:]
    )
    top_ref[:, :half] = near_top
    top_ref[:, half:] = far_top
    sum_ref[:, :half] = near_sum
    sum_ref[:, half:] = far_sum
    send_ref[0] = beside(near_top[:, tile_tok:], far_top[:, :tile_tok])
    send_ref[1] = beside(near_sum[:, tile_tok:], far_sum[:, :tile_tok])


def shares(near_top, near_sum, away_top, away_sum):
    top = jnp.maximum(near_top, away_top)
    near = jnp.exp2((near_top - top) * EXP_SCALE) * near_sum
    away = jnp.exp2((away_top - top) * EXP_SCALE) * away_sum
    return top, near + away


def centred(values, fill, tile_tok):
    side = jnp.full((values.shape[0], tile_tok), fill, values.dtype)
    return jnp.concatenate([side, values, side], axis=1)


def guest_blend_kernel(guest_out_ref, sent_ref, got_ref, late_ref, back_ref):
    heads, channels, _ = guest_out_ref.shape
    top, total = shares(sent_ref[2], sent_ref[3], got_ref[0], got_ref[1])
    share = jnp.exp2((sent_ref[2] - top) * EXP_SCALE) / total
    velocity = jnp.zeros(guest_out_ref.shape[1:], jnp.float32)
    for row in range(heads):
        velocity = velocity + share[row : row + 1] * guest_out_ref[row]
    back_ref[:channels] = velocity
    late = late_ref.shape[1]
    back_ref[channels : channels + late] = late_ref[2]
    back_ref[channels + late : channels + 2 * late] = late_ref[3]


def own_part(tile_tok, group, own_out_ref, side_out_ref, own_top_ref, side_top_ref,
             top, total, far_top, far_total):
    half = 2 * tile_tok
    top, total = shares(
        top, total, centred(far_top, NEG, tile_tok), centred(far_total, 0.0, tile_tok)
    )
    own_top = own_top_ref[group.start : group.stop]
    own_share = jnp.exp2((own_top - top) * EXP_SCALE) / total
    side_share = jnp.exp2((side_top_ref[...] - top[:, half:]) * EXP_SCALE) / total[:, half:]
    near = jnp.zeros((own_out_ref.shape[1], half), jnp.float32)
    far = jnp.zeros((own_out_ref.shape[1], half), jnp.float32)
    for row, head in enumerate(group):
        one = slice(row, row + 1)
        near = near + own_share[one, :half] * own_out_ref[head, :, :half]
        far = far + own_share[one, half:] * own_out_ref[head, :, half:]
        far = far + side_share[one] * side_out_ref[row]
    guest_top = beside(top[:, tile_tok:half], top[:, half : half + tile_tok])
    guest_total = beside(total[:, tile_tok:half], total[:, half : half + tile_tok])
    return beside(near, far), jnp.exp2((far_top - guest_top) * EXP_SCALE) / guest_total


def own_blend_kernel(
    tile_tok, group, own_out_ref, side_out_ref, own_top_ref, side_top_ref,
    top_ref, sum_ref, got_ref, velocity_ref,
):
    velocity_ref[...], _ = own_part(
        tile_tok, group, own_out_ref, side_out_ref, own_top_ref, side_top_ref,
        top_ref[...], sum_ref[...], got_ref[2], got_ref[3],
    )


def join_kernel(
    tile_tok, group, own_out_ref, side_out_ref, own_top_ref, side_top_ref,
    top_ref, sum_ref, velocity_ref, back_ref, back_out_ref, out_ref,
):
    channels = own_out_ref.shape[1]
    late = len(group)
    velocity, share = own_part(
        tile_tok, group, own_out_ref, side_out_ref, own_top_ref, side_top_ref,
        top_ref[...], sum_ref[...],
        back_ref[channels : channels + late], back_ref[channels + late : channels + 2 * late],
    )
    guest = back_ref[:channels]
    for row in range(late):
        guest = guest + share[row : row + 1] * back_out_ref[row].astype(jnp.float32)
    out_ref[...] = velocity_ref[...] + velocity + centred(guest, 0.0, tile_tok)


def update_kernel(
    block_count, block_cols, tile_tok, half_size,
    step_ref, velocity_ref, partner_ref, latent_ref,
    guided_ref, clean_ref, next_ref,
):
    spot = Spot(block_count, block_cols)
    half = 2 * tile_tok
    is_cond = spot.index < half_size
    own = velocity_ref[...]
    other = partner_ref[...]
    cond = jnp.where(is_cond, own, other)
    uncond = jnp.where(is_cond, other, own)
    blended = uncond + GUIDANCE * (cond - uncond)
    edge = blended[:, tile_tok : tile_tok + half]
    rest = jnp.concatenate([blended[:, :tile_tok], blended[:, tile_tok + half :]], axis=1)

    def natural(pair):
        swapped = jnp.concatenate([pair[:, tile_tok:], pair[:, :tile_tok]], axis=1)
        return jnp.where(spot.near == 0, pair, swapped)

    edge = natural(edge)
    rest = natural(rest)
    moment = jnp.full((1, half), step_ref[0].astype(jnp.float32))
    sigma_now = flow_sigma(moment)
    step_size = flow_sigma(moment + 1.0) - sigma_now
    for row in range(2):
        lanes = slice(row * half, (row + 1) * half)
        guided = jnp.where(spot.edge == row, edge, rest)
        latent = latent_ref[:, lanes]
        guided_ref[:, lanes] = guided
        clean_ref[:, lanes] = latent - sigma_now * guided
        next_ref[:, lanes] = latent + step_size * guided


def kernel_call(body, args, outs, smem=0, scratch=(), far=(), stay=True):
    spaces = [pltpu.SMEM] * smem + [pltpu.VMEM] * (len(args) - smem)
    for number in far:
        spaces[number] = pltpu.HBM
    args = [
        arg if space == pltpu.SMEM else pltpu.with_memory_space_constraint(arg, space)
        for arg, space in zip(args, spaces)
    ]
    specs = [pl.BlockSpec(memory_space=space) for space in spaces]
    return pl.pallas_call(
        body,
        out_shape=[
            pltpu.VMEM(shape, dtype) if stay else jax.ShapeDtypeStruct(shape, dtype)
            for shape, dtype in outs
        ],
        in_specs=specs,
        out_specs=[pl.BlockSpec(memory_space=pltpu.VMEM) for _ in outs],
        scratch_shapes=list(scratch),
        compiler_params=pltpu.CompilerParams(vmem_limit_bytes=VMEM_LIMIT),
    )(*args)


def one_frame_tile(frame_count):
    return frame_count == SH // 2 * (SW // 2) * 2 and SH == 4 and SW % 4 == 0


def per_device_plan(query_rows, key_rows, value_rows, tile_mask, head_weight, latent, step_index):
    frame_count = lax.axis_size("frame")
    half_size = frame_count // 2
    block_cols = SW // 2
    block_count = SH // 2 * block_cols
    tok_rows, _ = query_rows.shape
    tile_tok = tok_rows // 4
    half = 2 * tile_tok
    channels = head_weight.shape[1]
    places = range(frame_count)
    row_pairs = [
        (f, f + block_cols if f % block_count < block_cols else f - block_cols)
        for f in places
    ]
    mate_pairs = [(f, f + 1 - 2 * (f % 2)) for f in places]
    side_pairs = []
    group_count = lax.axis_size("groups")
    for f in places:
        step = 2 * (f % 2) - 1
        inside = 0 <= f % block_cols + step < block_cols
        for g in range(group_count):
            if inside:
                side_pairs.append((g * frame_count + f, g * frame_count + f + step))
            else:
                other = (g + 1) % group_count
                side_pairs.append((g * frame_count + f, other * frame_count + f))
    branch_pairs = [(f, (f + half_size) % frame_count) for f in places]
    sizes = (block_count, block_cols, tile_tok)
    single = jnp.float32
    half_type = query_rows.dtype
    groups = (range(FIRST_HEADS), range(FIRST_HEADS, HEADS))
    every = (range(HEADS),)
    _, late = (len(group) for group in groups)

    weight_t = head_weight.T
    *guest_sends, edge_bias, weight_t = kernel_call(
        functools.partial(guest_pack_kernel, *sizes, groups),
        (query_rows, tile_mask, weight_t),
        [((half, len(group) * HD), half_type) for group in groups]
        + [((4, half), single), (weight_t.shape, half_type)],
        0,
        (
            pltpu.SMEM(tile_mask.shape, tile_mask.dtype),
            pltpu.SemaphoreType.DMA((2 + 2 * len(groups),)),
        ),
        far=(0, 1, 2),
    )

    def sent_over(value, pairs, axes="frame"):
        return lax.ppermute(value, axes, pairs)

    guests = [sent_over(guest_sends[0], row_pairs)]
    *far, near = kernel_call(
        functools.partial(column_pack_kernel, *sizes, groups),
        (key_rows, value_rows, weight_t, *guest_sends),
        [((half, packed_width(len(group), channels)), half_type) for group in groups + every],
        0,
        (pltpu.SemaphoreType.DMA((2 + 2 * len(groups),)),),
        far=(0,),
    )
    outer = [sent_over(column, side_pairs, ("groups", "frame")) for column in far]
    guest_bias = sent_over(edge_bias, row_pairs)
    guests.append(sent_over(guest_sends[1], row_pairs))
    inner = sent_over(near, mate_pairs)
    stats = ((HEADS, tok_rows), single)
    own_out, own_top, own_sum, side_bias = kernel_call(
        functools.partial(own_kernel, *sizes, groups),
        (tile_mask, query_rows, near, *far, inner),
        (((HEADS, channels, tok_rows), single), stats, stats, ((2, half), single)),
        1,
        (
            pltpu.VMEM((HEADS, tok_rows, tok_rows), single),
            pltpu.VMEM((HEADS, half, half), single),
            pltpu.VMEM((HEADS, tok_rows, tok_rows), half_type),
            pltpu.VMEM((HEADS, half, half), half_type),
        ),
    )

    def edge(number, guest_type):
        group = groups[number]
        heads = len(group)
        return kernel_call(
            functools.partial(edge_kernel, *sizes, group),
            (
                side_bias, guest_bias, query_rows, near, far[number], inner,
                outer[number], guests[number], own_top, own_sum,
            ),
            (
                ((heads, channels, half), single),
                ((heads, channels, half), guest_type),
                ((heads, half), single),
                ((heads, tok_rows), single),
                ((heads, tok_rows), single),
                ((4, heads, half), single),
            ),
            0,
            (
                pltpu.VMEM((heads, half, half), single),
                pltpu.VMEM((heads, tok_rows, half), single),
                pltpu.VMEM((heads, half, half), half_type),
                pltpu.VMEM((heads, tok_rows, half), half_type),
            ),
        )

    side_out, guest_out, side_top, top, total, sent = edge(0, single)
    got = sent_over(sent, row_pairs)
    late_side, late_guest, late_side_top, late_top, late_total, late_sent = edge(1, half_type)
    (guest_velocity,) = kernel_call(
        guest_blend_kernel,
        (guest_out, sent, got, late_sent),
        (((channels + 2 * late, half), single),),
    )
    back = sent_over(guest_velocity, row_pairs)
    back_out = sent_over(late_guest, row_pairs)
    velocity_type = ((channels, tok_rows), single)
    (velocity,) = kernel_call(
        functools.partial(own_blend_kernel, tile_tok, groups[0]),
        (own_out, side_out, own_top, side_top, top, total, got),
        (velocity_type,),
    )
    (velocity,) = kernel_call(
        functools.partial(join_kernel, tile_tok, groups[1]),
        (
            own_out, late_side, own_top, late_side_top, late_top, late_total, velocity,
            back, back_out,
        ),
        (velocity_type,),
    )
    partner = sent_over(velocity, branch_pairs)
    out = ((channels, tok_rows), single)
    results = kernel_call(
        functools.partial(update_kernel, *sizes, half_size),
        (step_index, velocity, partner, latent.T),
        (out, out, out),
        1,
        stay=False,
    )
    return tuple(result.T for result in results)


def per_device(*args):
    return per_device_plan(*args)


def solution(mesh):
    placed = (
        P(("groups", "frame"), None),
        P(("groups", "frame"), None),
        P(("groups", "frame"), None),
        P(("groups", "frame"), None),
        P(),
        P(("groups", "frame"), None),
        P("groups"),
    )
    fast = one_frame_tile(mesh.shape["frame"])
    return jax.shard_map(
        per_device if fast else per_device_frames,
        mesh=mesh,
        in_specs=placed,
        out_specs=(
            P(("groups", "frame"), None),
            P(("groups", "frame"), None),
            P(("groups", "frame"), None),
        ),
        check_vma=False,
    )
```

```python
import functools
import math

import jax
import jax.numpy as jnp
from jax import lax
from jax.experimental import pallas as pl
from jax.experimental.pallas import tpu as pltpu
from jax.sharding import PartitionSpec as P


HEADS = 20
HD = 128
SH = 4
SW = 8
SAMPLE_STEPS = 50


GUIDANCE = 5.0
FLOW_SHIFT = 5.0


def passed_along(value, axis, steps):
    count = lax.axis_size(axis)
    pairs = [(source, (source + steps) % count) for source in range(count)]
    return lax.ppermute(value, axis, pairs)


def flow_sigma(moment):
    remain = 1.0 - moment / SAMPLE_STEPS
    return FLOW_SHIFT * remain / (1.0 + (FLOW_SHIFT - 1.0) * remain)


def edge_range(offset):
    if offset < 0:
        return (1, 2)
    if offset > 0:
        return (0, 1)
    return (0, 2)


def direct_window(stacked, block_count, block_cols):
    received_parts = {}
    for frame_step in (1, 0, -1):
        for row_step in (1, 0, -1):
            for col_step in (1, 0, -1):
                distance = frame_step * block_count + row_step * block_cols + col_step
                row_start, row_stop = edge_range(row_step)
                col_start, col_stop = edge_range(col_step)
                outgoing = stacked[row_start:row_stop, col_start:col_stop]
                if frame_step == 0 and row_step == 0 and (col_step == 0):
                    received = outgoing
                elif row_step == 0 and col_step == 0:
                    received = passed_along(outgoing, "frame", -distance)
                elif row_step != 0 and col_step != 0:
                    received = passed_along(outgoing, "frame", -distance)
                else:
                    received = passed_along(outgoing, "frame", -distance)
                received_parts[frame_step, row_step, col_step] = received
    planes = []
    for frame_step in (-1, 0, 1):
        row_parts = []
        for row_step in (-1, 0, 1):
            col_parts = [received_parts[frame_step, row_step, col_step] for col_step in (-1, 0, 1)]
            row_parts.append(jnp.concatenate(col_parts, axis=1))
        planes.append(jnp.concatenate(row_parts, axis=0))
    return planes


def window_allowed(tile_mask, frame_tile, block_row, block_col, tile_frames):
    offsets = jnp.arange(27, dtype=jnp.int32)
    frame_step = offsets // 9 - 1
    row_step = offsets // 3 % 3 - 1
    col_step = offsets % 3 - 1
    local_tile = jnp.arange(4, dtype=jnp.int32)
    tile_row = 2 * block_row + local_tile // 2
    tile_col = 2 * block_col + local_tile % 2
    frame_there = frame_tile + frame_step
    row_there = tile_row[:, None] + row_step[None, :]
    col_there = tile_col[:, None] + col_step[None, :]
    usable = ((frame_there >= 0) & (frame_there < tile_frames))[None, :]
    usable = usable & (row_there >= 0) & (row_there < SH) & (col_there >= 0) & (col_there < SW)
    return usable & (tile_mask > 0)


def attend_window(query_rows, planes, allowed):
    tok_rows, inner_width = query_rows.shape
    tile_tok = tok_rows // 4
    query_tiles = query_rows.reshape(4, tile_tok, inner_width)
    mask_full = allowed[:, None, :, None]

    def one_head(head_number, result_rows):
        key_planes = [lax.dynamic_slice_in_dim(plane, head_number * HD, HD, 3) for plane in planes]
        value_planes = [
            lax.dynamic_slice_in_dim(plane, inner_width + head_number * HD, HD, 3)
            for plane in planes
        ]
        key_list = []
        value_list = []
        for row_local in range(2):
            for col_local in range(2):
                key_list.append(
                    jnp.stack(
                        [
                            part[row_local : row_local + 3, col_local : col_local + 3]
                            for part in key_planes
                        ]
                    ).reshape(27 * tile_tok, HD)
                )
                value_list.append(
                    jnp.stack(
                        [
                            part[row_local : row_local + 3, col_local : col_local + 3]
                            for part in value_planes
                        ]
                    ).reshape(27 * tile_tok, HD)
                )
        key_tiles = jnp.stack(key_list)
        value_tiles = jnp.stack(value_list)
        head_query = lax.dynamic_slice_in_dim(query_tiles, head_number * HD, HD, 2)
        scores = jnp.einsum(
            "qtd,qkd->qtk", head_query, key_tiles, preferred_element_type=jnp.float32
        ) / math.sqrt(HD)
        scores = scores.reshape(4, tile_tok, 27, tile_tok)
        scores = jnp.where(mask_full, scores, -1e30)
        row_max = jnp.max(scores, axis=(2, 3), keepdims=True)
        shifted = jnp.where(mask_full, jnp.exp(scores - row_max), 0.0)
        weights = (shifted / jnp.sum(shifted, axis=(2, 3), keepdims=True)).astype(jnp.bfloat16)
        weights = weights.reshape(4, tile_tok, 27 * tile_tok)
        head_out = jnp.einsum(
            "qtk,qkd->qtd", weights, value_tiles, preferred_element_type=jnp.float32
        ).astype(jnp.bfloat16)
        return lax.dynamic_update_slice_in_dim(result_rows, head_out, head_number * HD, 2)

    result_rows = lax.fori_loop(
        0, HEADS, one_head, jnp.zeros((4, tile_tok, inner_width), jnp.bfloat16)
    )
    return result_rows.reshape(tok_rows, inner_width)


def per_device_frames(query_rows, key_rows, value_rows, tile_mask, head_weight, latent, step_index):
    frame_count = lax.axis_size("frame")
    frame_index = lax.axis_index("frame")
    half_size = frame_count // 2
    block_cols = SW // 2
    block_count = SH // 2 * block_cols
    tile_frames = frame_count // (2 * block_count)
    frame_tile = frame_index // block_count % tile_frames
    block_spot = frame_index % block_count
    block_row = block_spot // block_cols
    block_col = block_spot % block_cols
    tok_rows, inner_width = query_rows.shape
    tile_tok = tok_rows // 4
    stacked = jnp.concatenate([key_rows, value_rows], axis=1).reshape(
        2, 2, tile_tok, 2 * inner_width
    )
    planes = direct_window(stacked, block_count, block_cols)
    allowed = window_allowed(tile_mask, frame_tile, block_row, block_col, tile_frames)
    attention = attend_window(query_rows, planes, allowed)
    velocity = jnp.dot(attention, head_weight, preferred_element_type=jnp.float32)
    partner_rows = passed_along(velocity, "frame", half_size)
    is_cond = frame_index < half_size
    cond_rows = jnp.where(is_cond, velocity, partner_rows)
    uncond_rows = jnp.where(is_cond, partner_rows, velocity)
    guided = uncond_rows + GUIDANCE * (cond_rows - uncond_rows)
    moment = step_index[0].astype(jnp.float32)
    sigma_now = flow_sigma(moment)
    step_size = flow_sigma(moment + 1.0) - sigma_now
    clean = latent - sigma_now * guided
    latent_next = latent + step_size * guided
    return (guided, clean, latent_next)


NEG = -1e30
VMEM_LIMIT = 16 << 20
FIRST_HEADS = 14
EXP_SCALE = math.log2(math.e) / math.sqrt(HD)


def contract_last(left, right):
    return lax.dot_general(
        left, right, (((1,), (1,)), ((), ())), preferred_element_type=jnp.float32
    )


def contract(left, right):
    return jnp.dot(left, right, preferred_element_type=jnp.float32)


def head_lanes(head):
    return slice(head * HD, (head + 1) * HD)


class Spot:
    def __init__(self, block_count, block_cols):
        self.index = lax.axis_index("frame")
        spot = self.index % block_count
        block_row = spot // block_cols
        block_col = spot % block_cols
        odd = block_col % 2
        self.edge = 1 - block_row
        self.rest = block_row
        self.near = 1 - odd
        self.far = odd
        self.near_step = 1 - 2 * odd
        self.far_step = 2 * odd - 1
        side = block_col + self.far_step
        self.there = (side >= 0) & (side < block_cols)
        self.guest_step = 2 * block_row - 1
        self.lane_tiles = (
            (self.rest, self.near),
            (self.edge, self.near),
            (self.edge, self.far),
            (self.rest, self.far),
        )
        self.key_tiles = (
            (self.edge, self.near),
            (self.rest, self.near),
            (self.rest, self.far),
            (self.edge, self.far),
        )


def tile_rows(tile, tile_tok):
    row, col = tile
    return pl.ds(pl.multiple_of((2 * row + col) * tile_tok, tile_tok), tile_tok)


def entry(row_step, col_step):
    return 9 + 3 * (row_step + 1) + col_step + 1


def bias_of(flag):
    return jnp.where(flag, jnp.float32(0.0), jnp.float32(NEG))


def key_bias(rows, tile_tok):
    biases = []
    for flags in rows:
        lanes = len(flags) * tile_tok
        lane = lax.broadcasted_iota(jnp.int32, (1, lanes), 1) // tile_tok
        bias = jnp.zeros((1, lanes), jnp.float32)
        for number, flag in enumerate(flags):
            bias = jnp.where(lane == number, bias_of(flag), bias)
        biases.append(bias)
    return biases


def biased(scores, biases, tile_tok):
    return above(
        *[scores[t * tile_tok : (t + 1) * tile_tok] + row for t, row in enumerate(biases)]
    )


def beside(left, right):
    return jnp.concatenate([left, right], axis=1)


def above(*parts):
    return jnp.concatenate(parts, axis=0)


def largest(scores):
    return jnp.max(scores, axis=0, keepdims=True)


def softened(scores, top):
    return jnp.exp2((scores - top) * EXP_SCALE).astype(jnp.bfloat16)


def with_ones(folded):
    return above(folded, jnp.ones((16, folded.shape[1]), folded.dtype))


def pipelined(heads, *stages):
    for turn in range(len(heads) + len(stages) - 1):
        for number, stage in enumerate(stages):
            if 0 <= turn - number < len(heads):
                stage(heads[turn - number])


def packed_width(heads, channels):
    return heads * HD + (heads + 1) // 2 * 2 * channels


class Column:
    def __init__(self, refs, groups, channels):
        self.refs = refs
        self.groups = groups
        self.channels = channels

    def place(self, head):
        for ref, group in zip(self.refs, self.groups):
            if head in group:
                return ref, head - group.start, len(group) * HD

    def keys(self, head):
        ref, local, _ = self.place(head)
        return ref[:, head_lanes(local)]

    def folded_at(self, head):
        ref, local, width = self.place(head)
        row = local % 2 * self.channels
        lane = width + local // 2 * 2 * self.channels
        return ref, (slice(row, row + self.channels), slice(lane, lane + 2 * self.channels))

    def folded(self, head):
        ref, where = self.folded_at(head)
        return ref[where]


def copied(pairs, sems):
    copies = [
        pltpu.make_async_copy(source, target, sems.at[number])
        for number, (source, target) in enumerate(pairs)
    ]
    for copy in copies:
        copy.start()
    return copies


def guest_pack_kernel(
    block_count, block_cols, tile_tok,
    query_ref, key_ref, mask_ref, weight_ref,
    guest_ref, bias_ref, far_key_ref, near_weight_ref, mask, sems,
):
    spot = Spot(block_count, block_cols)
    pairs = [(mask_ref, mask)]
    lanes = pl.ds(0, guest_ref.shape[1])
    for number, col in enumerate((spot.near, spot.far)):
        target = pl.ds(number * tile_tok, tile_tok)
        rows = tile_rows((spot.edge, col), tile_tok)
        pairs.append((query_ref.at[rows, lanes], guest_ref.at[target]))
    pairs.append((weight_ref, near_weight_ref))
    for number, tile in enumerate(spot.key_tiles[2:]):
        target = pl.ds(number * tile_tok, tile_tok)
        pairs.append((key_ref.at[tile_rows(tile, tile_tok)], far_key_ref.at[target]))
    copies = copied(pairs, sems)
    copies[0].wait()
    steps = -spot.guest_step

    def flag(col, col_step):
        return mask[2 * spot.edge + col, entry(steps, col_step)] > 0

    never = spot.near < 0
    cols = (spot.near, spot.far)
    rows = [[flag(col, key - col) for col in cols] for key in cols] + [
        [flag(spot.near, spot.near_step), never],
        [never, flag(spot.far, spot.far_step) & spot.there],
    ]
    for number, row in enumerate(key_bias(rows, tile_tok)):
        bias_ref[number : number + 1] = row
    for copy in copies[1:]:
        copy.wait()


def fold_into(column, value_ref, weight_ref, places):
    for head in range(HEADS):
        lanes = head_lanes(head)
        values = above(*[value_ref[place, lanes] for place in places])
        folded = contract_last(weight_ref[:, lanes], values)
        ref, where = column.folded_at(head)
        ref[where] = folded.astype(jnp.bfloat16)


def far_pack_kernel(
    block_count, block_cols, tile_tok, groups, key_ref, value_ref, weight_ref, guest_ref, *refs
):
    spot = Spot(block_count, block_cols)
    for out_ref, group in zip(refs, groups):
        out_ref[:, : len(group) * HD] = key_ref[:, group.start * HD : group.stop * HD]
    places = [tile_rows(tile, tile_tok) for tile in spot.key_tiles[2:]]
    fold_into(Column(refs, groups, weight_ref.shape[0]), value_ref, weight_ref, places)


def near_pack_kernel(
    block_count, block_cols, tile_tok, group,
    query_ref, key_ref, value_ref, weight_ref, near_ref, guest_ref,
):
    spot = Spot(block_count, block_cols)
    places = [tile_rows(tile, tile_tok) for tile in spot.key_tiles[:2]]
    for number, col in enumerate((spot.near, spot.far)):
        rows = slice(number * tile_tok, (number + 1) * tile_tok)
        near_ref[rows, : HEADS * HD] = key_ref[places[number], :]
        guest_ref[rows] = query_ref[
            tile_rows((spot.edge, col), tile_tok), group.start * HD : group.stop * HD
        ]
    column = Column([near_ref], (range(HEADS),), weight_ref.shape[0])
    fold_into(column, value_ref, weight_ref, places)


def own_kernel(
    block_count, block_cols, tile_tok, groups, mask_ref, query_ref, *refs
):
    count = len(groups)
    far_refs = refs[1 : 1 + count]
    out_ref, top_ref, sum_ref, side_bias_ref = refs[2 + count : 6 + count]
    own_scores, halo_scores, own_weights, halo_weights = refs[6 + count :]
    spot = Spot(block_count, block_cols)
    channels = out_ref.shape[1]
    half = 2 * tile_tok
    every = (range(HEADS),)
    near_column = Column(refs[:1], every, channels)
    far_column = Column(far_refs, groups, channels)
    inner_column = Column(refs[1 + count : 2 + count], every, channels)

    def flag(tile, row_step, col_step):
        return mask_ref[2 * tile[0] + tile[1], entry(row_step, col_step)] > 0

    bias = key_bias(
        [
            [flag(t, key[0] - t[0], key[1] - t[1]) for t in spot.lane_tiles]
            for key in spot.key_tiles
        ],
        tile_tok,
    )
    halo_bias = key_bias(
        [
            [flag(t, row - t[0], spot.near_step) for t in spot.lane_tiles[:2]]
            for row in (spot.edge, spot.rest)
        ],
        tile_tok,
    )
    side_rows = [
        [flag(t, row - t[0], spot.far_step) & spot.there for t in spot.lane_tiles[2:]]
        for row in (spot.rest, spot.edge)
    ]
    for number, row in enumerate(key_bias(side_rows, tile_tok)):
        side_bias_ref[number : number + 1] = row
    places = [tile_rows(tile, tile_tok) for tile in spot.lane_tiles]

    def score(head):
        lanes = head_lanes(head)
        query = above(*[query_ref[place, lanes] for place in places])
        keys = above(near_column.keys(head), far_column.keys(head))
        own = biased(contract_last(keys, query), bias, tile_tok)
        halo = biased(
            contract_last(inner_column.keys(head), query[:half]), halo_bias, tile_tok
        )
        own_scores[head] = own
        halo_scores[head] = halo
        top = largest(own)
        top_ref[head : head + 1, :half] = jnp.maximum(top[:, :half], largest(halo))
        top_ref[head : head + 1, half:] = top[:, half:]

    def soften(head):
        top = top_ref[head : head + 1]
        own_weights[head] = softened(own_scores[head], top)
        halo_weights[head] = softened(halo_scores[head], top[:, :half])

    def weigh(head):
        folded = with_ones(beside(near_column.folded(head), far_column.folded(head)))
        own = contract(folded, own_weights[head])
        halo = contract(with_ones(inner_column.folded(head)), halo_weights[head])
        left = own[:, :half] + halo
        out_ref[head, :, :half] = left[:channels]
        out_ref[head, :, half:] = own[:channels, half:]
        sum_ref[head : head + 1, :half] = left[channels : channels + 1]
        sum_ref[head : head + 1, half:] = own[channels : channels + 1, half:]

    pipelined(range(HEADS), score, soften, weigh)


def edge_kernel(
    block_count, block_cols, tile_tok, group,
    side_bias_ref, guest_bias_ref,
    query_ref, near_ref, far_ref, inner_ref, outer_ref, guest_ref, own_top_ref, own_sum_ref,
    out_ref, guest_out_ref, side_top_ref, top_ref, sum_ref, send_ref,
    side_scores, guest_scores, side_weights, guest_weights,
):
    spot = Spot(block_count, block_cols)
    channels = out_ref.shape[1]
    half = 2 * tile_tok
    near_column = Column([near_ref], (range(HEADS),), channels)
    inner_column = Column([inner_ref], (range(HEADS),), channels)
    far_column = Column([far_ref], (group,), channels)
    outer_column = Column([outer_ref], (group,), channels)

    bias = [side_bias_ref[number : number + 1] for number in range(2)]
    guest_bias = [guest_bias_ref[number : number + 1] for number in range(4)]
    places = [tile_rows(tile, tile_tok) for tile in spot.lane_tiles[2:]]
    left = lax.broadcasted_iota(jnp.int32, (channels, half), 1) < tile_tok

    def score(head):
        row = head - group.start
        query = above(*[query_ref[place, head_lanes(head)] for place in places])
        scores = biased(contract_last(outer_column.keys(head), query), bias, tile_tok)
        side_scores[row] = scores
        side_top_ref[row : row + 1] = largest(scores)
        keys = above(
            near_column.keys(head)[:tile_tok],
            far_column.keys(head)[tile_tok:],
            inner_column.keys(head)[:tile_tok],
            outer_column.keys(head)[tile_tok:],
        )
        scores = contract_last(keys, guest_ref[:, head_lanes(row)])
        scores = biased(scores, guest_bias, tile_tok)
        guest_scores[row] = scores
        send_ref[2, row : row + 1] = largest(scores)

    def soften(head):
        row = head - group.start
        side_weights[row] = softened(side_scores[row], side_top_ref[row : row + 1])
        guest_weights[row] = softened(guest_scores[row], send_ref[2, row : row + 1])

    def weigh(head):
        row = head - group.start
        side = contract(with_ones(outer_column.folded(head)), side_weights[row])
        out_ref[row] = side[:channels]
        sum_ref[row : row + 1, half:] = side[channels : channels + 1]
        folded = beside(
            jnp.where(left, near_column.folded(head), far_column.folded(head)),
            jnp.where(left, inner_column.folded(head), outer_column.folded(head)),
        )
        guest = contract(with_ones(folded), guest_weights[row])
        guest_out_ref[row] = guest[:channels].astype(guest_out_ref.dtype)
        send_ref[3, row : row + 1] = guest[channels : channels + 1]

    pipelined(group, score, soften, weigh)

    mine = slice(group.start, group.stop)
    near_top = own_top_ref[mine, :half]
    near_sum = own_sum_ref[mine, :half]
    old_top = own_top_ref[mine, half:]
    side_top = side_top_ref[...]
    far_top, far_sum = shares(
        old_top, own_sum_ref[mine, half:], side_top, sum_ref[:, half:]
    )
    top_ref[:, :half] = near_top
    top_ref[:, half:] = far_top
    sum_ref[:, :half] = near_sum
    sum_ref[:, half:] = far_sum
    send_ref[0] = beside(near_top[:, tile_tok:], far_top[:, :tile_tok])
    send_ref[1] = beside(near_sum[:, tile_tok:], far_sum[:, :tile_tok])


def shares(near_top, near_sum, away_top, away_sum):
    top = jnp.maximum(near_top, away_top)
    near = jnp.exp2((near_top - top) * EXP_SCALE) * near_sum
    away = jnp.exp2((away_top - top) * EXP_SCALE) * away_sum
    return top, near + away


def centred(values, fill, tile_tok):
    side = jnp.full((values.shape[0], tile_tok), fill, values.dtype)
    return jnp.concatenate([side, values, side], axis=1)


def guest_blend_kernel(guest_out_ref, sent_ref, got_ref, late_ref, back_ref):
    heads, channels, _ = guest_out_ref.shape
    top, total = shares(sent_ref[2], sent_ref[3], got_ref[0], got_ref[1])
    share = jnp.exp2((sent_ref[2] - top) * EXP_SCALE) / total
    velocity = jnp.zeros(guest_out_ref.shape[1:], jnp.float32)
    for row in range(heads):
        velocity = velocity + share[row : row + 1] * guest_out_ref[row]
    back_ref[:channels] = velocity
    late = late_ref.shape[1]
    back_ref[channels : channels + late] = late_ref[2]
    back_ref[channels + late : channels + 2 * late] = late_ref[3]


def own_part(tile_tok, group, own_out_ref, side_out_ref, own_top_ref, side_top_ref,
             top, total, far_top, far_total):
    half = 2 * tile_tok
    top, total = shares(
        top, total, centred(far_top, NEG, tile_tok), centred(far_total, 0.0, tile_tok)
    )
    own_top = own_top_ref[group.start : group.stop]
    own_share = jnp.exp2((own_top - top) * EXP_SCALE) / total
    side_share = jnp.exp2((side_top_ref[...] - top[:, half:]) * EXP_SCALE) / total[:, half:]
    near = jnp.zeros((own_out_ref.shape[1], half), jnp.float32)
    far = jnp.zeros((own_out_ref.shape[1], half), jnp.float32)
    for row, head in enumerate(group):
        one = slice(row, row + 1)
        near = near + own_share[one, :half] * own_out_ref[head, :, :half]
        far = far + own_share[one, half:] * own_out_ref[head, :, half:]
        far = far + side_share[one] * side_out_ref[row]
    guest_top = beside(top[:, tile_tok:half], top[:, half : half + tile_tok])
    guest_total = beside(total[:, tile_tok:half], total[:, half : half + tile_tok])
    return beside(near, far), jnp.exp2((far_top - guest_top) * EXP_SCALE) / guest_total


def own_blend_kernel(
    tile_tok, group, own_out_ref, side_out_ref, own_top_ref, side_top_ref,
    top_ref, sum_ref, got_ref, velocity_ref,
):
    velocity_ref[...], _ = own_part(
        tile_tok, group, own_out_ref, side_out_ref, own_top_ref, side_top_ref,
        top_ref[...], sum_ref[...], got_ref[2], got_ref[3],
    )


def join_kernel(
    tile_tok, group, own_out_ref, side_out_ref, own_top_ref, side_top_ref,
    top_ref, sum_ref, velocity_ref, back_ref, back_out_ref, out_ref,
):
    channels = own_out_ref.shape[1]
    late = len(group)
    velocity, share = own_part(
        tile_tok, group, own_out_ref, side_out_ref, own_top_ref, side_top_ref,
        top_ref[...], sum_ref[...],
        back_ref[channels : channels + late], back_ref[channels + late : channels + 2 * late],
    )
    guest = back_ref[:channels]
    for row in range(late):
        guest = guest + share[row : row + 1] * back_out_ref[row].astype(jnp.float32)
    out_ref[...] = velocity_ref[...] + velocity + centred(guest, 0.0, tile_tok)


def update_kernel(
    block_count, block_cols, tile_tok, half_size,
    step_ref, velocity_ref, partner_ref, latent_ref,
    guided_ref, clean_ref, next_ref,
):
    spot = Spot(block_count, block_cols)
    half = 2 * tile_tok
    is_cond = spot.index < half_size
    own = velocity_ref[...]
    other = partner_ref[...]
    cond = jnp.where(is_cond, own, other)
    uncond = jnp.where(is_cond, other, own)
    blended = uncond + GUIDANCE * (cond - uncond)
    edge = blended[:, tile_tok : tile_tok + half]
    rest = jnp.concatenate([blended[:, :tile_tok], blended[:, tile_tok + half :]], axis=1)

    def natural(pair):
        swapped = jnp.concatenate([pair[:, tile_tok:], pair[:, :tile_tok]], axis=1)
        return jnp.where(spot.near == 0, pair, swapped)

    edge = natural(edge)
    rest = natural(rest)
    moment = jnp.full((1, half), step_ref[0].astype(jnp.float32))
    sigma_now = flow_sigma(moment)
    step_size = flow_sigma(moment + 1.0) - sigma_now
    for row in range(2):
        lanes = slice(row * half, (row + 1) * half)
        guided = jnp.where(spot.edge == row, edge, rest)
        latent = latent_ref[:, lanes]
        guided_ref[:, lanes] = guided
        clean_ref[:, lanes] = latent - sigma_now * guided
        next_ref[:, lanes] = latent + step_size * guided


def kernel_call(body, args, outs, smem=0, scratch=(), far=(), stay=True):
    spaces = [pltpu.SMEM] * smem + [pltpu.VMEM] * (len(args) - smem)
    for number in far:
        spaces[number] = pltpu.HBM
    args = [
        arg if space == pltpu.SMEM else pltpu.with_memory_space_constraint(arg, space)
        for arg, space in zip(args, spaces)
    ]
    specs = [pl.BlockSpec(memory_space=space) for space in spaces]
    return pl.pallas_call(
        body,
        out_shape=[
            pltpu.VMEM(shape, dtype) if stay else jax.ShapeDtypeStruct(shape, dtype)
            for shape, dtype in outs
        ],
        in_specs=specs,
        out_specs=[pl.BlockSpec(memory_space=pltpu.VMEM) for _ in outs],
        scratch_shapes=list(scratch),
        compiler_params=pltpu.CompilerParams(vmem_limit_bytes=VMEM_LIMIT),
    )(*args)


def one_frame_tile(frame_count):
    return frame_count == SH // 2 * (SW // 2) * 2 and SH == 4 and SW % 4 == 0


def per_device_plan(query_rows, key_rows, value_rows, tile_mask, head_weight, latent, step_index):
    frame_count = lax.axis_size("frame")
    half_size = frame_count // 2
    block_cols = SW // 2
    block_count = SH // 2 * block_cols
    tok_rows, width = query_rows.shape
    tile_tok = tok_rows // 4
    half = 2 * tile_tok
    channels = head_weight.shape[1]
    places = range(frame_count)
    row_pairs = [
        (f, f + block_cols if f % block_count < block_cols else f - block_cols)
        for f in places
    ]
    mate_pairs = [(f, f + 1 - 2 * (f % 2)) for f in places]
    side_pairs = []
    group_count = lax.axis_size("groups")
    for f in places:
        step = 2 * (f % 2) - 1
        inside = 0 <= f % block_cols + step < block_cols
        for g in range(group_count):
            if inside:
                side_pairs.append((g * frame_count + f, g * frame_count + f + step))
            else:
                other = (g + 1) % group_count
                side_pairs.append((g * frame_count + f, other * frame_count + f))
    branch_pairs = [(f, (f + half_size) % frame_count) for f in places]
    sizes = (block_count, block_cols, tile_tok)
    single = jnp.float32
    half_type = query_rows.dtype
    groups = (range(FIRST_HEADS), range(FIRST_HEADS, HEADS))
    every = (range(HEADS),)
    early, late = (len(group) for group in groups)

    weight_t = head_weight.T
    guest_send, edge_bias, far_keys, weight_t = kernel_call(
        functools.partial(guest_pack_kernel, *sizes),
        (query_rows, key_rows, tile_mask, weight_t),
        (
            ((half, early * HD), half_type),
            ((4, half), single),
            ((half, width), half_type),
            (weight_t.shape, half_type),
        ),
        0,
        (pltpu.SMEM(tile_mask.shape, tile_mask.dtype), pltpu.SemaphoreType.DMA((6,))),
        far=(0, 1, 2, 3),
    )

    def sent_over(value, pairs, axes="frame"):
        return lax.ppermute(value, axes, pairs)

    def column_type(group):
        return ((half, packed_width(len(group), channels)), half_type)

    guests = [sent_over(guest_send, row_pairs)]
    far = kernel_call(
        functools.partial(far_pack_kernel, *sizes, groups),
        (far_keys, value_rows, weight_t, guest_send),
        [column_type(group) for group in groups],
    )
    outer = [sent_over(column, side_pairs, ("groups", "frame")) for column in far]
    near, guest_send = kernel_call(
        functools.partial(near_pack_kernel, *sizes, groups[1]),
        (query_rows, key_rows, value_rows, weight_t),
        (column_type(every[0]), ((half, late * HD), half_type)),
    )
    inner = sent_over(near, mate_pairs)
    guest_bias = sent_over(edge_bias, row_pairs)
    guests.append(sent_over(guest_send, row_pairs))
    stats = ((HEADS, tok_rows), single)
    own_out, own_top, own_sum, side_bias = kernel_call(
        functools.partial(own_kernel, *sizes, groups),
        (tile_mask, query_rows, near, *far, inner),
        (((HEADS, channels, tok_rows), single), stats, stats, ((2, half), single)),
        1,
        (
            pltpu.VMEM((HEADS, tok_rows, tok_rows), single),
            pltpu.VMEM((HEADS, half, half), single),
            pltpu.VMEM((HEADS, tok_rows, tok_rows), half_type),
            pltpu.VMEM((HEADS, half, half), half_type),
        ),
    )

    def edge(number, guest_type):
        group = groups[number]
        heads = len(group)
        return kernel_call(
            functools.partial(edge_kernel, *sizes, group),
            (
                side_bias, guest_bias, query_rows, near, far[number], inner,
                outer[number], guests[number], own_top, own_sum,
            ),
            (
                ((heads, channels, half), single),
                ((heads, channels, half), guest_type),
                ((heads, half), single),
                ((heads, tok_rows), single),
                ((heads, tok_rows), single),
                ((4, heads, half), single),
            ),
            0,
            (
                pltpu.VMEM((heads, half, half), single),
                pltpu.VMEM((heads, tok_rows, half), single),
                pltpu.VMEM((heads, half, half), half_type),
                pltpu.VMEM((heads, tok_rows, half), half_type),
            ),
        )

    side_out, guest_out, side_top, top, total, sent = edge(0, single)
    got = sent_over(sent, row_pairs)
    late_side, late_guest, late_side_top, late_top, late_total, late_sent = edge(1, half_type)
    (guest_velocity,) = kernel_call(
        guest_blend_kernel,
        (guest_out, sent, got, late_sent),
        (((channels + 2 * late, half), single),),
    )
    back = sent_over(guest_velocity, row_pairs)
    back_out = sent_over(late_guest, row_pairs)
    velocity_type = ((channels, tok_rows), single)
    (velocity,) = kernel_call(
        functools.partial(own_blend_kernel, tile_tok, groups[0]),
        (own_out, side_out, own_top, side_top, top, total, got),
        (velocity_type,),
    )
    (velocity,) = kernel_call(
        functools.partial(join_kernel, tile_tok, groups[1]),
        (
            own_out, late_side, own_top, late_side_top, late_top, late_total, velocity,
            back, back_out,
        ),
        (velocity_type,),
    )
    partner = sent_over(velocity, branch_pairs)
    out = ((channels, tok_rows), single)
    results = kernel_call(
        functools.partial(update_kernel, *sizes, half_size),
        (step_index, velocity, partner, latent.T),
        (out, out, out),
        1,
        stay=False,
    )
    return tuple(result.T for result in results)


def per_device(*args):
    return per_device_plan(*args)


def solution(mesh):
    placed = (
        P(("groups", "frame"), None),
        P(("groups", "frame"), None),
        P(("groups", "frame"), None),
        P(("groups", "frame"), None),
        P(),
        P(("groups", "frame"), None),
        P("groups"),
    )
    fast = one_frame_tile(mesh.shape["frame"])
    return jax.shard_map(
        per_device if fast else per_device_frames,
        mesh=mesh,
        in_specs=placed,
        out_specs=(
            P(("groups", "frame"), None),
            P(("groups", "frame"), None),
            P(("groups", "frame"), None),
        ),
        check_vma=False,
    )
```

```python
import functools
import math

import jax
import jax.numpy as jnp
from jax import lax
from jax.experimental import pallas as pl
from jax.experimental.pallas import tpu as pltpu
from jax.sharding import PartitionSpec as P


HEADS = 20
HD = 128
SH = 4
SW = 8
SAMPLE_STEPS = 50


GUIDANCE = 5.0
FLOW_SHIFT = 5.0


def passed_along(value, axis, steps):
    count = lax.axis_size(axis)
    pairs = [(source, (source + steps) % count) for source in range(count)]
    return lax.ppermute(value, axis, pairs)


def flow_sigma(moment):
    remain = 1.0 - moment / SAMPLE_STEPS
    return FLOW_SHIFT * remain / (1.0 + (FLOW_SHIFT - 1.0) * remain)


def edge_range(offset):
    if offset < 0:
        return (1, 2)
    if offset > 0:
        return (0, 1)
    return (0, 2)


def direct_window(stacked, block_count, block_cols):
    received_parts = {}
    for frame_step in (1, 0, -1):
        for row_step in (1, 0, -1):
            for col_step in (1, 0, -1):
                distance = frame_step * block_count + row_step * block_cols + col_step
                row_start, row_stop = edge_range(row_step)
                col_start, col_stop = edge_range(col_step)
                outgoing = stacked[row_start:row_stop, col_start:col_stop]
                if frame_step == 0 and row_step == 0 and (col_step == 0):
                    received = outgoing
                elif row_step == 0 and col_step == 0:
                    received = passed_along(outgoing, "frame", -distance)
                elif row_step != 0 and col_step != 0:
                    received = passed_along(outgoing, "frame", -distance)
                else:
                    received = passed_along(outgoing, "frame", -distance)
                received_parts[frame_step, row_step, col_step] = received
    planes = []
    for frame_step in (-1, 0, 1):
        row_parts = []
        for row_step in (-1, 0, 1):
            col_parts = [received_parts[frame_step, row_step, col_step] for col_step in (-1, 0, 1)]
            row_parts.append(jnp.concatenate(col_parts, axis=1))
        planes.append(jnp.concatenate(row_parts, axis=0))
    return planes


def window_allowed(tile_mask, frame_tile, block_row, block_col, tile_frames):
    offsets = jnp.arange(27, dtype=jnp.int32)
    frame_step = offsets // 9 - 1
    row_step = offsets // 3 % 3 - 1
    col_step = offsets % 3 - 1
    local_tile = jnp.arange(4, dtype=jnp.int32)
    tile_row = 2 * block_row + local_tile // 2
    tile_col = 2 * block_col + local_tile % 2
    frame_there = frame_tile + frame_step
    row_there = tile_row[:, None] + row_step[None, :]
    col_there = tile_col[:, None] + col_step[None, :]
    usable = ((frame_there >= 0) & (frame_there < tile_frames))[None, :]
    usable = usable & (row_there >= 0) & (row_there < SH) & (col_there >= 0) & (col_there < SW)
    return usable & (tile_mask > 0)


def attend_window(query_rows, planes, allowed):
    tok_rows, inner_width = query_rows.shape
    tile_tok = tok_rows // 4
    query_tiles = query_rows.reshape(4, tile_tok, inner_width)
    mask_full = allowed[:, None, :, None]

    def one_head(head_number, result_rows):
        key_planes = [lax.dynamic_slice_in_dim(plane, head_number * HD, HD, 3) for plane in planes]
        value_planes = [
            lax.dynamic_slice_in_dim(plane, inner_width + head_number * HD, HD, 3)
            for plane in planes
        ]
        key_list = []
        value_list = []
        for row_local in range(2):
            for col_local in range(2):
                key_list.append(
                    jnp.stack(
                        [
                            part[row_local : row_local + 3, col_local : col_local + 3]
                            for part in key_planes
                        ]
                    ).reshape(27 * tile_tok, HD)
                )
                value_list.append(
                    jnp.stack(
                        [
                            part[row_local : row_local + 3, col_local : col_local + 3]
                            for part in value_planes
                        ]
                    ).reshape(27 * tile_tok, HD)
                )
        key_tiles = jnp.stack(key_list)
        value_tiles = jnp.stack(value_list)
        head_query = lax.dynamic_slice_in_dim(query_tiles, head_number * HD, HD, 2)
        scores = jnp.einsum(
            "qtd,qkd->qtk", head_query, key_tiles, preferred_element_type=jnp.float32
        ) / math.sqrt(HD)
        scores = scores.reshape(4, tile_tok, 27, tile_tok)
        scores = jnp.where(mask_full, scores, -1e30)
        row_max = jnp.max(scores, axis=(2, 3), keepdims=True)
        shifted = jnp.where(mask_full, jnp.exp(scores - row_max), 0.0)
        weights = (shifted / jnp.sum(shifted, axis=(2, 3), keepdims=True)).astype(jnp.bfloat16)
        weights = weights.reshape(4, tile_tok, 27 * tile_tok)
        head_out = jnp.einsum(
            "qtk,qkd->qtd", weights, value_tiles, preferred_element_type=jnp.float32
        ).astype(jnp.bfloat16)
        return lax.dynamic_update_slice_in_dim(result_rows, head_out, head_number * HD, 2)

    result_rows = lax.fori_loop(
        0, HEADS, one_head, jnp.zeros((4, tile_tok, inner_width), jnp.bfloat16)
    )
    return result_rows.reshape(tok_rows, inner_width)


def per_device_frames(query_rows, key_rows, value_rows, tile_mask, head_weight, latent, step_index):
    frame_count = lax.axis_size("frame")
    frame_index = lax.axis_index("frame")
    half_size = frame_count // 2
    block_cols = SW // 2
    block_count = SH // 2 * block_cols
    tile_frames = frame_count // (2 * block_count)
    frame_tile = frame_index // block_count % tile_frames
    block_spot = frame_index % block_count
    block_row = block_spot // block_cols
    block_col = block_spot % block_cols
    tok_rows, inner_width = query_rows.shape
    tile_tok = tok_rows // 4
    stacked = jnp.concatenate([key_rows, value_rows], axis=1).reshape(
        2, 2, tile_tok, 2 * inner_width
    )
    planes = direct_window(stacked, block_count, block_cols)
    allowed = window_allowed(tile_mask, frame_tile, block_row, block_col, tile_frames)
    attention = attend_window(query_rows, planes, allowed)
    velocity = jnp.dot(attention, head_weight, preferred_element_type=jnp.float32)
    partner_rows = passed_along(velocity, "frame", half_size)
    is_cond = frame_index < half_size
    cond_rows = jnp.where(is_cond, velocity, partner_rows)
    uncond_rows = jnp.where(is_cond, partner_rows, velocity)
    guided = uncond_rows + GUIDANCE * (cond_rows - uncond_rows)
    moment = step_index[0].astype(jnp.float32)
    sigma_now = flow_sigma(moment)
    step_size = flow_sigma(moment + 1.0) - sigma_now
    clean = latent - sigma_now * guided
    latent_next = latent + step_size * guided
    return (guided, clean, latent_next)


NEG = -1e30
VMEM_LIMIT = 16 << 20
FIRST_HEADS = 14
EXP_SCALE = math.log2(math.e) / math.sqrt(HD)


def contract_last(left, right):
    return lax.dot_general(
        left, right, (((1,), (1,)), ((), ())), preferred_element_type=jnp.float32
    )


def contract(left, right):
    return jnp.dot(left, right, preferred_element_type=jnp.float32)


def head_lanes(head):
    return slice(head * HD, (head + 1) * HD)


class Spot:
    def __init__(self, block_count, block_cols):
        self.index = lax.axis_index("frame")
        spot = self.index % block_count
        block_row = spot // block_cols
        block_col = spot % block_cols
        odd = block_col % 2
        self.edge = 1 - block_row
        self.rest = block_row
        self.near = 1 - odd
        self.far = odd
        self.near_step = 1 - 2 * odd
        self.far_step = 2 * odd - 1
        side = block_col + self.far_step
        self.there = (side >= 0) & (side < block_cols)
        self.guest_step = 2 * block_row - 1
        self.lane_tiles = (
            (self.rest, self.near),
            (self.edge, self.near),
            (self.edge, self.far),
            (self.rest, self.far),
        )
        self.key_tiles = (
            (self.edge, self.near),
            (self.rest, self.near),
            (self.rest, self.far),
            (self.edge, self.far),
        )


def tile_rows(tile, tile_tok):
    row, col = tile
    return pl.ds(pl.multiple_of((2 * row + col) * tile_tok, tile_tok), tile_tok)


def entry(row_step, col_step):
    return 9 + 3 * (row_step + 1) + col_step + 1


def bias_of(flag):
    return jnp.where(flag, jnp.float32(0.0), jnp.float32(NEG))


def key_bias(rows, tile_tok):
    biases = []
    for flags in rows:
        lanes = len(flags) * tile_tok
        lane = lax.broadcasted_iota(jnp.int32, (1, lanes), 1) // tile_tok
        bias = jnp.zeros((1, lanes), jnp.float32)
        for number, flag in enumerate(flags):
            bias = jnp.where(lane == number, bias_of(flag), bias)
        biases.append(bias)
    return biases


def biased(scores, biases, tile_tok):
    return above(
        *[scores[t * tile_tok : (t + 1) * tile_tok] + row for t, row in enumerate(biases)]
    )


def beside(left, right):
    return jnp.concatenate([left, right], axis=1)


def above(*parts):
    return jnp.concatenate(parts, axis=0)


def largest(scores):
    return jnp.max(scores, axis=0, keepdims=True)


def softened(scores, top):
    return jnp.exp2((scores - top) * EXP_SCALE).astype(jnp.bfloat16)


def with_ones(folded):
    return above(folded, jnp.ones((16, folded.shape[1]), folded.dtype))


def pipelined(heads, *stages):
    for turn in range(len(heads) + len(stages) - 1):
        for number, stage in enumerate(stages):
            if 0 <= turn - number < len(heads):
                stage(heads[turn - number])


def packed_width(heads, channels):
    return heads * HD + (heads + 1) // 2 * 2 * channels


class Column:
    def __init__(self, refs, groups, channels):
        self.refs = refs
        self.groups = groups
        self.channels = channels

    def place(self, head):
        for ref, group in zip(self.refs, self.groups):
            if head in group:
                return ref, head - group.start, len(group) * HD

    def keys(self, head):
        ref, local, _ = self.place(head)
        return ref[:, head_lanes(local)]

    def folded_at(self, head):
        ref, local, width = self.place(head)
        row = local % 2 * self.channels
        lane = width + local // 2 * 2 * self.channels
        return ref, (slice(row, row + self.channels), slice(lane, lane + 2 * self.channels))

    def folded(self, head):
        ref, where = self.folded_at(head)
        return ref[where]


def copied(pairs, sems):
    copies = [
        pltpu.make_async_copy(source, target, sems.at[number])
        for number, (source, target) in enumerate(pairs)
    ]
    for copy in copies:
        copy.start()
    return copies


def guest_pack_kernel(
    block_count, block_cols, tile_tok,
    query_ref, key_ref, mask_ref, weight_ref,
    guest_ref, bias_ref, far_key_ref, near_weight_ref, mask, sems,
):
    spot = Spot(block_count, block_cols)
    pairs = [(mask_ref, mask)]
    lanes = pl.ds(0, guest_ref.shape[1])
    for number, col in enumerate((spot.near, spot.far)):
        target = pl.ds(number * tile_tok, tile_tok)
        rows = tile_rows((spot.edge, col), tile_tok)
        pairs.append((query_ref.at[rows, lanes], guest_ref.at[target]))
    pairs.append((weight_ref, near_weight_ref))
    for number, tile in enumerate(spot.key_tiles[2:]):
        target = pl.ds(number * tile_tok, tile_tok)
        pairs.append((key_ref.at[tile_rows(tile, tile_tok)], far_key_ref.at[target]))
    copies = copied(pairs, sems)
    copies[0].wait()
    steps = -spot.guest_step

    def flag(col, col_step):
        return mask[2 * spot.edge + col, entry(steps, col_step)] > 0

    never = spot.near < 0
    cols = (spot.near, spot.far)
    rows = [[flag(col, key - col) for col in cols] for key in cols] + [
        [flag(spot.near, spot.near_step), never],
        [never, flag(spot.far, spot.far_step) & spot.there],
    ]
    for number, row in enumerate(key_bias(rows, tile_tok)):
        bias_ref[number : number + 1] = row
    for copy in copies[1:]:
        copy.wait()


def fold_into(column, value_ref, weight_ref, places):
    for head in range(HEADS):
        lanes = head_lanes(head)
        values = above(*[value_ref[place, lanes] for place in places])
        folded = contract_last(weight_ref[:, lanes], values)
        ref, where = column.folded_at(head)
        ref[where] = folded.astype(jnp.bfloat16)


def far_pack_kernel(
    block_count, block_cols, tile_tok, groups, key_ref, value_ref, weight_ref, guest_ref, *refs
):
    spot = Spot(block_count, block_cols)
    for out_ref, group in zip(refs, groups):
        out_ref[:, : len(group) * HD] = key_ref[:, group.start * HD : group.stop * HD]
    places = [tile_rows(tile, tile_tok) for tile in spot.key_tiles[2:]]
    fold_into(Column(refs, groups, weight_ref.shape[0]), value_ref, weight_ref, places)


def near_pack_kernel(
    block_count, block_cols, tile_tok, group,
    query_ref, key_ref, value_ref, weight_ref, near_ref, guest_ref,
):
    spot = Spot(block_count, block_cols)
    places = [tile_rows(tile, tile_tok) for tile in spot.key_tiles[:2]]
    for number, col in enumerate((spot.near, spot.far)):
        rows = slice(number * tile_tok, (number + 1) * tile_tok)
        near_ref[rows, : HEADS * HD] = key_ref[places[number], :]
        guest_ref[rows] = query_ref[
            tile_rows((spot.edge, col), tile_tok), group.start * HD : group.stop * HD
        ]
    column = Column([near_ref], (range(HEADS),), weight_ref.shape[0])
    fold_into(column, value_ref, weight_ref, places)


def own_kernel(
    block_count, block_cols, tile_tok, groups, mask_ref, query_ref, *refs
):
    count = len(groups)
    far_refs = refs[1 : 1 + count]
    out_ref, top_ref, sum_ref, side_bias_ref = refs[2 + count : 6 + count]
    own_scores, halo_scores, own_weights, halo_weights = refs[6 + count :]
    spot = Spot(block_count, block_cols)
    channels = out_ref.shape[1]
    half = 2 * tile_tok
    every = (range(HEADS),)
    near_column = Column(refs[:1], every, channels)
    far_column = Column(far_refs, groups, channels)
    inner_column = Column(refs[1 + count : 2 + count], every, channels)

    def flag(tile, row_step, col_step):
        return mask_ref[2 * tile[0] + tile[1], entry(row_step, col_step)] > 0

    bias = key_bias(
        [
            [flag(t, key[0] - t[0], key[1] - t[1]) for t in spot.lane_tiles]
            for key in spot.key_tiles
        ],
        tile_tok,
    )
    halo_bias = key_bias(
        [
            [flag(t, row - t[0], spot.near_step) for t in spot.lane_tiles[:2]]
            for row in (spot.edge, spot.rest)
        ],
        tile_tok,
    )
    side_rows = [
        [flag(t, row - t[0], spot.far_step) & spot.there for t in spot.lane_tiles[2:]]
        for row in (spot.rest, spot.edge)
    ]
    for number, row in enumerate(key_bias(side_rows, tile_tok)):
        side_bias_ref[number : number + 1] = row
    places = [tile_rows(tile, tile_tok) for tile in spot.lane_tiles]

    def score(head):
        lanes = head_lanes(head)
        query = above(*[query_ref[place, lanes] for place in places])
        keys = above(near_column.keys(head), far_column.keys(head))
        own = biased(contract_last(keys, query), bias, tile_tok)
        halo = biased(
            contract_last(inner_column.keys(head), query[:half]), halo_bias, tile_tok
        )
        own_scores[head] = own
        halo_scores[head] = halo
        top = largest(own)
        top_ref[head : head + 1, :half] = jnp.maximum(top[:, :half], largest(halo))
        top_ref[head : head + 1, half:] = top[:, half:]

    def soften(head):
        top = top_ref[head : head + 1]
        own_weights[head] = softened(own_scores[head], top)
        halo_weights[head] = softened(halo_scores[head], top[:, :half])

    def weigh(head):
        folded = with_ones(beside(near_column.folded(head), far_column.folded(head)))
        own = contract(folded, own_weights[head])
        halo = contract(with_ones(inner_column.folded(head)), halo_weights[head])
        left = own[:, :half] + halo
        out_ref[head, :, :half] = left[:channels]
        out_ref[head, :, half:] = own[:channels, half:]
        sum_ref[head : head + 1, :half] = left[channels : channels + 1]
        sum_ref[head : head + 1, half:] = own[channels : channels + 1, half:]

    pipelined(range(HEADS), score, soften, weigh)


def edge_kernel(
    block_count, block_cols, tile_tok, group,
    side_bias_ref, guest_bias_ref,
    query_ref, near_ref, far_ref, inner_ref, outer_ref, guest_ref, own_top_ref, own_sum_ref,
    out_ref, guest_out_ref, side_top_ref, guest_top_ref, log_ref, send_ref,
    side_scores, guest_scores, side_weights, guest_weights, side_sum_ref, guest_sum_ref,
):
    spot = Spot(block_count, block_cols)
    channels = out_ref.shape[1]
    half = 2 * tile_tok
    near_column = Column([near_ref], (range(HEADS),), channels)
    inner_column = Column([inner_ref], (range(HEADS),), channels)
    far_column = Column([far_ref], (group,), channels)
    outer_column = Column([outer_ref], (group,), channels)

    bias = [side_bias_ref[number : number + 1] for number in range(2)]
    guest_bias = [guest_bias_ref[number : number + 1] for number in range(4)]
    places = [tile_rows(tile, tile_tok) for tile in spot.lane_tiles[2:]]
    left = lax.broadcasted_iota(jnp.int32, (channels, half), 1) < tile_tok

    def score(head):
        row = head - group.start
        query = above(*[query_ref[place, head_lanes(head)] for place in places])
        scores = biased(contract_last(outer_column.keys(head), query), bias, tile_tok)
        side_scores[row] = scores
        side_top_ref[row : row + 1] = largest(scores)
        keys = above(
            near_column.keys(head)[:tile_tok],
            far_column.keys(head)[tile_tok:],
            inner_column.keys(head)[:tile_tok],
            outer_column.keys(head)[tile_tok:],
        )
        scores = contract_last(keys, guest_ref[:, head_lanes(row)])
        scores = biased(scores, guest_bias, tile_tok)
        guest_scores[row] = scores
        guest_top_ref[row : row + 1] = largest(scores)

    def soften(head):
        row = head - group.start
        side_weights[row] = softened(side_scores[row], side_top_ref[row : row + 1])
        guest_weights[row] = softened(guest_scores[row], guest_top_ref[row : row + 1])

    def weigh(head):
        row = head - group.start
        side = contract(with_ones(outer_column.folded(head)), side_weights[row])
        out_ref[row] = side[:channels]
        side_sum_ref[row : row + 1] = side[channels : channels + 1]
        folded = beside(
            jnp.where(left, near_column.folded(head), far_column.folded(head)),
            jnp.where(left, inner_column.folded(head), outer_column.folded(head)),
        )
        guest = contract(with_ones(folded), guest_weights[row])
        guest_out_ref[row] = guest[:channels].astype(guest_out_ref.dtype)
        guest_sum_ref[row : row + 1] = guest[channels : channels + 1]

    pipelined(group, score, soften, weigh)

    mine = slice(group.start, group.stop)
    near_log = log_sum(own_top_ref[mine, :half], own_sum_ref[mine, :half])
    far_log = joint(
        log_sum(own_top_ref[mine, half:], own_sum_ref[mine, half:]),
        log_sum(side_top_ref[...], side_sum_ref[...]),
    )
    log_ref[:, :half] = near_log
    log_ref[:, half:] = far_log
    send_ref[0] = beside(near_log[:, tile_tok:], far_log[:, :tile_tok])
    send_ref[1] = log_sum(guest_top_ref[...], guest_sum_ref[...])


def log_sum(top, total):
    return top * EXP_SCALE + jnp.log2(total)


def joint(left, right):
    top = jnp.maximum(left, right)
    return top + jnp.log2(jnp.exp2(left - top) + jnp.exp2(right - top))


def share_of(top, whole):
    return jnp.exp2(top * EXP_SCALE - whole)


def centred(values, fill, tile_tok):
    side = jnp.full((values.shape[0], tile_tok), fill, values.dtype)
    return jnp.concatenate([side, values, side], axis=1)


def guest_blend_kernel(
    guest_out_ref, guest_top_ref, sent_ref, got_ref, late_top_ref, late_sent_ref, back_ref
):
    heads, channels, _ = guest_out_ref.shape
    share = share_of(guest_top_ref[...], joint(sent_ref[1], got_ref[0]))
    velocity = jnp.zeros(guest_out_ref.shape[1:], jnp.float32)
    for row in range(heads):
        velocity = velocity + share[row : row + 1] * guest_out_ref[row]
    late = late_top_ref.shape[0]
    back_ref[:channels] = velocity
    back_ref[channels : channels + late] = late_sent_ref[1]
    back_ref[channels + late : channels + 2 * late] = late_top_ref[...]


def own_part(tile_tok, group, own_out_ref, side_out_ref, own_top_ref, side_top_ref, whole):
    half = 2 * tile_tok
    own_share = share_of(own_top_ref[group.start : group.stop], whole)
    side_share = share_of(side_top_ref[...], whole[:, half:])
    near = jnp.zeros((own_out_ref.shape[1], half), jnp.float32)
    far = jnp.zeros((own_out_ref.shape[1], half), jnp.float32)
    for row, head in enumerate(group):
        one = slice(row, row + 1)
        near = near + own_share[one, :half] * own_out_ref[head, :, :half]
        far = far + own_share[one, half:] * own_out_ref[head, :, half:]
        far = far + side_share[one] * side_out_ref[row]
    return beside(near, far)


def own_blend_kernel(
    tile_tok, group, own_out_ref, side_out_ref, own_top_ref, side_top_ref,
    log_ref, got_ref, velocity_ref,
):
    whole = joint(log_ref[...], centred(got_ref[1], NEG, tile_tok))
    velocity_ref[...] = own_part(
        tile_tok, group, own_out_ref, side_out_ref, own_top_ref, side_top_ref, whole
    )


def join_kernel(
    tile_tok, group, own_out_ref, side_out_ref, own_top_ref, side_top_ref,
    log_ref, velocity_ref, back_ref, back_out_ref, out_ref,
):
    channels = own_out_ref.shape[1]
    half = 2 * tile_tok
    late = len(group)
    guest_log = back_ref[channels : channels + late]
    whole = joint(log_ref[...], centred(guest_log, NEG, tile_tok))
    velocity = own_part(
        tile_tok, group, own_out_ref, side_out_ref, own_top_ref, side_top_ref, whole
    )
    edge = beside(whole[:, tile_tok:half], whole[:, half : half + tile_tok])
    share = share_of(back_ref[channels + late : channels + 2 * late], edge)
    guest = back_ref[:channels]
    for row in range(late):
        guest = guest + share[row : row + 1] * back_out_ref[row].astype(jnp.float32)
    out_ref[...] = velocity_ref[...] + velocity + centred(guest, 0.0, tile_tok)


def update_kernel(
    block_count, block_cols, tile_tok, half_size,
    step_ref, velocity_ref, partner_ref, latent_ref,
    guided_ref, clean_ref, next_ref,
):
    spot = Spot(block_count, block_cols)
    half = 2 * tile_tok
    is_cond = spot.index < half_size
    own = velocity_ref[...]
    other = partner_ref[...]
    cond = jnp.where(is_cond, own, other)
    uncond = jnp.where(is_cond, other, own)
    blended = uncond + GUIDANCE * (cond - uncond)
    edge = blended[:, tile_tok : tile_tok + half]
    rest = jnp.concatenate([blended[:, :tile_tok], blended[:, tile_tok + half :]], axis=1)

    def natural(pair):
        swapped = jnp.concatenate([pair[:, tile_tok:], pair[:, :tile_tok]], axis=1)
        return jnp.where(spot.near == 0, pair, swapped)

    edge = natural(edge)
    rest = natural(rest)
    moment = jnp.full((1, half), step_ref[0].astype(jnp.float32))
    sigma_now = flow_sigma(moment)
    step_size = flow_sigma(moment + 1.0) - sigma_now
    for row in range(2):
        lanes = slice(row * half, (row + 1) * half)
        guided = jnp.where(spot.edge == row, edge, rest)
        latent = latent_ref[:, lanes]
        guided_ref[:, lanes] = guided
        clean_ref[:, lanes] = latent - sigma_now * guided
        next_ref[:, lanes] = latent + step_size * guided


def kernel_call(body, args, outs, smem=0, scratch=(), far=(), stay=True):
    spaces = [pltpu.SMEM] * smem + [pltpu.VMEM] * (len(args) - smem)
    for number in far:
        spaces[number] = pltpu.HBM
    args = [
        arg if space == pltpu.SMEM else pltpu.with_memory_space_constraint(arg, space)
        for arg, space in zip(args, spaces)
    ]
    specs = [pl.BlockSpec(memory_space=space) for space in spaces]
    return pl.pallas_call(
        body,
        out_shape=[
            pltpu.VMEM(shape, dtype) if stay else jax.ShapeDtypeStruct(shape, dtype)
            for shape, dtype in outs
        ],
        in_specs=specs,
        out_specs=[pl.BlockSpec(memory_space=pltpu.VMEM) for _ in outs],
        scratch_shapes=list(scratch),
        compiler_params=pltpu.CompilerParams(vmem_limit_bytes=VMEM_LIMIT),
    )(*args)


def one_frame_tile(frame_count):
    return frame_count == SH // 2 * (SW // 2) * 2 and SH == 4 and SW % 4 == 0


def per_device_plan(query_rows, key_rows, value_rows, tile_mask, head_weight, latent, step_index):
    frame_count = lax.axis_size("frame")
    half_size = frame_count // 2
    block_cols = SW // 2
    block_count = SH // 2 * block_cols
    tok_rows, width = query_rows.shape
    tile_tok = tok_rows // 4
    half = 2 * tile_tok
    channels = head_weight.shape[1]
    places = range(frame_count)
    row_pairs = [
        (f, f + block_cols if f % block_count < block_cols else f - block_cols)
        for f in places
    ]
    mate_pairs = [(f, f + 1 - 2 * (f % 2)) for f in places]
    side_pairs = []
    group_count = lax.axis_size("groups")
    for f in places:
        step = 2 * (f % 2) - 1
        inside = 0 <= f % block_cols + step < block_cols
        for g in range(group_count):
            if inside:
                side_pairs.append((g * frame_count + f, g * frame_count + f + step))
            else:
                other = (g + 1) % group_count
                side_pairs.append((g * frame_count + f, other * frame_count + f))
    branch_pairs = [(f, (f + half_size) % frame_count) for f in places]
    sizes = (block_count, block_cols, tile_tok)
    single = jnp.float32
    half_type = query_rows.dtype
    groups = (range(FIRST_HEADS), range(FIRST_HEADS, HEADS))
    every = (range(HEADS),)
    early, late = (len(group) for group in groups)

    weight_t = head_weight.T
    guest_send, edge_bias, far_keys, weight_t = kernel_call(
        functools.partial(guest_pack_kernel, *sizes),
        (query_rows, key_rows, tile_mask, weight_t),
        (
            ((half, early * HD), half_type),
            ((4, half), single),
            ((half, width), half_type),
            (weight_t.shape, half_type),
        ),
        0,
        (pltpu.SMEM(tile_mask.shape, tile_mask.dtype), pltpu.SemaphoreType.DMA((6,))),
        far=(0, 1, 2, 3),
    )

    def sent_over(value, pairs, axes="frame"):
        return lax.ppermute(value, axes, pairs)

    def column_type(group):
        return ((half, packed_width(len(group), channels)), half_type)

    guests = [sent_over(guest_send, row_pairs)]
    far = kernel_call(
        functools.partial(far_pack_kernel, *sizes, groups),
        (far_keys, value_rows, weight_t, guest_send),
        [column_type(group) for group in groups],
    )
    outer = [sent_over(column, side_pairs, ("groups", "frame")) for column in far]
    near, guest_send = kernel_call(
        functools.partial(near_pack_kernel, *sizes, groups[1]),
        (query_rows, key_rows, value_rows, weight_t),
        (column_type(every[0]), ((half, late * HD), half_type)),
    )
    inner = sent_over(near, mate_pairs)
    guest_bias = sent_over(edge_bias, row_pairs)
    guests.append(sent_over(guest_send, row_pairs))
    stats = ((HEADS, tok_rows), single)
    own_out, own_top, own_sum, side_bias = kernel_call(
        functools.partial(own_kernel, *sizes, groups),
        (tile_mask, query_rows, near, *far, inner),
        (((HEADS, channels, tok_rows), single), stats, stats, ((2, half), single)),
        1,
        (
            pltpu.VMEM((HEADS, tok_rows, tok_rows), single),
            pltpu.VMEM((HEADS, half, half), single),
            pltpu.VMEM((HEADS, tok_rows, tok_rows), half_type),
            pltpu.VMEM((HEADS, half, half), half_type),
        ),
    )

    def edge(number, guest_type):
        group = groups[number]
        heads = len(group)
        return kernel_call(
            functools.partial(edge_kernel, *sizes, group),
            (
                side_bias, guest_bias, query_rows, near, far[number], inner,
                outer[number], guests[number], own_top, own_sum,
            ),
            (
                ((heads, channels, half), single),
                ((heads, channels, half), guest_type),
                ((heads, half), single),
                ((heads, half), single),
                ((heads, tok_rows), single),
                ((2, heads, half), single),
            ),
            0,
            (
                pltpu.VMEM((heads, half, half), single),
                pltpu.VMEM((heads, tok_rows, half), single),
                pltpu.VMEM((heads, half, half), half_type),
                pltpu.VMEM((heads, tok_rows, half), half_type),
                pltpu.VMEM((heads, half), single),
                pltpu.VMEM((heads, half), single),
            ),
        )

    side_out, guest_out, side_top, guest_top, log, sent = edge(0, single)
    got = sent_over(sent, row_pairs)
    late_side, late_guest, late_side_top, late_guest_top, late_log, late_sent = edge(1, half_type)
    (guest_velocity,) = kernel_call(
        guest_blend_kernel,
        (guest_out, guest_top, sent, got, late_guest_top, late_sent),
        (((channels + 2 * late, half), single),),
    )
    back = sent_over(guest_velocity, row_pairs)
    back_out = sent_over(late_guest, row_pairs)
    velocity_type = ((channels, tok_rows), single)
    (velocity,) = kernel_call(
        functools.partial(own_blend_kernel, tile_tok, groups[0]),
        (own_out, side_out, own_top, side_top, log, got),
        (velocity_type,),
    )
    (velocity,) = kernel_call(
        functools.partial(join_kernel, tile_tok, groups[1]),
        (
            own_out, late_side, own_top, late_side_top, late_log, velocity,
            back, back_out,
        ),
        (velocity_type,),
    )
    partner = sent_over(velocity, branch_pairs)
    out = ((channels, tok_rows), single)
    results = kernel_call(
        functools.partial(update_kernel, *sizes, half_size),
        (step_index, velocity, partner, latent.T),
        (out, out, out),
        1,
        stay=False,
    )
    return tuple(result.T for result in results)


def per_device(*args):
    return per_device_plan(*args)


def solution(mesh):
    placed = (
        P(("groups", "frame"), None),
        P(("groups", "frame"), None),
        P(("groups", "frame"), None),
        P(("groups", "frame"), None),
        P(),
        P(("groups", "frame"), None),
        P("groups"),
    )
    fast = one_frame_tile(mesh.shape["frame"])
    return jax.shard_map(
        per_device if fast else per_device_frames,
        mesh=mesh,
        in_specs=placed,
        out_specs=(
            P(("groups", "frame"), None),
            P(("groups", "frame"), None),
            P(("groups", "frame"), None),
        ),
        check_vma=False,
    )
```

```python
import functools
import math

import jax
import jax.numpy as jnp
from jax import lax
from jax.experimental import pallas as pl
from jax.experimental.pallas import tpu as pltpu
from jax.sharding import PartitionSpec as P


HEADS = 20
HD = 128
SH = 4
SW = 8
SAMPLE_STEPS = 50


GUIDANCE = 5.0
FLOW_SHIFT = 5.0


def passed_along(value, axis, steps):
    count = lax.axis_size(axis)
    pairs = [(source, (source + steps) % count) for source in range(count)]
    return lax.ppermute(value, axis, pairs)


def flow_sigma(moment):
    remain = 1.0 - moment / SAMPLE_STEPS
    return FLOW_SHIFT * remain / (1.0 + (FLOW_SHIFT - 1.0) * remain)


def edge_range(offset):
    if offset < 0:
        return (1, 2)
    if offset > 0:
        return (0, 1)
    return (0, 2)


def direct_window(stacked, block_count, block_cols):
    received_parts = {}
    for frame_step in (1, 0, -1):
        for row_step in (1, 0, -1):
            for col_step in (1, 0, -1):
                distance = frame_step * block_count + row_step * block_cols + col_step
                row_start, row_stop = edge_range(row_step)
                col_start, col_stop = edge_range(col_step)
                outgoing = stacked[row_start:row_stop, col_start:col_stop]
                if frame_step == 0 and row_step == 0 and (col_step == 0):
                    received = outgoing
                elif row_step == 0 and col_step == 0:
                    received = passed_along(outgoing, "frame", -distance)
                elif row_step != 0 and col_step != 0:
                    received = passed_along(outgoing, "frame", -distance)
                else:
                    received = passed_along(outgoing, "frame", -distance)
                received_parts[frame_step, row_step, col_step] = received
    planes = []
    for frame_step in (-1, 0, 1):
        row_parts = []
        for row_step in (-1, 0, 1):
            col_parts = [received_parts[frame_step, row_step, col_step] for col_step in (-1, 0, 1)]
            row_parts.append(jnp.concatenate(col_parts, axis=1))
        planes.append(jnp.concatenate(row_parts, axis=0))
    return planes


def window_allowed(tile_mask, frame_tile, block_row, block_col, tile_frames):
    offsets = jnp.arange(27, dtype=jnp.int32)
    frame_step = offsets // 9 - 1
    row_step = offsets // 3 % 3 - 1
    col_step = offsets % 3 - 1
    local_tile = jnp.arange(4, dtype=jnp.int32)
    tile_row = 2 * block_row + local_tile // 2
    tile_col = 2 * block_col + local_tile % 2
    frame_there = frame_tile + frame_step
    row_there = tile_row[:, None] + row_step[None, :]
    col_there = tile_col[:, None] + col_step[None, :]
    usable = ((frame_there >= 0) & (frame_there < tile_frames))[None, :]
    usable = usable & (row_there >= 0) & (row_there < SH) & (col_there >= 0) & (col_there < SW)
    return usable & (tile_mask > 0)


def attend_window(query_rows, planes, allowed):
    tok_rows, inner_width = query_rows.shape
    tile_tok = tok_rows // 4
    query_tiles = query_rows.reshape(4, tile_tok, inner_width)
    mask_full = allowed[:, None, :, None]

    def one_head(head_number, result_rows):
        key_planes = [lax.dynamic_slice_in_dim(plane, head_number * HD, HD, 3) for plane in planes]
        value_planes = [
            lax.dynamic_slice_in_dim(plane, inner_width + head_number * HD, HD, 3)
            for plane in planes
        ]
        key_list = []
        value_list = []
        for row_local in range(2):
            for col_local in range(2):
                key_list.append(
                    jnp.stack(
                        [
                            part[row_local : row_local + 3, col_local : col_local + 3]
                            for part in key_planes
                        ]
                    ).reshape(27 * tile_tok, HD)
                )
                value_list.append(
                    jnp.stack(
                        [
                            part[row_local : row_local + 3, col_local : col_local + 3]
                            for part in value_planes
                        ]
                    ).reshape(27 * tile_tok, HD)
                )
        key_tiles = jnp.stack(key_list)
        value_tiles = jnp.stack(value_list)
        head_query = lax.dynamic_slice_in_dim(query_tiles, head_number * HD, HD, 2)
        scores = jnp.einsum(
            "qtd,qkd->qtk", head_query, key_tiles, preferred_element_type=jnp.float32
        ) / math.sqrt(HD)
        scores = scores.reshape(4, tile_tok, 27, tile_tok)
        scores = jnp.where(mask_full, scores, -1e30)
        row_max = jnp.max(scores, axis=(2, 3), keepdims=True)
        shifted = jnp.where(mask_full, jnp.exp(scores - row_max), 0.0)
        weights = (shifted / jnp.sum(shifted, axis=(2, 3), keepdims=True)).astype(jnp.bfloat16)
        weights = weights.reshape(4, tile_tok, 27 * tile_tok)
        head_out = jnp.einsum(
            "qtk,qkd->qtd", weights, value_tiles, preferred_element_type=jnp.float32
        ).astype(jnp.bfloat16)
        return lax.dynamic_update_slice_in_dim(result_rows, head_out, head_number * HD, 2)

    result_rows = lax.fori_loop(
        0, HEADS, one_head, jnp.zeros((4, tile_tok, inner_width), jnp.bfloat16)
    )
    return result_rows.reshape(tok_rows, inner_width)


def per_device_frames(query_rows, key_rows, value_rows, tile_mask, head_weight, latent, step_index):
    frame_count = lax.axis_size("frame")
    frame_index = lax.axis_index("frame")
    half_size = frame_count // 2
    block_cols = SW // 2
    block_count = SH // 2 * block_cols
    tile_frames = frame_count // (2 * block_count)
    frame_tile = frame_index // block_count % tile_frames
    block_spot = frame_index % block_count
    block_row = block_spot // block_cols
    block_col = block_spot % block_cols
    tok_rows, inner_width = query_rows.shape
    tile_tok = tok_rows // 4
    stacked = jnp.concatenate([key_rows, value_rows], axis=1).reshape(
        2, 2, tile_tok, 2 * inner_width
    )
    planes = direct_window(stacked, block_count, block_cols)
    allowed = window_allowed(tile_mask, frame_tile, block_row, block_col, tile_frames)
    attention = attend_window(query_rows, planes, allowed)
    velocity = jnp.dot(attention, head_weight, preferred_element_type=jnp.float32)
    partner_rows = passed_along(velocity, "frame", half_size)
    is_cond = frame_index < half_size
    cond_rows = jnp.where(is_cond, velocity, partner_rows)
    uncond_rows = jnp.where(is_cond, partner_rows, velocity)
    guided = uncond_rows + GUIDANCE * (cond_rows - uncond_rows)
    moment = step_index[0].astype(jnp.float32)
    sigma_now = flow_sigma(moment)
    step_size = flow_sigma(moment + 1.0) - sigma_now
    clean = latent - sigma_now * guided
    latent_next = latent + step_size * guided
    return (guided, clean, latent_next)


NEG = -1e30
VMEM_LIMIT = 16 << 20
FIRST_HEADS = 14
EXP_SCALE = math.log2(math.e) / math.sqrt(HD)


def contract_last(left, right):
    return lax.dot_general(
        left, right, (((1,), (1,)), ((), ())), preferred_element_type=jnp.float32
    )


def contract(left, right):
    return jnp.dot(left, right, preferred_element_type=jnp.float32)


def head_lanes(head):
    return slice(head * HD, (head + 1) * HD)


class Spot:
    def __init__(self, block_count, block_cols):
        self.index = lax.axis_index("frame")
        spot = self.index % block_count
        block_row = spot // block_cols
        block_col = spot % block_cols
        odd = block_col % 2
        self.edge = 1 - block_row
        self.rest = block_row
        self.near = 1 - odd
        self.far = odd
        self.near_step = 1 - 2 * odd
        self.far_step = 2 * odd - 1
        side = block_col + self.far_step
        self.there = (side >= 0) & (side < block_cols)
        self.guest_step = 2 * block_row - 1
        self.lane_tiles = (
            (self.rest, self.near),
            (self.edge, self.near),
            (self.edge, self.far),
            (self.rest, self.far),
        )
        self.key_tiles = (
            (self.edge, self.near),
            (self.rest, self.near),
            (self.rest, self.far),
            (self.edge, self.far),
        )


def tile_rows(tile, tile_tok):
    row, col = tile
    return pl.ds(pl.multiple_of((2 * row + col) * tile_tok, tile_tok), tile_tok)


def entry(row_step, col_step):
    return 9 + 3 * (row_step + 1) + col_step + 1


def bias_of(flag):
    return jnp.where(flag, jnp.float32(0.0), jnp.float32(NEG))


def key_bias(rows, tile_tok):
    biases = []
    for flags in rows:
        lanes = len(flags) * tile_tok
        lane = lax.broadcasted_iota(jnp.int32, (1, lanes), 1) // tile_tok
        bias = jnp.zeros((1, lanes), jnp.float32)
        for number, flag in enumerate(flags):
            bias = jnp.where(lane == number, bias_of(flag), bias)
        biases.append(bias)
    return biases


def biased(scores, biases, tile_tok):
    return above(
        *[scores[t * tile_tok : (t + 1) * tile_tok] + row for t, row in enumerate(biases)]
    )


def beside(left, right):
    return jnp.concatenate([left, right], axis=1)


def above(*parts):
    return jnp.concatenate(parts, axis=0)


def largest(scores):
    return jnp.max(scores, axis=0, keepdims=True)


def softened(scores, top):
    return jnp.exp2((scores - top) * EXP_SCALE).astype(jnp.bfloat16)


def with_ones(folded):
    return above(folded, jnp.ones((16, folded.shape[1]), folded.dtype))


def pipelined(heads, *stages):
    for turn in range(len(heads) + len(stages) - 1):
        for number, stage in enumerate(stages):
            if 0 <= turn - number < len(heads):
                stage(heads[turn - number])


def packed_width(heads, channels):
    return heads * HD + (heads + 1) // 2 * 2 * channels


class Column:
    def __init__(self, refs, groups, channels):
        self.refs = refs
        self.groups = groups
        self.channels = channels

    def place(self, head):
        for ref, group in zip(self.refs, self.groups):
            if head in group:
                return ref, head - group.start, len(group) * HD

    def keys(self, head):
        ref, local, _ = self.place(head)
        return ref[:, head_lanes(local)]

    def folded_at(self, head):
        ref, local, width = self.place(head)
        row = local % 2 * self.channels
        lane = width + local // 2 * 2 * self.channels
        return ref, (slice(row, row + self.channels), slice(lane, lane + 2 * self.channels))

    def folded(self, head):
        ref, where = self.folded_at(head)
        return ref[where]


def copied(pairs, sems):
    copies = [
        pltpu.make_async_copy(source, target, sems.at[number])
        for number, (source, target) in enumerate(pairs)
    ]
    for copy in copies:
        copy.start()
    return copies


def guest_pack_kernel(
    block_count, block_cols, tile_tok,
    query_ref, key_ref, mask_ref, weight_ref,
    guest_ref, bias_ref, far_key_ref, near_weight_ref, mask, sems,
):
    spot = Spot(block_count, block_cols)
    pairs = [(mask_ref, mask)]
    lanes = pl.ds(0, guest_ref.shape[1])
    for number, col in enumerate((spot.near, spot.far)):
        target = pl.ds(number * tile_tok, tile_tok)
        rows = tile_rows((spot.edge, col), tile_tok)
        pairs.append((query_ref.at[rows, lanes], guest_ref.at[target]))
    pairs.append((weight_ref, near_weight_ref))
    for number, tile in enumerate(spot.key_tiles[2:]):
        target = pl.ds(number * tile_tok, tile_tok)
        pairs.append((key_ref.at[tile_rows(tile, tile_tok)], far_key_ref.at[target]))
    copies = copied(pairs, sems)
    copies[0].wait()
    steps = -spot.guest_step

    def flag(col, col_step):
        return mask[2 * spot.edge + col, entry(steps, col_step)] > 0

    never = spot.near < 0
    cols = (spot.near, spot.far)
    rows = [[flag(col, key - col) for col in cols] for key in cols] + [
        [flag(spot.near, spot.near_step), never],
        [never, flag(spot.far, spot.far_step) & spot.there],
    ]
    for number, row in enumerate(key_bias(rows, tile_tok)):
        bias_ref[number : number + 1] = row
    for copy in copies[1:]:
        copy.wait()


def fold_into(column, value_ref, weight_ref, places):
    for head in (head for group in column.groups for head in group):
        lanes = head_lanes(head)
        values = above(*[value_ref[place, lanes] for place in places])
        folded = contract_last(weight_ref[:, lanes], values)
        ref, where = column.folded_at(head)
        ref[where] = folded.astype(jnp.bfloat16)


def far_pack_kernel(
    block_count, block_cols, tile_tok, group,
    key_ref, value_ref, weight_ref, guest_ref, far_ref,
):
    spot = Spot(block_count, block_cols)
    far_ref[:, : len(group) * HD] = key_ref[:, group.start * HD : group.stop * HD]
    places = [tile_rows(tile, tile_tok) for tile in spot.key_tiles[2:]]
    fold_into(Column([far_ref], (group,), weight_ref.shape[0]), value_ref, weight_ref, places)


def near_pack_kernel(
    block_count, block_cols, tile_tok, group,
    query_ref, key_ref, value_ref, weight_ref, far_key_ref, near_ref, guest_ref, far_ref,
):
    spot = Spot(block_count, block_cols)
    far_pack_kernel(
        block_count, block_cols, tile_tok, group,
        far_key_ref, value_ref, weight_ref, None, far_ref,
    )
    places = [tile_rows(tile, tile_tok) for tile in spot.key_tiles[:2]]
    for number, col in enumerate((spot.near, spot.far)):
        rows = slice(number * tile_tok, (number + 1) * tile_tok)
        near_ref[rows, : HEADS * HD] = key_ref[places[number], :]
        guest_ref[rows] = query_ref[
            tile_rows((spot.edge, col), tile_tok), group.start * HD : group.stop * HD
        ]
    column = Column([near_ref], (range(HEADS),), weight_ref.shape[0])
    fold_into(column, value_ref, weight_ref, places)


def own_kernel(
    block_count, block_cols, tile_tok, groups, mask_ref, query_ref, *refs
):
    count = len(groups)
    far_refs = refs[1 : 1 + count]
    out_ref, top_ref, sum_ref, side_bias_ref = refs[2 + count : 6 + count]
    own_scores, halo_scores, own_weights, halo_weights = refs[6 + count :]
    spot = Spot(block_count, block_cols)
    channels = out_ref.shape[1]
    half = 2 * tile_tok
    every = (range(HEADS),)
    near_column = Column(refs[:1], every, channels)
    far_column = Column(far_refs, groups, channels)
    inner_column = Column(refs[1 + count : 2 + count], every, channels)

    def flag(tile, row_step, col_step):
        return mask_ref[2 * tile[0] + tile[1], entry(row_step, col_step)] > 0

    bias = key_bias(
        [
            [flag(t, key[0] - t[0], key[1] - t[1]) for t in spot.lane_tiles]
            for key in spot.key_tiles
        ],
        tile_tok,
    )
    halo_bias = key_bias(
        [
            [flag(t, row - t[0], spot.near_step) for t in spot.lane_tiles[:2]]
            for row in (spot.edge, spot.rest)
        ],
        tile_tok,
    )
    side_rows = [
        [flag(t, row - t[0], spot.far_step) & spot.there for t in spot.lane_tiles[2:]]
        for row in (spot.rest, spot.edge)
    ]
    for number, row in enumerate(key_bias(side_rows, tile_tok)):
        side_bias_ref[number : number + 1] = row
    places = [tile_rows(tile, tile_tok) for tile in spot.lane_tiles]

    def score(head):
        lanes = head_lanes(head)
        query = above(*[query_ref[place, lanes] for place in places])
        keys = above(near_column.keys(head), far_column.keys(head))
        own = biased(contract_last(keys, query), bias, tile_tok)
        halo = biased(
            contract_last(inner_column.keys(head), query[:half]), halo_bias, tile_tok
        )
        own_scores[head] = own
        halo_scores[head] = halo
        top = largest(own)
        top_ref[head : head + 1, :half] = jnp.maximum(top[:, :half], largest(halo))
        top_ref[head : head + 1, half:] = top[:, half:]

    def soften(head):
        top = top_ref[head : head + 1]
        own_weights[head] = softened(own_scores[head], top)
        halo_weights[head] = softened(halo_scores[head], top[:, :half])

    def weigh(head):
        folded = with_ones(beside(near_column.folded(head), far_column.folded(head)))
        own = contract(folded, own_weights[head])
        halo = contract(with_ones(inner_column.folded(head)), halo_weights[head])
        left = own[:, :half] + halo
        out_ref[head, :, :half] = left[:channels]
        out_ref[head, :, half:] = own[:channels, half:]
        sum_ref[head : head + 1, :half] = left[channels : channels + 1]
        sum_ref[head : head + 1, half:] = own[channels : channels + 1, half:]

    pipelined(range(HEADS), score, soften, weigh)


def edge_kernel(
    block_count, block_cols, tile_tok, group,
    side_bias_ref, guest_bias_ref,
    query_ref, near_ref, far_ref, inner_ref, outer_ref, guest_ref, own_top_ref, own_sum_ref,
    out_ref, guest_out_ref, side_top_ref, guest_top_ref, log_ref, send_ref,
    side_scores, guest_scores, side_weights, guest_weights, side_sum_ref, guest_sum_ref,
):
    spot = Spot(block_count, block_cols)
    channels = out_ref.shape[1]
    half = 2 * tile_tok
    near_column = Column([near_ref], (range(HEADS),), channels)
    inner_column = Column([inner_ref], (range(HEADS),), channels)
    far_column = Column([far_ref], (group,), channels)
    outer_column = Column([outer_ref], (group,), channels)

    bias = [side_bias_ref[number : number + 1] for number in range(2)]
    guest_bias = [guest_bias_ref[number : number + 1] for number in range(4)]
    places = [tile_rows(tile, tile_tok) for tile in spot.lane_tiles[2:]]
    left = lax.broadcasted_iota(jnp.int32, (channels, half), 1) < tile_tok

    def score(head):
        row = head - group.start
        query = above(*[query_ref[place, head_lanes(head)] for place in places])
        scores = biased(contract_last(outer_column.keys(head), query), bias, tile_tok)
        side_scores[row] = scores
        side_top_ref[row : row + 1] = largest(scores)
        keys = above(
            near_column.keys(head)[:tile_tok],
            far_column.keys(head)[tile_tok:],
            inner_column.keys(head)[:tile_tok],
            outer_column.keys(head)[tile_tok:],
        )
        scores = contract_last(keys, guest_ref[:, head_lanes(row)])
        scores = biased(scores, guest_bias, tile_tok)
        guest_scores[row] = scores
        guest_top_ref[row : row + 1] = largest(scores)

    def soften(head):
        row = head - group.start
        side_weights[row] = softened(side_scores[row], side_top_ref[row : row + 1])
        guest_weights[row] = softened(guest_scores[row], guest_top_ref[row : row + 1])

    def weigh(head):
        row = head - group.start
        side = contract(with_ones(outer_column.folded(head)), side_weights[row])
        out_ref[row] = side[:channels]
        side_sum_ref[row : row + 1] = side[channels : channels + 1]
        folded = beside(
            jnp.where(left, near_column.folded(head), far_column.folded(head)),
            jnp.where(left, inner_column.folded(head), outer_column.folded(head)),
        )
        guest = contract(with_ones(folded), guest_weights[row])
        guest_out_ref[row] = guest[:channels].astype(guest_out_ref.dtype)
        guest_sum_ref[row : row + 1] = guest[channels : channels + 1]

    pipelined(group, score, soften, weigh)

    mine = slice(group.start, group.stop)
    near_log = log_sum(own_top_ref[mine, :half], own_sum_ref[mine, :half])
    far_log = joint(
        log_sum(own_top_ref[mine, half:], own_sum_ref[mine, half:]),
        log_sum(side_top_ref[...], side_sum_ref[...]),
    )
    log_ref[:, :half] = near_log
    log_ref[:, half:] = far_log
    send_ref[0] = beside(near_log[:, tile_tok:], far_log[:, :tile_tok])
    send_ref[1] = log_sum(guest_top_ref[...], guest_sum_ref[...])


def log_sum(top, total):
    return top * EXP_SCALE + jnp.log2(total)


def joint(left, right):
    top = jnp.maximum(left, right)
    return top + jnp.log2(jnp.exp2(left - top) + jnp.exp2(right - top))


def share_of(top, whole):
    return jnp.exp2(top * EXP_SCALE - whole)


def centred(values, fill, tile_tok):
    side = jnp.full((values.shape[0], tile_tok), fill, values.dtype)
    return jnp.concatenate([side, values, side], axis=1)


def guest_blend_kernel(
    guest_out_ref, guest_top_ref, sent_ref, got_ref, late_top_ref, late_sent_ref, back_ref
):
    heads, channels, _ = guest_out_ref.shape
    share = share_of(guest_top_ref[...], joint(sent_ref[1], got_ref[0]))
    velocity = jnp.zeros(guest_out_ref.shape[1:], jnp.float32)
    for row in range(heads):
        velocity = velocity + share[row : row + 1] * guest_out_ref[row]
    late = late_top_ref.shape[0]
    back_ref[:channels] = velocity
    back_ref[channels : channels + late] = late_sent_ref[1]
    back_ref[channels + late : channels + 2 * late] = late_top_ref[...]


def own_part(tile_tok, group, own_out_ref, side_out_ref, own_top_ref, side_top_ref, whole):
    half = 2 * tile_tok
    own_share = share_of(own_top_ref[group.start : group.stop], whole)
    side_share = share_of(side_top_ref[...], whole[:, half:])
    near = jnp.zeros((own_out_ref.shape[1], half), jnp.float32)
    far = jnp.zeros((own_out_ref.shape[1], half), jnp.float32)
    for row, head in enumerate(group):
        one = slice(row, row + 1)
        near = near + own_share[one, :half] * own_out_ref[head, :, :half]
        far = far + own_share[one, half:] * own_out_ref[head, :, half:]
        far = far + side_share[one] * side_out_ref[row]
    return beside(near, far)


def own_blend_kernel(
    tile_tok, group, own_out_ref, side_out_ref, own_top_ref, side_top_ref,
    log_ref, got_ref, velocity_ref,
):
    whole = joint(log_ref[...], centred(got_ref[1], NEG, tile_tok))
    velocity_ref[...] = own_part(
        tile_tok, group, own_out_ref, side_out_ref, own_top_ref, side_top_ref, whole
    )


def join_kernel(
    tile_tok, group, own_out_ref, side_out_ref, own_top_ref, side_top_ref,
    log_ref, velocity_ref, back_ref, back_out_ref, out_ref,
):
    channels = own_out_ref.shape[1]
    half = 2 * tile_tok
    late = len(group)
    guest_log = back_ref[channels : channels + late]
    whole = joint(log_ref[...], centred(guest_log, NEG, tile_tok))
    velocity = own_part(
        tile_tok, group, own_out_ref, side_out_ref, own_top_ref, side_top_ref, whole
    )
    edge = beside(whole[:, tile_tok:half], whole[:, half : half + tile_tok])
    share = share_of(back_ref[channels + late : channels + 2 * late], edge)
    guest = back_ref[:channels]
    for row in range(late):
        guest = guest + share[row : row + 1] * back_out_ref[row].astype(jnp.float32)
    out_ref[...] = velocity_ref[...] + velocity + centred(guest, 0.0, tile_tok)


def update_kernel(
    block_count, block_cols, tile_tok, half_size,
    step_ref, velocity_ref, partner_ref, latent_ref,
    guided_ref, clean_ref, next_ref,
):
    spot = Spot(block_count, block_cols)
    half = 2 * tile_tok
    is_cond = spot.index < half_size
    own = velocity_ref[...]
    other = partner_ref[...]
    cond = jnp.where(is_cond, own, other)
    uncond = jnp.where(is_cond, other, own)
    blended = uncond + GUIDANCE * (cond - uncond)
    left, right = blended[:, :half], blended[:, half:]
    first = lax.broadcasted_iota(jnp.int32, left.shape, 1) < tile_tok
    outside = jnp.where(first, left, right)
    inside = jnp.where(first, right, left)
    straight = spot.near == 0
    rolled = pltpu.roll(jnp.where(straight, inside, outside), tile_tok, 1)
    edge = jnp.where(straight, rolled, inside)
    rest = jnp.where(straight, outside, rolled)
    moment = jnp.full((1, half), step_ref[0].astype(jnp.float32))
    sigma_now = flow_sigma(moment)
    step_size = flow_sigma(moment + 1.0) - sigma_now
    for row in range(2):
        lanes = slice(row * half, (row + 1) * half)
        guided = jnp.where(spot.edge == row, edge, rest)
        latent = latent_ref[:, lanes]
        guided_ref[:, lanes] = guided
        clean_ref[:, lanes] = latent - sigma_now * guided
        next_ref[:, lanes] = latent + step_size * guided


def kernel_call(body, args, outs, smem=0, scratch=(), far=(), stay=True):
    spaces = [pltpu.SMEM] * smem + [pltpu.VMEM] * (len(args) - smem)
    for number in far:
        spaces[number] = pltpu.HBM
    args = [
        arg if space == pltpu.SMEM else pltpu.with_memory_space_constraint(arg, space)
        for arg, space in zip(args, spaces)
    ]
    specs = [pl.BlockSpec(memory_space=space) for space in spaces]
    return pl.pallas_call(
        body,
        out_shape=[
            pltpu.VMEM(shape, dtype) if stay else jax.ShapeDtypeStruct(shape, dtype)
            for shape, dtype in outs
        ],
        in_specs=specs,
        out_specs=[pl.BlockSpec(memory_space=pltpu.VMEM) for _ in outs],
        scratch_shapes=list(scratch),
        compiler_params=pltpu.CompilerParams(vmem_limit_bytes=VMEM_LIMIT),
    )(*args)


def one_frame_tile(frame_count):
    return frame_count == SH // 2 * (SW // 2) * 2 and SH == 4 and SW % 4 == 0


def per_device_plan(query_rows, key_rows, value_rows, tile_mask, head_weight, latent, step_index):
    frame_count = lax.axis_size("frame")
    half_size = frame_count // 2
    block_cols = SW // 2
    block_count = SH // 2 * block_cols
    tok_rows, width = query_rows.shape
    tile_tok = tok_rows // 4
    half = 2 * tile_tok
    channels = head_weight.shape[1]
    places = range(frame_count)
    row_pairs = [
        (f, f + block_cols if f % block_count < block_cols else f - block_cols)
        for f in places
    ]
    mate_pairs = [(f, f + 1 - 2 * (f % 2)) for f in places]
    side_pairs = []
    group_count = lax.axis_size("groups")
    for f in places:
        step = 2 * (f % 2) - 1
        inside = 0 <= f % block_cols + step < block_cols
        for g in range(group_count):
            if inside:
                side_pairs.append((g * frame_count + f, g * frame_count + f + step))
            else:
                other = (g + 1) % group_count
                side_pairs.append((g * frame_count + f, other * frame_count + f))
    branch_pairs = [(f, (f + half_size) % frame_count) for f in places]
    sizes = (block_count, block_cols, tile_tok)
    single = jnp.float32
    half_type = query_rows.dtype
    groups = (range(FIRST_HEADS), range(FIRST_HEADS, HEADS))
    every = (range(HEADS),)
    early, late = (len(group) for group in groups)

    weight_t = head_weight.T
    guest_send, edge_bias, far_keys, weight_t = kernel_call(
        functools.partial(guest_pack_kernel, *sizes),
        (query_rows, key_rows, tile_mask, weight_t),
        (
            ((half, early * HD), half_type),
            ((4, half), single),
            ((half, width), half_type),
            (weight_t.shape, half_type),
        ),
        0,
        (pltpu.SMEM(tile_mask.shape, tile_mask.dtype), pltpu.SemaphoreType.DMA((6,))),
        far=(0, 1, 2, 3),
    )

    def sent_over(value, pairs, axes="frame"):
        return lax.ppermute(value, axes, pairs)

    def column_type(group):
        return ((half, packed_width(len(group), channels)), half_type)

    guests = [sent_over(guest_send, row_pairs)]
    far = kernel_call(
        functools.partial(far_pack_kernel, *sizes, groups[0]),
        (far_keys, value_rows, weight_t, guest_send),
        (column_type(groups[0]),),
    )
    side_axes = ("groups", "frame")
    outer = [sent_over(far[0], side_pairs, side_axes)]
    near, guest_send, late_far = kernel_call(
        functools.partial(near_pack_kernel, *sizes, groups[1]),
        (query_rows, key_rows, value_rows, weight_t, far_keys),
        (column_type(every[0]), ((half, late * HD), half_type), column_type(groups[1])),
    )
    far = [*far, late_far]
    outer.append(sent_over(late_far, side_pairs, side_axes))
    inner = sent_over(near, mate_pairs)
    guest_bias = sent_over(edge_bias, row_pairs)
    guests.append(sent_over(guest_send, row_pairs))
    stats = ((HEADS, tok_rows), single)
    own_out, own_top, own_sum, side_bias = kernel_call(
        functools.partial(own_kernel, *sizes, groups),
        (tile_mask, query_rows, near, *far, inner),
        (((HEADS, channels, tok_rows), single), stats, stats, ((2, half), single)),
        1,
        (
            pltpu.VMEM((HEADS, tok_rows, tok_rows), single),
            pltpu.VMEM((HEADS, half, half), single),
            pltpu.VMEM((HEADS, tok_rows, tok_rows), half_type),
            pltpu.VMEM((HEADS, half, half), half_type),
        ),
    )

    def edge(number, guest_type):
        group = groups[number]
        heads = len(group)
        return kernel_call(
            functools.partial(edge_kernel, *sizes, group),
            (
                side_bias, guest_bias, query_rows, near, far[number], inner,
                outer[number], guests[number], own_top, own_sum,
            ),
            (
                ((heads, channels, half), single),
                ((heads, channels, half), guest_type),
                ((heads, half), single),
                ((heads, half), single),
                ((heads, tok_rows), single),
                ((2, heads, half), single),
            ),
            0,
            (
                pltpu.VMEM((heads, half, half), single),
                pltpu.VMEM((heads, tok_rows, half), single),
                pltpu.VMEM((heads, half, half), half_type),
                pltpu.VMEM((heads, tok_rows, half), half_type),
                pltpu.VMEM((heads, half), single),
                pltpu.VMEM((heads, half), single),
            ),
        )

    side_out, guest_out, side_top, guest_top, log, sent = edge(0, single)
    got = sent_over(sent, row_pairs)
    late_side, late_guest, late_side_top, late_guest_top, late_log, late_sent = edge(1, half_type)
    (guest_velocity,) = kernel_call(
        guest_blend_kernel,
        (guest_out, guest_top, sent, got, late_guest_top, late_sent),
        (((channels + 2 * late, half), single),),
    )
    back = sent_over(guest_velocity, row_pairs)
    back_out = sent_over(late_guest, row_pairs)
    velocity_type = ((channels, tok_rows), single)
    (velocity,) = kernel_call(
        functools.partial(own_blend_kernel, tile_tok, groups[0]),
        (own_out, side_out, own_top, side_top, log, got),
        (velocity_type,),
    )
    (velocity,) = kernel_call(
        functools.partial(join_kernel, tile_tok, groups[1]),
        (
            own_out, late_side, own_top, late_side_top, late_log, velocity,
            back, back_out,
        ),
        (velocity_type,),
    )
    partner = sent_over(velocity, branch_pairs)
    out = ((channels, tok_rows), single)
    results = kernel_call(
        functools.partial(update_kernel, *sizes, half_size),
        (step_index, velocity, partner, latent.T),
        (out, out, out),
        1,
        stay=False,
    )
    return tuple(result.T for result in results)


def per_device(*args):
    return per_device_plan(*args)


def solution(mesh):
    placed = (
        P(("groups", "frame"), None),
        P(("groups", "frame"), None),
        P(("groups", "frame"), None),
        P(("groups", "frame"), None),
        P(),
        P(("groups", "frame"), None),
        P("groups"),
    )
    fast = one_frame_tile(mesh.shape["frame"])
    return jax.shard_map(
        per_device if fast else per_device_frames,
        mesh=mesh,
        in_specs=placed,
        out_specs=(
            P(("groups", "frame"), None),
            P(("groups", "frame"), None),
            P(("groups", "frame"), None),
        ),
        check_vma=False,
    )
```

```python
import functools
import math

import jax
import jax.numpy as jnp
from jax import lax
from jax.experimental import pallas as pl
from jax.experimental.pallas import tpu as pltpu
from jax.sharding import PartitionSpec as P


HEADS = 20
HD = 128
SH = 4
SW = 8
SAMPLE_STEPS = 50


GUIDANCE = 5.0
FLOW_SHIFT = 5.0


def passed_along(value, axis, steps):
    count = lax.axis_size(axis)
    pairs = [(source, (source + steps) % count) for source in range(count)]
    return lax.ppermute(value, axis, pairs)


def flow_sigma(moment):
    remain = 1.0 - moment / SAMPLE_STEPS
    return FLOW_SHIFT * remain / (1.0 + (FLOW_SHIFT - 1.0) * remain)


def edge_range(offset):
    if offset < 0:
        return (1, 2)
    if offset > 0:
        return (0, 1)
    return (0, 2)


def direct_window(stacked, block_count, block_cols):
    received_parts = {}
    for frame_step in (1, 0, -1):
        for row_step in (1, 0, -1):
            for col_step in (1, 0, -1):
                distance = frame_step * block_count + row_step * block_cols + col_step
                row_start, row_stop = edge_range(row_step)
                col_start, col_stop = edge_range(col_step)
                outgoing = stacked[row_start:row_stop, col_start:col_stop]
                if frame_step == 0 and row_step == 0 and (col_step == 0):
                    received = outgoing
                elif row_step == 0 and col_step == 0:
                    received = passed_along(outgoing, "frame", -distance)
                elif row_step != 0 and col_step != 0:
                    received = passed_along(outgoing, "frame", -distance)
                else:
                    received = passed_along(outgoing, "frame", -distance)
                received_parts[frame_step, row_step, col_step] = received
    planes = []
    for frame_step in (-1, 0, 1):
        row_parts = []
        for row_step in (-1, 0, 1):
            col_parts = [received_parts[frame_step, row_step, col_step] for col_step in (-1, 0, 1)]
            row_parts.append(jnp.concatenate(col_parts, axis=1))
        planes.append(jnp.concatenate(row_parts, axis=0))
    return planes


def window_allowed(tile_mask, frame_tile, block_row, block_col, tile_frames):
    offsets = jnp.arange(27, dtype=jnp.int32)
    frame_step = offsets // 9 - 1
    row_step = offsets // 3 % 3 - 1
    col_step = offsets % 3 - 1
    local_tile = jnp.arange(4, dtype=jnp.int32)
    tile_row = 2 * block_row + local_tile // 2
    tile_col = 2 * block_col + local_tile % 2
    frame_there = frame_tile + frame_step
    row_there = tile_row[:, None] + row_step[None, :]
    col_there = tile_col[:, None] + col_step[None, :]
    usable = ((frame_there >= 0) & (frame_there < tile_frames))[None, :]
    usable = usable & (row_there >= 0) & (row_there < SH) & (col_there >= 0) & (col_there < SW)
    return usable & (tile_mask > 0)


def attend_window(query_rows, planes, allowed):
    tok_rows, inner_width = query_rows.shape
    tile_tok = tok_rows // 4
    query_tiles = query_rows.reshape(4, tile_tok, inner_width)
    mask_full = allowed[:, None, :, None]

    def one_head(head_number, result_rows):
        key_planes = [lax.dynamic_slice_in_dim(plane, head_number * HD, HD, 3) for plane in planes]
        value_planes = [
            lax.dynamic_slice_in_dim(plane, inner_width + head_number * HD, HD, 3)
            for plane in planes
        ]
        key_list = []
        value_list = []
        for row_local in range(2):
            for col_local in range(2):
                key_list.append(
                    jnp.stack(
                        [
                            part[row_local : row_local + 3, col_local : col_local + 3]
                            for part in key_planes
                        ]
                    ).reshape(27 * tile_tok, HD)
                )
                value_list.append(
                    jnp.stack(
                        [
                            part[row_local : row_local + 3, col_local : col_local + 3]
                            for part in value_planes
                        ]
                    ).reshape(27 * tile_tok, HD)
                )
        key_tiles = jnp.stack(key_list)
        value_tiles = jnp.stack(value_list)
        head_query = lax.dynamic_slice_in_dim(query_tiles, head_number * HD, HD, 2)
        scores = jnp.einsum(
            "qtd,qkd->qtk", head_query, key_tiles, preferred_element_type=jnp.float32
        ) / math.sqrt(HD)
        scores = scores.reshape(4, tile_tok, 27, tile_tok)
        scores = jnp.where(mask_full, scores, -1e30)
        row_max = jnp.max(scores, axis=(2, 3), keepdims=True)
        shifted = jnp.where(mask_full, jnp.exp(scores - row_max), 0.0)
        weights = (shifted / jnp.sum(shifted, axis=(2, 3), keepdims=True)).astype(jnp.bfloat16)
        weights = weights.reshape(4, tile_tok, 27 * tile_tok)
        head_out = jnp.einsum(
            "qtk,qkd->qtd", weights, value_tiles, preferred_element_type=jnp.float32
        ).astype(jnp.bfloat16)
        return lax.dynamic_update_slice_in_dim(result_rows, head_out, head_number * HD, 2)

    result_rows = lax.fori_loop(
        0, HEADS, one_head, jnp.zeros((4, tile_tok, inner_width), jnp.bfloat16)
    )
    return result_rows.reshape(tok_rows, inner_width)


def per_device_frames(query_rows, key_rows, value_rows, tile_mask, head_weight, latent, step_index):
    frame_count = lax.axis_size("frame")
    frame_index = lax.axis_index("frame")
    half_size = frame_count // 2
    block_cols = SW // 2
    block_count = SH // 2 * block_cols
    tile_frames = frame_count // (2 * block_count)
    frame_tile = frame_index // block_count % tile_frames
    block_spot = frame_index % block_count
    block_row = block_spot // block_cols
    block_col = block_spot % block_cols
    tok_rows, inner_width = query_rows.shape
    tile_tok = tok_rows // 4
    stacked = jnp.concatenate([key_rows, value_rows], axis=1).reshape(
        2, 2, tile_tok, 2 * inner_width
    )
    planes = direct_window(stacked, block_count, block_cols)
    allowed = window_allowed(tile_mask, frame_tile, block_row, block_col, tile_frames)
    attention = attend_window(query_rows, planes, allowed)
    velocity = jnp.dot(attention, head_weight, preferred_element_type=jnp.float32)
    partner_rows = passed_along(velocity, "frame", half_size)
    is_cond = frame_index < half_size
    cond_rows = jnp.where(is_cond, velocity, partner_rows)
    uncond_rows = jnp.where(is_cond, partner_rows, velocity)
    guided = uncond_rows + GUIDANCE * (cond_rows - uncond_rows)
    moment = step_index[0].astype(jnp.float32)
    sigma_now = flow_sigma(moment)
    step_size = flow_sigma(moment + 1.0) - sigma_now
    clean = latent - sigma_now * guided
    latent_next = latent + step_size * guided
    return (guided, clean, latent_next)


NEG = -1e30
VMEM_LIMIT = 16 << 20
FIRST_HEADS = 14
EXP_SCALE = math.log2(math.e) / math.sqrt(HD)


def contract_last(left, right):
    return lax.dot_general(
        left, right, (((1,), (1,)), ((), ())), preferred_element_type=jnp.float32
    )


def contract(left, right):
    return jnp.dot(left, right, preferred_element_type=jnp.float32)


def head_lanes(head):
    return slice(head * HD, (head + 1) * HD)


class Spot:
    def __init__(self, block_count, block_cols):
        self.index = lax.axis_index("frame")
        spot = self.index % block_count
        block_row = spot // block_cols
        block_col = spot % block_cols
        odd = block_col % 2
        self.edge = 1 - block_row
        self.rest = block_row
        self.near = 1 - odd
        self.far = odd
        self.near_step = 1 - 2 * odd
        self.far_step = 2 * odd - 1
        side = block_col + self.far_step
        self.there = (side >= 0) & (side < block_cols)
        self.guest_step = 2 * block_row - 1
        self.lane_tiles = (
            (self.rest, self.near),
            (self.edge, self.near),
            (self.edge, self.far),
            (self.rest, self.far),
        )
        self.key_tiles = (
            (self.edge, self.near),
            (self.rest, self.near),
            (self.rest, self.far),
            (self.edge, self.far),
        )


def tile_rows(tile, tile_tok):
    row, col = tile
    return pl.ds(pl.multiple_of((2 * row + col) * tile_tok, tile_tok), tile_tok)


def entry(row_step, col_step):
    return 9 + 3 * (row_step + 1) + col_step + 1


def bias_of(flag):
    return jnp.where(flag, jnp.float32(0.0), jnp.float32(NEG))


def key_bias(rows, tile_tok):
    biases = []
    for flags in rows:
        lanes = len(flags) * tile_tok
        lane = lax.broadcasted_iota(jnp.int32, (1, lanes), 1) // tile_tok
        bias = jnp.zeros((1, lanes), jnp.float32)
        for number, flag in enumerate(flags):
            bias = jnp.where(lane == number, bias_of(flag), bias)
        biases.append(bias)
    return biases


def biased(scores, biases, tile_tok):
    return above(
        *[scores[t * tile_tok : (t + 1) * tile_tok] + row for t, row in enumerate(biases)]
    )


def beside(left, right):
    return jnp.concatenate([left, right], axis=1)


def above(*parts):
    return jnp.concatenate(parts, axis=0)


def largest(scores):
    return jnp.max(scores, axis=0, keepdims=True)


def softened(scores, top):
    return jnp.exp2((scores - top) * EXP_SCALE).astype(jnp.bfloat16)


def with_ones(folded):
    return above(folded, jnp.ones((16, folded.shape[1]), folded.dtype))


def pipelined(heads, *stages):
    for turn in range(len(heads) + len(stages) - 1):
        for number, stage in enumerate(stages):
            if 0 <= turn - number < len(heads):
                stage(heads[turn - number])


def packed_width(heads, channels):
    return heads * HD + (heads + 1) // 2 * 2 * channels


class Column:
    def __init__(self, refs, groups, channels):
        self.refs = refs
        self.groups = groups
        self.channels = channels

    def place(self, head):
        for ref, group in zip(self.refs, self.groups):
            if head in group:
                return ref, head - group.start, len(group) * HD

    def keys(self, head):
        ref, local, _ = self.place(head)
        return ref[:, head_lanes(local)]

    def folded_at(self, head):
        ref, local, width = self.place(head)
        row = local % 2 * self.channels
        lane = width + local // 2 * 2 * self.channels
        return ref, (slice(row, row + self.channels), slice(lane, lane + 2 * self.channels))

    def folded(self, head):
        ref, where = self.folded_at(head)
        return ref[where]


def copied(pairs, sems):
    copies = [
        pltpu.make_async_copy(source, target, sems.at[number])
        for number, (source, target) in enumerate(pairs)
    ]
    for copy in copies:
        copy.start()
    return copies


def guest_pack_kernel(
    block_count, block_cols, tile_tok,
    query_ref, key_ref, mask_ref, weight_ref,
    guest_ref, bias_ref, far_key_ref, near_weight_ref, mask, sems,
):
    spot = Spot(block_count, block_cols)
    pairs = [(mask_ref, mask)]
    lanes = pl.ds(0, guest_ref.shape[1])
    for number, col in enumerate((spot.near, spot.far)):
        target = pl.ds(number * tile_tok, tile_tok)
        rows = tile_rows((spot.edge, col), tile_tok)
        pairs.append((query_ref.at[rows, lanes], guest_ref.at[target]))
    pairs.append((weight_ref, near_weight_ref))
    for number, tile in enumerate(spot.key_tiles[2:]):
        target = pl.ds(number * tile_tok, tile_tok)
        pairs.append((key_ref.at[tile_rows(tile, tile_tok)], far_key_ref.at[target]))
    copies = copied(pairs, sems)
    copies[0].wait()
    steps = -spot.guest_step

    def flag(col, col_step):
        return mask[2 * spot.edge + col, entry(steps, col_step)] > 0

    never = spot.near < 0
    cols = (spot.near, spot.far)
    rows = [[flag(col, key - col) for col in cols] for key in cols] + [
        [flag(spot.near, spot.near_step), never],
        [never, flag(spot.far, spot.far_step) & spot.there],
    ]
    for number, row in enumerate(key_bias(rows, tile_tok)):
        bias_ref[number : number + 1] = row
    for copy in copies[1:]:
        copy.wait()


def fold_into(column, value_ref, weight_ref, places):
    for head in (head for group in column.groups for head in group):
        lanes = head_lanes(head)
        values = above(*[value_ref[place, lanes] for place in places])
        folded = contract_last(weight_ref[:, lanes], values)
        ref, where = column.folded_at(head)
        ref[where] = folded.astype(jnp.bfloat16)


def far_pack_kernel(
    block_count, block_cols, tile_tok, group,
    key_ref, value_ref, weight_ref, guest_ref, far_ref,
):
    spot = Spot(block_count, block_cols)
    far_ref[:, : len(group) * HD] = key_ref[:, group.start * HD : group.stop * HD]
    places = [tile_rows(tile, tile_tok) for tile in spot.key_tiles[2:]]
    fold_into(Column([far_ref], (group,), weight_ref.shape[0]), value_ref, weight_ref, places)


def near_pack_kernel(
    block_count, block_cols, tile_tok, group,
    query_ref, key_ref, value_ref, weight_ref, far_key_ref, near_ref, guest_ref, far_ref,
):
    spot = Spot(block_count, block_cols)
    far_pack_kernel(
        block_count, block_cols, tile_tok, group,
        far_key_ref, value_ref, weight_ref, None, far_ref,
    )
    places = [tile_rows(tile, tile_tok) for tile in spot.key_tiles[:2]]
    for number, col in enumerate((spot.near, spot.far)):
        rows = slice(number * tile_tok, (number + 1) * tile_tok)
        near_ref[rows, : HEADS * HD] = key_ref[places[number], :]
        guest_ref[rows] = query_ref[
            tile_rows((spot.edge, col), tile_tok), group.start * HD : group.stop * HD
        ]
    column = Column([near_ref], (range(HEADS),), weight_ref.shape[0])
    fold_into(column, value_ref, weight_ref, places)


def own_kernel(
    block_count, block_cols, tile_tok, groups, mask_ref, query_ref, *refs
):
    count = len(groups)
    far_refs = refs[1 : 1 + count]
    out_ref, top_ref, sum_ref, side_bias_ref = refs[2 + count : 6 + count]
    own_scores, halo_scores, own_weights, halo_weights = refs[6 + count :]
    spot = Spot(block_count, block_cols)
    channels = out_ref.shape[1]
    half = 2 * tile_tok
    every = (range(HEADS),)
    near_column = Column(refs[:1], every, channels)
    far_column = Column(far_refs, groups, channels)
    inner_column = Column(refs[1 + count : 2 + count], every, channels)

    def flag(tile, row_step, col_step):
        return mask_ref[2 * tile[0] + tile[1], entry(row_step, col_step)] > 0

    bias = key_bias(
        [
            [flag(t, key[0] - t[0], key[1] - t[1]) for t in spot.lane_tiles]
            for key in spot.key_tiles
        ],
        tile_tok,
    )
    halo_bias = key_bias(
        [
            [flag(t, row - t[0], spot.near_step) for t in spot.lane_tiles[:2]]
            for row in (spot.edge, spot.rest)
        ],
        tile_tok,
    )
    side_rows = [
        [flag(t, row - t[0], spot.far_step) & spot.there for t in spot.lane_tiles[2:]]
        for row in (spot.rest, spot.edge)
    ]
    for number, row in enumerate(key_bias(side_rows, tile_tok)):
        side_bias_ref[number : number + 1] = row
    places = [tile_rows(tile, tile_tok) for tile in spot.lane_tiles]

    def score(head):
        lanes = head_lanes(head)
        query = above(*[query_ref[place, lanes] for place in places])
        keys = above(near_column.keys(head), far_column.keys(head))
        own = biased(contract_last(keys, query), bias, tile_tok)
        halo = biased(
            contract_last(inner_column.keys(head), query[:half]), halo_bias, tile_tok
        )
        own_scores[head] = own
        halo_scores[head] = halo
        top = largest(own)
        top_ref[head : head + 1, :half] = jnp.maximum(top[:, :half], largest(halo))
        top_ref[head : head + 1, half:] = top[:, half:]

    def soften(head):
        top = top_ref[head : head + 1]
        own_weights[head] = softened(own_scores[head], top)
        halo_weights[head] = softened(halo_scores[head], top[:, :half])

    def weigh(head):
        folded = with_ones(beside(near_column.folded(head), far_column.folded(head)))
        own = contract(folded, own_weights[head])
        halo = contract(with_ones(inner_column.folded(head)), halo_weights[head])
        left = own[:, :half] + halo
        out_ref[head, :, :half] = left[:channels]
        out_ref[head, :, half:] = own[:channels, half:]
        sum_ref[head : head + 1, :half] = left[channels : channels + 1]
        sum_ref[head : head + 1, half:] = own[channels : channels + 1, half:]

    pipelined(range(HEADS), score, soften, weigh)


def edge_kernel(
    block_count, block_cols, tile_tok, group, late,
    side_bias_ref, guest_bias_ref,
    query_ref, near_ref, far_ref, inner_ref, outer_ref, guest_ref, own_top_ref, own_sum_ref,
    out_ref, guest_out_ref, side_top_ref, guest_top_ref, log_ref, send_ref,
    side_scores, guest_scores, side_weights, guest_weights, side_sum_ref, guest_sum_ref,
):
    spot = Spot(block_count, block_cols)
    channels = out_ref.shape[1]
    half = 2 * tile_tok
    near_column = Column([near_ref], (range(HEADS),), channels)
    inner_column = Column([inner_ref], (range(HEADS),), channels)
    far_column = Column([far_ref], (group,), channels)
    outer_column = Column([outer_ref], (group,), channels)

    bias = [side_bias_ref[number : number + 1] for number in range(2)]
    guest_bias = [guest_bias_ref[number : number + 1] for number in range(4)]
    places = [tile_rows(tile, tile_tok) for tile in spot.lane_tiles[2:]]
    left = lax.broadcasted_iota(jnp.int32, (channels, half), 1) < tile_tok

    def score(head):
        row = head - group.start
        query = above(*[query_ref[place, head_lanes(head)] for place in places])
        scores = biased(contract_last(outer_column.keys(head), query), bias, tile_tok)
        side_scores[row] = scores
        side_top_ref[row : row + 1] = largest(scores)
        keys = above(
            near_column.keys(head)[:tile_tok],
            far_column.keys(head)[tile_tok:],
            inner_column.keys(head)[:tile_tok],
            outer_column.keys(head)[tile_tok:],
        )
        scores = contract_last(keys, guest_ref[:, head_lanes(row)])
        scores = biased(scores, guest_bias, tile_tok)
        guest_scores[row] = scores
        guest_top_ref[row : row + 1] = largest(scores)

    def soften(head):
        row = head - group.start
        side_weights[row] = softened(side_scores[row], side_top_ref[row : row + 1])
        guest_weights[row] = softened(guest_scores[row], guest_top_ref[row : row + 1])

    def weigh(head):
        row = head - group.start
        side = contract(with_ones(outer_column.folded(head)), side_weights[row])
        out_ref[row] = side[:channels]
        side_sum_ref[row : row + 1] = side[channels : channels + 1]
        folded = beside(
            jnp.where(left, near_column.folded(head), far_column.folded(head)),
            jnp.where(left, inner_column.folded(head), outer_column.folded(head)),
        )
        guest = contract(with_ones(folded), guest_weights[row])
        if late:
            share = guest[:channels] / guest[channels : channels + 1]
            place = slice(row * channels, (row + 1) * channels)
            guest_out_ref[place] = share.astype(guest_out_ref.dtype)
        else:
            guest_out_ref[row] = guest[:channels]
        guest_sum_ref[row : row + 1] = guest[channels : channels + 1]

    pipelined(group, score, soften, weigh)

    mine = slice(group.start, group.stop)
    near_log = log_sum(own_top_ref[mine, :half], own_sum_ref[mine, :half])
    far_log = joint(
        log_sum(own_top_ref[mine, half:], own_sum_ref[mine, half:]),
        log_sum(side_top_ref[...], side_sum_ref[...]),
    )
    log_ref[:, :half] = near_log
    log_ref[:, half:] = far_log
    send_ref[0] = beside(near_log[:, tile_tok:], far_log[:, :tile_tok])
    guest_log = log_sum(guest_top_ref[...], guest_sum_ref[...])
    send_ref[1] = guest_log
    if late:
        first = len(group) * channels
        guest_out_ref[first:] = jnp.zeros_like(guest_out_ref[first:])
        for number in range(3):
            part = guest_log.astype(guest_out_ref.dtype)
            start = first + 16 * number
            guest_out_ref[start : start + len(group)] = part
            guest_log = guest_log - part.astype(jnp.float32)


def log_sum(top, total):
    return top * EXP_SCALE + jnp.log2(total)


def joint(left, right):
    top = jnp.maximum(left, right)
    return top + jnp.log2(jnp.exp2(left - top) + jnp.exp2(right - top))


def share_of(top, whole):
    return jnp.exp2(top * EXP_SCALE - whole)


def centred(values, fill, tile_tok):
    side = jnp.full((values.shape[0], tile_tok), fill, values.dtype)
    return jnp.concatenate([side, values, side], axis=1)


def guest_blend_kernel(
    guest_out_ref, guest_top_ref, sent_ref, got_ref, late_ref, back_ref
):
    heads, _, _ = guest_out_ref.shape
    share = share_of(guest_top_ref[...], joint(sent_ref[1], got_ref[0]))
    velocity = jnp.zeros(guest_out_ref.shape[1:], jnp.float32)
    for row in range(heads):
        velocity = velocity + share[row : row + 1] * guest_out_ref[row]
    back_ref[...] = velocity.astype(back_ref.dtype)


def own_part(tile_tok, group, own_out_ref, side_out_ref, own_top_ref, side_top_ref, whole):
    half = 2 * tile_tok
    own_share = share_of(own_top_ref[group.start : group.stop], whole)
    side_share = share_of(side_top_ref[...], whole[:, half:])
    near = jnp.zeros((own_out_ref.shape[1], half), jnp.float32)
    far = jnp.zeros((own_out_ref.shape[1], half), jnp.float32)
    for row, head in enumerate(group):
        one = slice(row, row + 1)
        near = near + own_share[one, :half] * own_out_ref[head, :, :half]
        far = far + own_share[one, half:] * own_out_ref[head, :, half:]
        far = far + side_share[one] * side_out_ref[row]
    return beside(near, far)


def own_blend_kernel(
    tile_tok, group, own_out_ref, side_out_ref, own_top_ref, side_top_ref,
    log_ref, got_ref, velocity_ref,
):
    whole = joint(log_ref[...], centred(got_ref[1], NEG, tile_tok))
    velocity_ref[...] = own_part(
        tile_tok, group, own_out_ref, side_out_ref, own_top_ref, side_top_ref, whole
    )


def join_kernel(
    tile_tok, group, own_out_ref, side_out_ref, own_top_ref, side_top_ref,
    log_ref, velocity_ref, back_ref, back_out_ref, out_ref,
):
    channels = own_out_ref.shape[1]
    half = 2 * tile_tok
    late = len(group)
    first = late * channels
    guest_log = jnp.zeros((late, half), jnp.float32)
    for number in range(3):
        start = first + 16 * number
        guest_log = guest_log + back_out_ref[start : start + late].astype(jnp.float32)
    whole = joint(log_ref[...], centred(guest_log, NEG, tile_tok))
    velocity = own_part(
        tile_tok, group, own_out_ref, side_out_ref, own_top_ref, side_top_ref, whole
    )
    edge = beside(whole[:, tile_tok:half], whole[:, half : half + tile_tok])
    share = jnp.exp2(guest_log - edge)
    guest = back_ref[...].astype(jnp.float32)
    for row in range(late):
        guest = guest + share[row : row + 1] * back_out_ref[
            row * channels : (row + 1) * channels
        ].astype(jnp.float32)
    out_ref[...] = velocity_ref[...] + velocity + centred(guest, 0.0, tile_tok)


def update_kernel(
    block_count, block_cols, tile_tok, half_size,
    step_ref, velocity_ref, partner_ref, latent_ref,
    guided_ref, clean_ref, next_ref,
):
    spot = Spot(block_count, block_cols)
    half = 2 * tile_tok
    is_cond = spot.index < half_size
    own = velocity_ref[...]
    other = partner_ref[...]
    cond = jnp.where(is_cond, own, other)
    uncond = jnp.where(is_cond, other, own)
    blended = uncond + GUIDANCE * (cond - uncond)
    left, right = blended[:, :half], blended[:, half:]
    first = lax.broadcasted_iota(jnp.int32, left.shape, 1) < tile_tok
    outside = jnp.where(first, left, right)
    inside = jnp.where(first, right, left)
    straight = spot.near == 0
    rolled = pltpu.roll(jnp.where(straight, inside, outside), tile_tok, 1)
    edge = jnp.where(straight, rolled, inside)
    rest = jnp.where(straight, outside, rolled)
    moment = jnp.full((1, half), step_ref[0].astype(jnp.float32))
    sigma_now = flow_sigma(moment)
    step_size = flow_sigma(moment + 1.0) - sigma_now
    for row in range(2):
        lanes = slice(row * half, (row + 1) * half)
        guided = jnp.where(spot.edge == row, edge, rest)
        latent = latent_ref[:, lanes]
        guided_ref[:, lanes] = guided
        clean_ref[:, lanes] = latent - sigma_now * guided
        next_ref[:, lanes] = latent + step_size * guided


def kernel_call(body, args, outs, smem=0, scratch=(), far=(), stay=True):
    spaces = [pltpu.SMEM] * smem + [pltpu.VMEM] * (len(args) - smem)
    for number in far:
        spaces[number] = pltpu.HBM
    args = [
        arg if space == pltpu.SMEM else pltpu.with_memory_space_constraint(arg, space)
        for arg, space in zip(args, spaces)
    ]
    specs = [pl.BlockSpec(memory_space=space) for space in spaces]
    return pl.pallas_call(
        body,
        out_shape=[
            pltpu.VMEM(shape, dtype) if stay else jax.ShapeDtypeStruct(shape, dtype)
            for shape, dtype in outs
        ],
        in_specs=specs,
        out_specs=[pl.BlockSpec(memory_space=pltpu.VMEM) for _ in outs],
        scratch_shapes=list(scratch),
        compiler_params=pltpu.CompilerParams(vmem_limit_bytes=VMEM_LIMIT),
    )(*args)


def one_frame_tile(frame_count):
    return frame_count == SH // 2 * (SW // 2) * 2 and SH == 4 and SW % 4 == 0


def per_device_plan(query_rows, key_rows, value_rows, tile_mask, head_weight, latent, step_index):
    frame_count = lax.axis_size("frame")
    half_size = frame_count // 2
    block_cols = SW // 2
    block_count = SH // 2 * block_cols
    tok_rows, width = query_rows.shape
    tile_tok = tok_rows // 4
    half = 2 * tile_tok
    channels = head_weight.shape[1]
    places = range(frame_count)
    row_pairs = [
        (f, f + block_cols if f % block_count < block_cols else f - block_cols)
        for f in places
    ]
    mate_pairs = [(f, f + 1 - 2 * (f % 2)) for f in places]
    side_pairs = []
    group_count = lax.axis_size("groups")
    for f in places:
        step = 2 * (f % 2) - 1
        inside = 0 <= f % block_cols + step < block_cols
        for g in range(group_count):
            if inside:
                side_pairs.append((g * frame_count + f, g * frame_count + f + step))
            else:
                other = (g + 1) % group_count
                side_pairs.append((g * frame_count + f, other * frame_count + f))
    branch_pairs = [(f, (f + half_size) % frame_count) for f in places]
    sizes = (block_count, block_cols, tile_tok)
    single = jnp.float32
    half_type = query_rows.dtype
    groups = (range(FIRST_HEADS), range(FIRST_HEADS, HEADS))
    every = (range(HEADS),)
    early, late = (len(group) for group in groups)

    weight_t = head_weight.T
    guest_send, edge_bias, far_keys, weight_t = kernel_call(
        functools.partial(guest_pack_kernel, *sizes),
        (query_rows, key_rows, tile_mask, weight_t),
        (
            ((half, early * HD), half_type),
            ((4, half), single),
            ((half, width), half_type),
            (weight_t.shape, half_type),
        ),
        0,
        (pltpu.SMEM(tile_mask.shape, tile_mask.dtype), pltpu.SemaphoreType.DMA((6,))),
        far=(0, 1, 2, 3),
    )

    def sent_over(value, pairs, axes="frame"):
        return lax.ppermute(value, axes, pairs)

    def column_type(group):
        return ((half, packed_width(len(group), channels)), half_type)

    guests = [sent_over(guest_send, row_pairs)]
    far = kernel_call(
        functools.partial(far_pack_kernel, *sizes, groups[0]),
        (far_keys, value_rows, weight_t, guest_send),
        (column_type(groups[0]),),
    )
    side_axes = ("groups", "frame")
    outer = [sent_over(far[0], side_pairs, side_axes)]
    near, guest_send, late_far = kernel_call(
        functools.partial(near_pack_kernel, *sizes, groups[1]),
        (query_rows, key_rows, value_rows, weight_t, far_keys),
        (column_type(every[0]), ((half, late * HD), half_type), column_type(groups[1])),
    )
    far = [*far, late_far]
    outer.append(sent_over(late_far, side_pairs, side_axes))
    inner = sent_over(near, mate_pairs)
    guest_bias = sent_over(edge_bias, row_pairs)
    guests.append(sent_over(guest_send, row_pairs))
    stats = ((HEADS, tok_rows), single)
    own_out, own_top, own_sum, side_bias = kernel_call(
        functools.partial(own_kernel, *sizes, groups),
        (tile_mask, query_rows, near, *far, inner),
        (((HEADS, channels, tok_rows), single), stats, stats, ((2, half), single)),
        1,
        (
            pltpu.VMEM((HEADS, tok_rows, tok_rows), single),
            pltpu.VMEM((HEADS, half, half), single),
            pltpu.VMEM((HEADS, tok_rows, tok_rows), half_type),
            pltpu.VMEM((HEADS, half, half), half_type),
        ),
    )

    def edge(number, guest_type):
        group = groups[number]
        heads = len(group)
        return kernel_call(
            functools.partial(edge_kernel, *sizes, group, number > 0),
            (
                side_bias, guest_bias, query_rows, near, far[number], inner,
                outer[number], guests[number], own_top, own_sum,
            ),
            (
                ((heads, channels, half), single),
                (
                    (heads * channels + 48, half) if number else (heads, channels, half),
                    guest_type,
                ),
                ((heads, half), single),
                ((heads, half), single),
                ((heads, tok_rows), single),
                ((2, heads, half), single),
            ),
            0,
            (
                pltpu.VMEM((heads, half, half), single),
                pltpu.VMEM((heads, tok_rows, half), single),
                pltpu.VMEM((heads, half, half), half_type),
                pltpu.VMEM((heads, tok_rows, half), half_type),
                pltpu.VMEM((heads, half), single),
                pltpu.VMEM((heads, half), single),
            ),
        )

    side_out, guest_out, side_top, guest_top, log, sent = edge(0, single)
    got = sent_over(sent, row_pairs)
    late_side, late_guest, late_side_top, _, late_log, late_sent = edge(1, half_type)
    (guest_velocity,) = kernel_call(
        guest_blend_kernel,
        (guest_out, guest_top, sent, got, late_sent),
        (((channels, half), half_type),),
    )
    back = sent_over(guest_velocity, row_pairs)
    back_out = sent_over(late_guest, row_pairs)
    velocity_type = ((channels, tok_rows), single)
    (velocity,) = kernel_call(
        functools.partial(own_blend_kernel, tile_tok, groups[0]),
        (own_out, side_out, own_top, side_top, log, got),
        (velocity_type,),
    )
    (velocity,) = kernel_call(
        functools.partial(join_kernel, tile_tok, groups[1]),
        (
            own_out, late_side, own_top, late_side_top, late_log, velocity,
            back, back_out,
        ),
        (velocity_type,),
    )
    partner = sent_over(velocity, branch_pairs)
    out = ((channels, tok_rows), single)
    results = kernel_call(
        functools.partial(update_kernel, *sizes, half_size),
        (step_index, velocity, partner, latent.T),
        (out, out, out),
        1,
        stay=False,
    )
    return tuple(result.T for result in results)


def per_device(*args):
    return per_device_plan(*args)


def solution(mesh):
    placed = (
        P(("groups", "frame"), None),
        P(("groups", "frame"), None),
        P(("groups", "frame"), None),
        P(("groups", "frame"), None),
        P(),
        P(("groups", "frame"), None),
        P("groups"),
    )
    fast = one_frame_tile(mesh.shape["frame"])
    return jax.shard_map(
        per_device if fast else per_device_frames,
        mesh=mesh,
        in_specs=placed,
        out_specs=(
            P(("groups", "frame"), None),
            P(("groups", "frame"), None),
            P(("groups", "frame"), None),
        ),
        check_vma=False,
    )
```

```python
import functools
import math

import jax
import jax.numpy as jnp
from jax import lax
from jax.experimental import pallas as pl
from jax.experimental.pallas import tpu as pltpu
from jax.sharding import PartitionSpec as P


HEADS = 20
HD = 128
SH = 4
SW = 8
SAMPLE_STEPS = 50


GUIDANCE = 5.0
FLOW_SHIFT = 5.0


def passed_along(value, axis, steps):
    count = lax.axis_size(axis)
    pairs = [(source, (source + steps) % count) for source in range(count)]
    return lax.ppermute(value, axis, pairs)


def flow_sigma(moment):
    remain = 1.0 - moment / SAMPLE_STEPS
    return FLOW_SHIFT * remain / (1.0 + (FLOW_SHIFT - 1.0) * remain)


def edge_range(offset):
    if offset < 0:
        return (1, 2)
    if offset > 0:
        return (0, 1)
    return (0, 2)


def direct_window(stacked, block_count, block_cols):
    received_parts = {}
    for frame_step in (1, 0, -1):
        for row_step in (1, 0, -1):
            for col_step in (1, 0, -1):
                distance = frame_step * block_count + row_step * block_cols + col_step
                row_start, row_stop = edge_range(row_step)
                col_start, col_stop = edge_range(col_step)
                outgoing = stacked[row_start:row_stop, col_start:col_stop]
                if frame_step == 0 and row_step == 0 and (col_step == 0):
                    received = outgoing
                elif row_step == 0 and col_step == 0:
                    received = passed_along(outgoing, "frame", -distance)
                elif row_step != 0 and col_step != 0:
                    received = passed_along(outgoing, "frame", -distance)
                else:
                    received = passed_along(outgoing, "frame", -distance)
                received_parts[frame_step, row_step, col_step] = received
    planes = []
    for frame_step in (-1, 0, 1):
        row_parts = []
        for row_step in (-1, 0, 1):
            col_parts = [received_parts[frame_step, row_step, col_step] for col_step in (-1, 0, 1)]
            row_parts.append(jnp.concatenate(col_parts, axis=1))
        planes.append(jnp.concatenate(row_parts, axis=0))
    return planes


def window_allowed(tile_mask, frame_tile, block_row, block_col, tile_frames):
    offsets = jnp.arange(27, dtype=jnp.int32)
    frame_step = offsets // 9 - 1
    row_step = offsets // 3 % 3 - 1
    col_step = offsets % 3 - 1
    local_tile = jnp.arange(4, dtype=jnp.int32)
    tile_row = 2 * block_row + local_tile // 2
    tile_col = 2 * block_col + local_tile % 2
    frame_there = frame_tile + frame_step
    row_there = tile_row[:, None] + row_step[None, :]
    col_there = tile_col[:, None] + col_step[None, :]
    usable = ((frame_there >= 0) & (frame_there < tile_frames))[None, :]
    usable = usable & (row_there >= 0) & (row_there < SH) & (col_there >= 0) & (col_there < SW)
    return usable & (tile_mask > 0)


def attend_window(query_rows, planes, allowed):
    tok_rows, inner_width = query_rows.shape
    tile_tok = tok_rows // 4
    query_tiles = query_rows.reshape(4, tile_tok, inner_width)
    mask_full = allowed[:, None, :, None]

    def one_head(head_number, result_rows):
        key_planes = [lax.dynamic_slice_in_dim(plane, head_number * HD, HD, 3) for plane in planes]
        value_planes = [
            lax.dynamic_slice_in_dim(plane, inner_width + head_number * HD, HD, 3)
            for plane in planes
        ]
        key_list = []
        value_list = []
        for row_local in range(2):
            for col_local in range(2):
                key_list.append(
                    jnp.stack(
                        [
                            part[row_local : row_local + 3, col_local : col_local + 3]
                            for part in key_planes
                        ]
                    ).reshape(27 * tile_tok, HD)
                )
                value_list.append(
                    jnp.stack(
                        [
                            part[row_local : row_local + 3, col_local : col_local + 3]
                            for part in value_planes
                        ]
                    ).reshape(27 * tile_tok, HD)
                )
        key_tiles = jnp.stack(key_list)
        value_tiles = jnp.stack(value_list)
        head_query = lax.dynamic_slice_in_dim(query_tiles, head_number * HD, HD, 2)
        scores = jnp.einsum(
            "qtd,qkd->qtk", head_query, key_tiles, preferred_element_type=jnp.float32
        ) / math.sqrt(HD)
        scores = scores.reshape(4, tile_tok, 27, tile_tok)
        scores = jnp.where(mask_full, scores, -1e30)
        row_max = jnp.max(scores, axis=(2, 3), keepdims=True)
        shifted = jnp.where(mask_full, jnp.exp(scores - row_max), 0.0)
        weights = (shifted / jnp.sum(shifted, axis=(2, 3), keepdims=True)).astype(jnp.bfloat16)
        weights = weights.reshape(4, tile_tok, 27 * tile_tok)
        head_out = jnp.einsum(
            "qtk,qkd->qtd", weights, value_tiles, preferred_element_type=jnp.float32
        ).astype(jnp.bfloat16)
        return lax.dynamic_update_slice_in_dim(result_rows, head_out, head_number * HD, 2)

    result_rows = lax.fori_loop(
        0, HEADS, one_head, jnp.zeros((4, tile_tok, inner_width), jnp.bfloat16)
    )
    return result_rows.reshape(tok_rows, inner_width)


def per_device_frames(query_rows, key_rows, value_rows, tile_mask, head_weight, latent, step_index):
    frame_count = lax.axis_size("frame")
    frame_index = lax.axis_index("frame")
    half_size = frame_count // 2
    block_cols = SW // 2
    block_count = SH // 2 * block_cols
    tile_frames = frame_count // (2 * block_count)
    frame_tile = frame_index // block_count % tile_frames
    block_spot = frame_index % block_count
    block_row = block_spot // block_cols
    block_col = block_spot % block_cols
    tok_rows, inner_width = query_rows.shape
    tile_tok = tok_rows // 4
    stacked = jnp.concatenate([key_rows, value_rows], axis=1).reshape(
        2, 2, tile_tok, 2 * inner_width
    )
    planes = direct_window(stacked, block_count, block_cols)
    allowed = window_allowed(tile_mask, frame_tile, block_row, block_col, tile_frames)
    attention = attend_window(query_rows, planes, allowed)
    velocity = jnp.dot(attention, head_weight, preferred_element_type=jnp.float32)
    partner_rows = passed_along(velocity, "frame", half_size)
    is_cond = frame_index < half_size
    cond_rows = jnp.where(is_cond, velocity, partner_rows)
    uncond_rows = jnp.where(is_cond, partner_rows, velocity)
    guided = uncond_rows + GUIDANCE * (cond_rows - uncond_rows)
    moment = step_index[0].astype(jnp.float32)
    sigma_now = flow_sigma(moment)
    step_size = flow_sigma(moment + 1.0) - sigma_now
    clean = latent - sigma_now * guided
    latent_next = latent + step_size * guided
    return (guided, clean, latent_next)


NEG = -1e30
VMEM_LIMIT = 16 << 20
FIRST_HEADS = 14
EXP_SCALE = math.log2(math.e) / math.sqrt(HD)


def contract_last(left, right):
    return lax.dot_general(
        left, right, (((1,), (1,)), ((), ())), preferred_element_type=jnp.float32
    )


def contract(left, right):
    return jnp.dot(left, right, preferred_element_type=jnp.float32)


def head_lanes(head):
    return slice(head * HD, (head + 1) * HD)


class Spot:
    def __init__(self, block_count, block_cols):
        self.index = lax.axis_index("frame")
        spot = self.index % block_count
        block_row = spot // block_cols
        block_col = spot % block_cols
        odd = block_col % 2
        self.edge = 1 - block_row
        self.rest = block_row
        self.near = 1 - odd
        self.far = odd
        self.near_step = 1 - 2 * odd
        self.far_step = 2 * odd - 1
        side = block_col + self.far_step
        self.there = (side >= 0) & (side < block_cols)
        self.guest_step = 2 * block_row - 1
        self.lane_tiles = (
            (self.rest, self.near),
            (self.edge, self.near),
            (self.edge, self.far),
            (self.rest, self.far),
        )
        self.key_tiles = (
            (self.edge, self.near),
            (self.rest, self.near),
            (self.rest, self.far),
            (self.edge, self.far),
        )


def tile_rows(tile, tile_tok):
    row, col = tile
    return pl.ds(pl.multiple_of((2 * row + col) * tile_tok, tile_tok), tile_tok)


def entry(row_step, col_step):
    return 9 + 3 * (row_step + 1) + col_step + 1


def bias_of(flag):
    return jnp.where(flag, jnp.float32(0.0), jnp.float32(NEG))


def key_bias(rows, tile_tok):
    biases = []
    for flags in rows:
        lanes = len(flags) * tile_tok
        lane = lax.broadcasted_iota(jnp.int32, (1, lanes), 1) // tile_tok
        bias = jnp.zeros((1, lanes), jnp.float32)
        for number, flag in enumerate(flags):
            bias = jnp.where(lane == number, bias_of(flag), bias)
        biases.append(bias)
    return biases


def biased(scores, biases, tile_tok):
    return above(
        *[scores[t * tile_tok : (t + 1) * tile_tok] + row for t, row in enumerate(biases)]
    )


def beside(left, right):
    return jnp.concatenate([left, right], axis=1)


def above(*parts):
    return jnp.concatenate(parts, axis=0)


def largest(scores):
    return jnp.max(scores, axis=0, keepdims=True)


def softened(scores, top):
    return jnp.exp2((scores - top) * EXP_SCALE).astype(jnp.bfloat16)


def with_ones(folded):
    return above(folded, jnp.ones((16, folded.shape[1]), folded.dtype))


def pipelined(heads, *stages):
    for turn in range(len(heads) + len(stages) - 1):
        for number, stage in enumerate(stages):
            if 0 <= turn - number < len(heads):
                stage(heads[turn - number])


def packed_width(heads, channels):
    return heads * HD + (heads + 1) // 2 * 2 * channels


class Column:
    def __init__(self, refs, groups, channels):
        self.refs = refs
        self.groups = groups
        self.channels = channels

    def place(self, head):
        for ref, group in zip(self.refs, self.groups):
            if head in group:
                return ref, head - group.start, len(group) * HD

    def keys(self, head):
        ref, local, _ = self.place(head)
        return ref[:, head_lanes(local)]

    def folded_at(self, head):
        ref, local, width = self.place(head)
        row = local % 2 * self.channels
        lane = width + local // 2 * 2 * self.channels
        return ref, (slice(row, row + self.channels), slice(lane, lane + 2 * self.channels))

    def folded(self, head):
        ref, where = self.folded_at(head)
        return ref[where]


def copied(pairs, sems):
    copies = [
        pltpu.make_async_copy(source, target, sems.at[number])
        for number, (source, target) in enumerate(pairs)
    ]
    for copy in copies:
        copy.start()
    return copies


def guest_pack_kernel(
    block_count, block_cols, tile_tok,
    query_ref, key_ref, mask_ref, weight_ref,
    guest_ref, bias_ref, far_key_ref, near_weight_ref, mask, sems,
):
    spot = Spot(block_count, block_cols)
    pairs = [(mask_ref, mask)]
    lanes = pl.ds(0, guest_ref.shape[1])
    for number, col in enumerate((spot.near, spot.far)):
        target = pl.ds(number * tile_tok, tile_tok)
        rows = tile_rows((spot.edge, col), tile_tok)
        pairs.append((query_ref.at[rows, lanes], guest_ref.at[target]))
    pairs.append((weight_ref, near_weight_ref))
    for number, tile in enumerate(spot.key_tiles[2:]):
        target = pl.ds(number * tile_tok, tile_tok)
        pairs.append((key_ref.at[tile_rows(tile, tile_tok)], far_key_ref.at[target]))
    copies = copied(pairs, sems)
    copies[0].wait()
    steps = -spot.guest_step

    def flag(col, col_step):
        return mask[2 * spot.edge + col, entry(steps, col_step)] > 0

    never = spot.near < 0
    cols = (spot.near, spot.far)
    rows = [[flag(col, key - col) for col in cols] for key in cols] + [
        [flag(spot.near, spot.near_step), never],
        [never, flag(spot.far, spot.far_step) & spot.there],
    ]
    for number, row in enumerate(key_bias(rows, tile_tok)):
        bias_ref[number : number + 1] = row
    for copy in copies[1:]:
        copy.wait()


def fold_into(column, value_ref, weight_ref, places):
    for head in (head for group in column.groups for head in group):
        lanes = head_lanes(head)
        values = above(*[value_ref[place, lanes] for place in places])
        folded = contract_last(weight_ref[:, lanes], values)
        ref, where = column.folded_at(head)
        ref[where] = folded.astype(jnp.bfloat16)


def far_pack_kernel(
    block_count, block_cols, tile_tok, group,
    key_ref, value_ref, weight_ref, guest_ref, far_ref,
):
    spot = Spot(block_count, block_cols)
    far_ref[:, : len(group) * HD] = key_ref[:, group.start * HD : group.stop * HD]
    places = [tile_rows(tile, tile_tok) for tile in spot.key_tiles[2:]]
    fold_into(Column([far_ref], (group,), weight_ref.shape[0]), value_ref, weight_ref, places)


def near_pack_kernel(
    block_count, block_cols, tile_tok, group,
    query_ref, key_ref, value_ref, weight_ref, far_key_ref, near_ref, guest_ref, far_ref,
):
    spot = Spot(block_count, block_cols)
    far_pack_kernel(
        block_count, block_cols, tile_tok, group,
        far_key_ref, value_ref, weight_ref, None, far_ref,
    )
    places = [tile_rows(tile, tile_tok) for tile in spot.key_tiles[:2]]
    for number, col in enumerate((spot.near, spot.far)):
        rows = slice(number * tile_tok, (number + 1) * tile_tok)
        near_ref[rows, : HEADS * HD] = key_ref[places[number], :]
        guest_ref[rows] = query_ref[
            tile_rows((spot.edge, col), tile_tok), group.start * HD : group.stop * HD
        ]
    column = Column([near_ref], (range(HEADS),), weight_ref.shape[0])
    fold_into(column, value_ref, weight_ref, places)


def own_kernel(
    block_count, block_cols, tile_tok, groups, mask_ref, query_ref, *refs
):
    count = len(groups)
    far_refs = refs[1 : 1 + count]
    out_ref, top_ref, sum_ref, side_bias_ref = refs[2 + count : 6 + count]
    own_scores, halo_scores, own_weights, halo_weights = refs[6 + count :]
    spot = Spot(block_count, block_cols)
    channels = out_ref.shape[1]
    half = 2 * tile_tok
    every = (range(HEADS),)
    near_column = Column(refs[:1], every, channels)
    far_column = Column(far_refs, groups, channels)
    inner_column = Column(refs[1 + count : 2 + count], every, channels)

    def flag(tile, row_step, col_step):
        return mask_ref[2 * tile[0] + tile[1], entry(row_step, col_step)] > 0

    bias = key_bias(
        [
            [flag(t, key[0] - t[0], key[1] - t[1]) for t in spot.lane_tiles]
            for key in spot.key_tiles
        ],
        tile_tok,
    )
    halo_bias = key_bias(
        [
            [flag(t, row - t[0], spot.near_step) for t in spot.lane_tiles[:2]]
            for row in (spot.edge, spot.rest)
        ],
        tile_tok,
    )
    side_rows = [
        [flag(t, row - t[0], spot.far_step) & spot.there for t in spot.lane_tiles[2:]]
        for row in (spot.rest, spot.edge)
    ]
    for number, row in enumerate(key_bias(side_rows, tile_tok)):
        side_bias_ref[number : number + 1] = row
    places = [tile_rows(tile, tile_tok) for tile in spot.lane_tiles]

    def score(head):
        lanes = head_lanes(head)
        query = above(*[query_ref[place, lanes] for place in places])
        keys = above(near_column.keys(head), far_column.keys(head))
        own = biased(contract_last(keys, query), bias, tile_tok)
        halo = biased(
            contract_last(inner_column.keys(head), query[:half]), halo_bias, tile_tok
        )
        own_scores[head] = own
        halo_scores[head] = halo
        top = largest(own)
        top_ref[head : head + 1, :half] = jnp.maximum(top[:, :half], largest(halo))
        top_ref[head : head + 1, half:] = top[:, half:]

    def soften(head):
        top = top_ref[head : head + 1]
        own_weights[head] = softened(own_scores[head], top)
        halo_weights[head] = softened(halo_scores[head], top[:, :half])

    def weigh(head):
        folded = with_ones(beside(near_column.folded(head), far_column.folded(head)))
        own = contract(folded, own_weights[head])
        halo = contract(with_ones(inner_column.folded(head)), halo_weights[head])
        left = own[:, :half] + halo
        out_ref[head, :, :half] = left[:channels]
        out_ref[head, :, half:] = own[:channels, half:]
        sum_ref[head : head + 1, :half] = left[channels : channels + 1]
        sum_ref[head : head + 1, half:] = own[channels : channels + 1, half:]

    pipelined(range(HEADS), score, soften, weigh)


def edge_kernel(
    block_count, block_cols, tile_tok, group,
    side_bias_ref, guest_bias_ref,
    query_ref, near_ref, far_ref, inner_ref, outer_ref, guest_ref, own_top_ref, own_sum_ref,
    out_ref, guest_out_ref, side_top_ref, guest_top_ref, log_ref, send_ref,
    side_scores, guest_scores, side_weights, guest_weights, side_sum_ref, guest_sum_ref,
):
    spot = Spot(block_count, block_cols)
    channels = out_ref.shape[1]
    half = 2 * tile_tok
    near_column = Column([near_ref], (range(HEADS),), channels)
    inner_column = Column([inner_ref], (range(HEADS),), channels)
    far_column = Column([far_ref], (group,), channels)
    outer_column = Column([outer_ref], (group,), channels)

    bias = [side_bias_ref[number : number + 1] for number in range(2)]
    guest_bias = [guest_bias_ref[number : number + 1] for number in range(4)]
    places = [tile_rows(tile, tile_tok) for tile in spot.lane_tiles[2:]]
    left = lax.broadcasted_iota(jnp.int32, (channels, half), 1) < tile_tok

    def score(head):
        row = head - group.start
        query = above(*[query_ref[place, head_lanes(head)] for place in places])
        scores = biased(contract_last(outer_column.keys(head), query), bias, tile_tok)
        side_scores[row] = scores
        side_top_ref[row : row + 1] = largest(scores)
        keys = above(
            near_column.keys(head)[:tile_tok],
            far_column.keys(head)[tile_tok:],
            inner_column.keys(head)[:tile_tok],
            outer_column.keys(head)[tile_tok:],
        )
        scores = contract_last(keys, guest_ref[:, head_lanes(row)])
        scores = biased(scores, guest_bias, tile_tok)
        guest_scores[row] = scores
        guest_top_ref[row : row + 1] = largest(scores)

    def soften(head):
        row = head - group.start
        side_weights[row] = softened(side_scores[row], side_top_ref[row : row + 1])
        guest_weights[row] = softened(guest_scores[row], guest_top_ref[row : row + 1])

    def weigh(head):
        row = head - group.start
        side = contract(with_ones(outer_column.folded(head)), side_weights[row])
        out_ref[row] = side[:channels]
        side_sum_ref[row : row + 1] = side[channels : channels + 1]
        folded = beside(
            jnp.where(left, near_column.folded(head), far_column.folded(head)),
            jnp.where(left, inner_column.folded(head), outer_column.folded(head)),
        )
        guest = contract(with_ones(folded), guest_weights[row])
        guest_out_ref[row] = guest[:channels].astype(guest_out_ref.dtype)
        guest_sum_ref[row : row + 1] = guest[channels : channels + 1]

    pipelined(group, score, soften, weigh)

    mine = slice(group.start, group.stop)
    near_log = log_sum(own_top_ref[mine, :half], own_sum_ref[mine, :half])
    far_log = joint(
        log_sum(own_top_ref[mine, half:], own_sum_ref[mine, half:]),
        log_sum(side_top_ref[...], side_sum_ref[...]),
    )
    log_ref[:, :half] = near_log
    log_ref[:, half:] = far_log
    send_ref[0] = beside(near_log[:, tile_tok:], far_log[:, :tile_tok])
    send_ref[1] = log_sum(guest_top_ref[...], guest_sum_ref[...])


def log_sum(top, total):
    return top * EXP_SCALE + jnp.log2(total)


def joint(left, right):
    top = jnp.maximum(left, right)
    return top + jnp.log2(jnp.exp2(left - top) + jnp.exp2(right - top))


def share_of(top, whole):
    return jnp.exp2(top * EXP_SCALE - whole)


def centred(values, fill, tile_tok):
    side = jnp.full((values.shape[0], tile_tok), fill, values.dtype)
    return jnp.concatenate([side, values, side], axis=1)


def guest_blend_kernel(
    guest_out_ref, guest_top_ref, sent_ref, got_ref, late_top_ref, late_sent_ref, back_ref
):
    heads, channels, _ = guest_out_ref.shape
    share = share_of(guest_top_ref[...], joint(sent_ref[1], got_ref[0]))
    velocity = jnp.zeros(guest_out_ref.shape[1:], jnp.float32)
    for row in range(heads):
        velocity = velocity + share[row : row + 1] * guest_out_ref[row]
    late = late_top_ref.shape[0]
    back_ref[:channels] = velocity
    back_ref[channels : channels + late] = late_sent_ref[1]
    back_ref[channels + late : channels + 2 * late] = late_top_ref[...]


def own_part(tile_tok, group, own_out_ref, side_out_ref, own_top_ref, side_top_ref, whole):
    half = 2 * tile_tok
    own_share = share_of(own_top_ref[group.start : group.stop], whole)
    side_share = share_of(side_top_ref[...], whole[:, half:])
    near = jnp.zeros((own_out_ref.shape[1], half), jnp.float32)
    far = jnp.zeros((own_out_ref.shape[1], half), jnp.float32)
    for row, head in enumerate(group):
        one = slice(row, row + 1)
        near = near + own_share[one, :half] * own_out_ref[head, :, :half]
        far = far + own_share[one, half:] * own_out_ref[head, :, half:]
        far = far + side_share[one] * side_out_ref[row]
    return beside(near, far)


def own_blend_kernel(
    tile_tok, group, own_out_ref, side_out_ref, own_top_ref, side_top_ref,
    log_ref, got_ref, velocity_ref,
):
    whole = joint(log_ref[...], centred(got_ref[1], NEG, tile_tok))
    velocity_ref[...] = own_part(
        tile_tok, group, own_out_ref, side_out_ref, own_top_ref, side_top_ref, whole
    )


def join_kernel(
    tile_tok, group, own_out_ref, side_out_ref, own_top_ref, side_top_ref,
    log_ref, velocity_ref, back_ref, back_out_ref, out_ref,
):
    channels = own_out_ref.shape[1]
    half = 2 * tile_tok
    late = len(group)
    guest_log = back_ref[channels : channels + late]
    whole = joint(log_ref[...], centred(guest_log, NEG, tile_tok))
    velocity = own_part(
        tile_tok, group, own_out_ref, side_out_ref, own_top_ref, side_top_ref, whole
    )
    edge = beside(whole[:, tile_tok:half], whole[:, half : half + tile_tok])
    share = share_of(back_ref[channels + late : channels + 2 * late], edge)
    guest = back_ref[:channels]
    for row in range(late):
        guest = guest + share[row : row + 1] * back_out_ref[row].astype(jnp.float32)
    first = lax.broadcasted_iota(jnp.int32, guest.shape, 1) < tile_tok
    rolled = pltpu.roll(guest, tile_tok, 1)
    out_ref[:, :half] = (
        velocity_ref[:, :half] + velocity[:, :half] + jnp.where(first, 0.0, rolled)
    )
    out_ref[:, half:] = (
        velocity_ref[:, half:] + velocity[:, half:] + jnp.where(first, rolled, 0.0)
    )


def update_kernel(
    block_count, block_cols, tile_tok, half_size,
    step_ref, velocity_ref, partner_ref, latent_ref,
    guided_ref, clean_ref, next_ref,
):
    spot = Spot(block_count, block_cols)
    half = 2 * tile_tok
    is_cond = spot.index < half_size
    own = velocity_ref[...]
    other = partner_ref[...]
    cond = jnp.where(is_cond, own, other)
    uncond = jnp.where(is_cond, other, own)
    blended = uncond + GUIDANCE * (cond - uncond)
    left, right = blended[:, :half], blended[:, half:]
    first = lax.broadcasted_iota(jnp.int32, left.shape, 1) < tile_tok
    outside = jnp.where(first, left, right)
    inside = jnp.where(first, right, left)
    straight = spot.near == 0
    rolled = pltpu.roll(jnp.where(straight, inside, outside), tile_tok, 1)
    edge = jnp.where(straight, rolled, inside)
    rest = jnp.where(straight, outside, rolled)
    moment = jnp.full((1, half), step_ref[0].astype(jnp.float32))
    sigma_now = flow_sigma(moment)
    step_size = flow_sigma(moment + 1.0) - sigma_now
    for row in range(2):
        lanes = slice(row * half, (row + 1) * half)
        guided = jnp.where(spot.edge == row, edge, rest)
        latent = latent_ref[:, lanes]
        guided_ref[:, lanes] = guided
        clean_ref[:, lanes] = latent - sigma_now * guided
        next_ref[:, lanes] = latent + step_size * guided


def kernel_call(body, args, outs, smem=0, scratch=(), far=(), stay=True):
    spaces = [pltpu.SMEM] * smem + [pltpu.VMEM] * (len(args) - smem)
    for number in far:
        spaces[number] = pltpu.HBM
    args = [
        arg if space == pltpu.SMEM else pltpu.with_memory_space_constraint(arg, space)
        for arg, space in zip(args, spaces)
    ]
    specs = [pl.BlockSpec(memory_space=space) for space in spaces]
    return pl.pallas_call(
        body,
        out_shape=[
            pltpu.VMEM(shape, dtype) if stay else jax.ShapeDtypeStruct(shape, dtype)
            for shape, dtype in outs
        ],
        in_specs=specs,
        out_specs=[pl.BlockSpec(memory_space=pltpu.VMEM) for _ in outs],
        scratch_shapes=list(scratch),
        compiler_params=pltpu.CompilerParams(vmem_limit_bytes=VMEM_LIMIT),
    )(*args)


def one_frame_tile(frame_count):
    return frame_count == SH // 2 * (SW // 2) * 2 and SH == 4 and SW % 4 == 0


def per_device_plan(query_rows, key_rows, value_rows, tile_mask, head_weight, latent, step_index):
    frame_count = lax.axis_size("frame")
    half_size = frame_count // 2
    block_cols = SW // 2
    block_count = SH // 2 * block_cols
    tok_rows, width = query_rows.shape
    tile_tok = tok_rows // 4
    half = 2 * tile_tok
    channels = head_weight.shape[1]
    places = range(frame_count)
    row_pairs = [
        (f, f + block_cols if f % block_count < block_cols else f - block_cols)
        for f in places
    ]
    mate_pairs = [(f, f + 1 - 2 * (f % 2)) for f in places]
    side_pairs = []
    group_count = lax.axis_size("groups")
    for f in places:
        step = 2 * (f % 2) - 1
        inside = 0 <= f % block_cols + step < block_cols
        for g in range(group_count):
            if inside:
                side_pairs.append((g * frame_count + f, g * frame_count + f + step))
            else:
                other = (g + 1) % group_count
                side_pairs.append((g * frame_count + f, other * frame_count + f))
    branch_pairs = [(f, (f + half_size) % frame_count) for f in places]
    sizes = (block_count, block_cols, tile_tok)
    single = jnp.float32
    half_type = query_rows.dtype
    groups = (range(FIRST_HEADS), range(FIRST_HEADS, HEADS))
    every = (range(HEADS),)
    early, late = (len(group) for group in groups)

    weight_t = head_weight.T
    guest_send, edge_bias, far_keys, weight_t = kernel_call(
        functools.partial(guest_pack_kernel, *sizes),
        (query_rows, key_rows, tile_mask, weight_t),
        (
            ((half, early * HD), half_type),
            ((4, half), single),
            ((half, width), half_type),
            (weight_t.shape, half_type),
        ),
        0,
        (pltpu.SMEM(tile_mask.shape, tile_mask.dtype), pltpu.SemaphoreType.DMA((6,))),
        far=(0, 1, 2, 3),
    )

    def sent_over(value, pairs, axes="frame"):
        return lax.ppermute(value, axes, pairs)

    def column_type(group):
        return ((half, packed_width(len(group), channels)), half_type)

    guests = [sent_over(guest_send, row_pairs)]
    far = kernel_call(
        functools.partial(far_pack_kernel, *sizes, groups[0]),
        (far_keys, value_rows, weight_t, guest_send),
        (column_type(groups[0]),),
    )
    side_axes = ("groups", "frame")
    outer = [sent_over(far[0], side_pairs, side_axes)]
    near, guest_send, late_far = kernel_call(
        functools.partial(near_pack_kernel, *sizes, groups[1]),
        (query_rows, key_rows, value_rows, weight_t, far_keys),
        (column_type(every[0]), ((half, late * HD), half_type), column_type(groups[1])),
    )
    far = [*far, late_far]
    outer.append(sent_over(late_far, side_pairs, side_axes))
    inner = sent_over(near, mate_pairs)
    guest_bias = sent_over(edge_bias, row_pairs)
    guests.append(sent_over(guest_send, row_pairs))
    stats = ((HEADS, tok_rows), single)
    own_out, own_top, own_sum, side_bias = kernel_call(
        functools.partial(own_kernel, *sizes, groups),
        (tile_mask, query_rows, near, *far, inner),
        (((HEADS, channels, tok_rows), single), stats, stats, ((2, half), single)),
        1,
        (
            pltpu.VMEM((HEADS, tok_rows, tok_rows), single),
            pltpu.VMEM((HEADS, half, half), single),
            pltpu.VMEM((HEADS, tok_rows, tok_rows), half_type),
            pltpu.VMEM((HEADS, half, half), half_type),
        ),
    )

    def edge(number, guest_type):
        group = groups[number]
        heads = len(group)
        return kernel_call(
            functools.partial(edge_kernel, *sizes, group),
            (
                side_bias, guest_bias, query_rows, near, far[number], inner,
                outer[number], guests[number], own_top, own_sum,
            ),
            (
                ((heads, channels, half), single),
                ((heads, channels, half), guest_type),
                ((heads, half), single),
                ((heads, half), single),
                ((heads, tok_rows), single),
                ((2, heads, half), single),
            ),
            0,
            (
                pltpu.VMEM((heads, half, half), single),
                pltpu.VMEM((heads, tok_rows, half), single),
                pltpu.VMEM((heads, half, half), half_type),
                pltpu.VMEM((heads, tok_rows, half), half_type),
                pltpu.VMEM((heads, half), single),
                pltpu.VMEM((heads, half), single),
            ),
        )

    side_out, guest_out, side_top, guest_top, log, sent = edge(0, single)
    got = sent_over(sent, row_pairs)
    late_side, late_guest, late_side_top, late_guest_top, late_log, late_sent = edge(1, half_type)
    (guest_velocity,) = kernel_call(
        guest_blend_kernel,
        (guest_out, guest_top, sent, got, late_guest_top, late_sent),
        (((channels + 2 * late, half), single),),
    )
    back = sent_over(guest_velocity, row_pairs)
    back_out = sent_over(late_guest, row_pairs)
    velocity_type = ((channels, tok_rows), single)
    (velocity,) = kernel_call(
        functools.partial(own_blend_kernel, tile_tok, groups[0]),
        (own_out, side_out, own_top, side_top, log, got),
        (velocity_type,),
    )
    (velocity,) = kernel_call(
        functools.partial(join_kernel, tile_tok, groups[1]),
        (
            own_out, late_side, own_top, late_side_top, late_log, velocity,
            back, back_out,
        ),
        (velocity_type,),
    )
    partner = sent_over(velocity, branch_pairs)
    out = ((channels, tok_rows), single)
    results = kernel_call(
        functools.partial(update_kernel, *sizes, half_size),
        (step_index, velocity, partner, latent.T),
        (out, out, out),
        1,
        stay=False,
    )
    return tuple(result.T for result in results)


def per_device(*args):
    return per_device_plan(*args)


def solution(mesh):
    placed = (
        P(("groups", "frame"), None),
        P(("groups", "frame"), None),
        P(("groups", "frame"), None),
        P(("groups", "frame"), None),
        P(),
        P(("groups", "frame"), None),
        P("groups"),
    )
    fast = one_frame_tile(mesh.shape["frame"])
    return jax.shard_map(
        per_device if fast else per_device_frames,
        mesh=mesh,
        in_specs=placed,
        out_specs=(
            P(("groups", "frame"), None),
            P(("groups", "frame"), None),
            P(("groups", "frame"), None),
        ),
        check_vma=False,
    )
```
